256 devices in a mesh: step: 16 (over y, x), frame: 16 (over z, core).
Axes of the slice: x: 4, y: 4, z: 8, core: 2. Of those that a mesh axis runs over, the one named last changes fastest.
Arguments:
- start_state: bfloat16 [16, 32, 32, 320], P('frame'), may hold values from -6 to 6
- step_noise: bfloat16 [16, 16, 32, 32, 320], P('step', 'frame'), may hold values from -6 to 6
- timesteps: int32 [16], P('step'), may hold values from 0 to 999
- gn_gain: float32 [320], replicated, may hold values from 0.1 to 1.9
- gn_bias: float32 [320], replicated, may hold values from -3 to 3
- spatial_weight: bfloat16 [3, 3, 320, 320], replicated, may hold values from -0.109375 to 0.109375
- temporal_weight: bfloat16 [3, 320, 320], replicated, may hold values from -0.1875 to 0.1875
- temb_weight: bfloat16 [320, 320], replicated, may hold values from -0.3125 to 0.3125
Outputs:
- next_states: bfloat16 [16, 16, 32, 32, 320], P('step', 'frame')
The draws below stay inside these ranges and needn't reach their ends.
All inputs are finite; a program needn't handle non-finite values.
Results may differ from the reference program's by a relative error of at most 0.005.
Values may be sent and summed in bfloat16 or wider, within the bound.
No kernel may reach another device: no remote copies, remote signals or barrier semaphores. Data moves between devices by JAX's collectives and lax.ppermute only.
A program may use at most 128 MiB of HBM per device.

```python
import math
import jax
import jax.numpy as jnp
from jax import lax

C = 320
TEMB = 320
GROUPS = 32
H = 32
W = 32
STEPS = 16
FRAMES = 16


def place_ends(array, rng, least, high):
    longest = array.shape.index(max(array.shape))
    spots = []
    for shift in (0, 1):
        where = [jax.random.randint(jax.random.fold_in(rng, axis), (), 0, length) for axis, length in enumerate(array.shape)]
        where[longest] = (where[longest] + shift) % array.shape[longest]
        spots.append(tuple(where))
    return array.at[spots[0]].set(least).at[spots[1]].set(high)


def block_scale(stream_key, dims, pieces, low, top_value):
    level = 1.0
    for axis_at, parts in pieces:
        steps = jax.random.uniform(jax.random.fold_in(jax.random.fold_in(stream_key, 6), axis_at), (parts,), jnp.float32, low / len(pieces), top_value / len(pieces))
        level = level * jnp.repeat(jnp.exp(steps), dims[axis_at] // parts).reshape((-1,) + (1,) * (len(dims) - 1 - axis_at))
    return level


def scatter_about(rng, shape, deviation, most, pieces=(), kind=jnp.bfloat16):
    array = jax.random.normal(rng, shape, jnp.float32) * deviation
    if len(pieces) > 0:
        array = block_scale(rng, shape, pieces, -0.22, 0.18) * array
    return jnp.clip(array, min=-most, max=most).astype(kind)


def setup_inputs(seed: int = 0) -> dict:
    arg_keys = jax.random.split(jax.random.key(seed), 9)
    return {
        "start_state": scatter_about(arg_keys[0], (FRAMES, H, W, C), 1.0, 6.0, ((0, 16),)),
        "step_noise": scatter_about(arg_keys[1], (STEPS, FRAMES, H, W, C), 1.0, 6.0, ((0, 16), (1, 16))),
        "timesteps": place_ends(jax.random.randint(arg_keys[2], (STEPS,), 0, 1000), jax.random.fold_in(arg_keys[2], 1), 0, 999).astype(jnp.int32),
        "gn_gain": jnp.clip(1.0 + 0.18 * jax.random.normal(arg_keys[3], (C,), jnp.float32), 0.1, 1.9),
        "gn_bias": scatter_about(arg_keys[4], (C,), 0.5, 3.0, (), jnp.float32),
        "spatial_weight": scatter_about(arg_keys[5], (3, 3, C, C), (9 * C) ** -0.5, 0.109375),
        "temporal_weight": scatter_about(arg_keys[6], (3, C, C), (3 * C) ** -0.5, 0.1875),
        "temb_weight": scatter_about(arg_keys[7], (TEMB, C), TEMB ** -0.5, 0.3125),
    }


def norm_silu(current, gn_gain, gn_bias):
    frames_here, rows, columns, channels = current.shape
    grouped = current.astype(jnp.float32).reshape(frames_here, rows, columns, GROUPS, channels // GROUPS)
    group_mean = lax.optimization_barrier(jnp.mean(grouped, axis=(1, 2, 4), keepdims=True))
    centered = grouped - group_mean
    group_var = lax.optimization_barrier(jnp.mean(centered * centered, axis=(1, 2, 4), keepdims=True))
    scaled = (centered * lax.rsqrt(group_var + 1e-05)).reshape(frames_here, rows, columns, channels)
    return jax.nn.silu(scaled * gn_gain + gn_bias).astype(jnp.bfloat16)

def time_vector(step_index, temb_weight):
    half_dim = temb_weight.shape[0] // 2
    frequencies = jnp.exp(-math.log(10000.0) * jnp.arange(half_dim, dtype=jnp.float32) / half_dim)
    angles = step_index.astype(jnp.float32) * frequencies
    embedding = jnp.concatenate([jnp.cos(angles), jnp.sin(angles)]).astype(jnp.bfloat16)
    return jax.nn.silu(jnp.dot(embedding, temb_weight, preferred_element_type=jnp.float32))

def spatial_conv(normed, spatial_weight):
    rows, columns = (normed.shape[1], normed.shape[2])
    padded = jnp.pad(normed, ((0, 0), (1, 1), (1, 1), (0, 0)))
    total = None
    for row_off in range(3):
        for col_off in range(3):
            window = padded[:, row_off:row_off + rows, col_off:col_off + columns, :]
            term = jnp.dot(window, spatial_weight[row_off, col_off], preferred_element_type=jnp.float32)
            total = term if total is None else total + term
    return total

def frame_conv(extended, temporal_weight, frames_out):
    total = None
    for offset in range(3):
        term = jnp.dot(extended[offset:offset + frames_out], temporal_weight[offset], preferred_element_type=jnp.float32)
        total = term if total is None else total + term
    return total.astype(jnp.bfloat16)

def reference(start_state, step_noise, timesteps, gn_gain, gn_bias, spatial_weight, temporal_weight, temb_weight):
    frame_count = start_state.shape[0]

    def drift_one(inputs):
        current, noise_now, step_index = inputs
        normed = norm_silu(current, gn_gain, gn_bias)
        time_bias = time_vector(step_index, temb_weight)
        activated = jax.nn.silu(spatial_conv(normed, spatial_weight) + time_bias).astype(jnp.bfloat16)
        extended = jnp.pad(activated, ((1, 1), (0, 0), (0, 0), (0, 0)))
        update = frame_conv(extended, temporal_weight, frame_count)
        return 0.25 * update.astype(jnp.float32) + 0.25 * noise_now.astype(jnp.float32)
    start_wide = start_state.astype(jnp.float32)
    first_states = jnp.broadcast_to(start_state, (STEPS,) + start_state.shape)
    first_drift = lax.map(drift_one, (first_states, step_noise, timesteps))
    inclusive = jnp.cumsum(first_drift, axis=0)
    exclusive = jnp.concatenate([jnp.zeros_like(inclusive[:1]), inclusive[:-1]], axis=0)
    states = (start_wide + exclusive).astype(jnp.bfloat16)
    second_drift = lax.map(drift_one, (states, step_noise, timesteps))
    return (start_wide + jnp.cumsum(second_drift, axis=0)).astype(jnp.bfloat16)
```

```python
import math

import jax
import jax.numpy as jnp
from jax import lax
from jax.experimental import pallas as pl
from jax.experimental.pallas import tpu as pltpu
from jax.sharding import Mesh, PartitionSpec as P

F32, BF16 = jnp.float32, jnp.bfloat16
AXES = ("y", "x", "z", "core")
HIGHEST = lax.Precision.HIGHEST

POS, ROWS, LANES = 256, 640, 128


def silu(a):
    half = 0.5 * a
    return half + half * jnp.tanh(half)


def low_lanes(rows):
    return lax.broadcasted_iota(jnp.int32, (rows, LANES), 1) < 64


def swapped(tile):
    return pltpu.roll(tile, 64, 1)


def pack_tail(tail):
    return jnp.concatenate([tail[:128], tail[128:]], axis=1)


def twice(tail):
    return jnp.concatenate([tail, tail], axis=1)


def spread_tail(tile):
    low, other = low_lanes(128), swapped(tile)
    return jnp.concatenate([jnp.where(low, tile, other), jnp.where(low, other, tile)], axis=0)


def same_group(size):
    rows = lax.broadcasted_iota(jnp.int32, (size, size), 0)
    columns = lax.broadcasted_iota(jnp.int32, (size, size), 1)
    return (((rows * 6554) >> 16) == ((columns * 6554) >> 16)).astype(F32)


def group_sum(sums, members):
    wide = jnp.broadcast_to(sums, (8, sums.shape[1]))
    return jnp.dot(wide, members, precision=HIGHEST, preferred_element_type=F32)[0:1]


def store_taps(taps, tiles):
    column = lax.broadcasted_iota(jnp.int32, (320, LANES), 0) & 31
    low = low_lanes(320)
    shifted = []
    for place, step in enumerate((-1, 0, 1)):
        moved = []
        for tile in tiles:
            if step:
                tile = pltpu.roll(tile, -step % 320, 0)
                tile = jnp.where(column == (0 if step < 0 else 31), 0.0, tile)
            moved.append(tile)
        taps[:, place * 256 : place * 256 + 128] = moved[0].astype(BF16)
        taps[:, place * 256 + 128 : place * 256 + 256] = moved[1].astype(BF16)
        shifted.append(moved[2])
    taps[:, 768:896] = jnp.where(low, shifted[0], shifted[1]).astype(BF16)
    taps[:, 896:1024] = jnp.where(low, shifted[2], 0.0).astype(BF16)


def conv_rows(taps, wp):
    total = None
    for row in range(3):
        term = jnp.dot(taps[row * 32 : row * 32 + POS, :], wp[row], preferred_element_type=F32)
        total = term if total is None else total + term
    return total


def pack_noise_kernel(noise, emb, *outs):
    x = lax.axis_index("x")
    for hop, out in enumerate(outs):
        start = pl.multiple_of(lax.rem(x + hop, 4) * POS, POS)
        out[0:256] = noise[pl.ds(start, POS), 0:128]
        out[256:512] = noise[pl.ds(start, POS), 128:256]
        out[512:640] = pack_tail(noise[pl.ds(start, POS), 256:320].astype(F32)).astype(BF16)
        for tile in range(3):
            out[640 + 16 * tile : 656 + 16 * tile] = emb[:, tile * 128 : tile * 128 + 128]


def weights_kernel(sw, tw, wp, tp):
    for row in range(4):
        out = tp if row == 3 else wp.at[row]
        for place in range(3):
            one = tw.at[place] if row == 3 else sw.at[row, place]
            out[place * 256 : place * 256 + 256] = one[0:256]
            out[768 + 64 * place : 832 + 64 * place] = one[256:320]
        out[960:1024] = jnp.zeros((64, 320), BF16)


def norm_start_kernel(start, gain, bias, nq, sp):
    x = lax.axis_index("x")
    members = same_group(320)
    values = start[...].astype(F32)
    mean = group_sum(jnp.sum(values, axis=0, keepdims=True), members) * (1.0 / 10240)
    centered = start[...].astype(F32) - mean
    var = group_sum(jnp.sum(centered * centered, axis=0, keepdims=True), members) * (1.0 / 10240)
    scale = lax.rsqrt(var + 1e-05)
    first = pl.multiple_of(x * POS, POS)
    above = pl.multiple_of(jnp.maximum(x * POS - 32, 0), 32)
    below = pl.multiple_of(jnp.minimum(x * POS + POS, 992), 32)
    for at, size, rows, kept in (
        (above, 32, 0, x > 0),
        (first, POS, 32, None),
        (below, 32, 288, x < 3),
    ):
        block = start[pl.ds(at, size), :].astype(F32)
        normed = silu((block - mean) * scale * gain[...] + bias[...])
        if kept is not None:
            normed = jnp.where(kept, normed, 0.0)
        nq[0, rows : rows + size] = normed[:, 0:128].astype(BF16)
        nq[1, rows : rows + size] = normed[:, 128:256].astype(BF16)
        nq[2, rows : rows + size] = twice(normed[:, 256:320]).astype(BF16)
    sp[0:256] = start[pl.ds(first, POS), 0:128]
    sp[256:512] = start[pl.ds(first, POS), 128:256]
    sp[512:640] = pack_tail(start[pl.ds(first, POS), 256:320].astype(F32)).astype(BF16)


def drift_of(a3, tp, noise, step):
    update = jnp.dot(a3[...], tp[...], preferred_element_type=F32)
    packed = (update[:, 0:128], update[:, 128:256], pack_tail(update[:, 256:320]))
    spans = ((0, 256), (256, 512), (512, 640))
    return [(a, b, 0.25 * (u + noise[step, a:b].astype(F32))) for u, (a, b) in zip(packed, spans)]


def first_sweep_kernel(own, before, after, wp, tp, tew, n0, n1, n2, n3, rt, prefix, noise, tb, taps, pre, a3, run):
    x = lax.axis_index("x")
    frame = lax.axis_index("z") * 2 + lax.axis_index("core")
    for hop, one in enumerate((n0, n1, n2, n3)):
        step = lax.rem(x + 4 - hop, 4)
        noise[step] = one[0:640]
        bias = (
            jnp.dot(one[640:656], tew[0:128], preferred_element_type=F32)
            + jnp.dot(one[656:672], tew[128:256], preferred_element_type=F32)
            + jnp.dot(one[672:688, 0:64], tew[256:320], preferred_element_type=F32)
        )
        tb[step] = bias / (1.0 + jnp.exp(-bias))
    for place, normed in enumerate((before, own, after)):
        store_taps(taps, [normed[i].astype(F32) for i in range(3)])
        pre[place] = conv_rows(taps, wp)
    run[...] = jnp.zeros_like(run)

    def one_step(step, carry):
        bias = tb[step][0:1]
        tails = []
        for place, there in enumerate((frame > 0, None, frame < 15)):
            activated = silu(pre[place] + bias)
            if there is not None:
                activated = jnp.where(there, activated, 0.0)
            a3[:, place * 256 : place * 256 + 256] = activated[:, 0:256].astype(BF16)
            tails.append(activated[:, 256:320])
        a3[:, 768:896] = jnp.concatenate(tails[:2], axis=1).astype(BF16)
        a3[:, 896:1024] = jnp.concatenate([tails[2], jnp.zeros_like(tails[2])], axis=1).astype(BF16)
        for a, b, drift in drift_of(a3, tp, noise, step):
            earlier = run[a:b]
            prefix[step, a:b] = earlier
            run[a:b] = earlier + drift
        return carry

    lax.fori_loop(0, 4, one_step, 0)
    rt[...] = run[...].astype(BF16)


def dup_third(parts):
    third = parts[:, 256:384]
    third = jnp.where(low_lanes(third.shape[0]), third, swapped(third))
    return jnp.concatenate([parts[:, 0:256], third], axis=1)


def position_sum(tiles):
    sums = [jnp.sum(tile, axis=0, keepdims=True) for tile in tiles]
    third = jnp.broadcast_to(sums[2], (8, LANES))
    return jnp.concatenate(sums[:2] + [(third + swapped(third))[0:1]], axis=1)


def states_kernel(sp, prefix, r1, r2, r3, states, up, down, far):
    members = same_group(384)
    base = sp[...].astype(F32) + (r1[...].astype(F32) + r2[...].astype(F32) + r3[...].astype(F32))
    means, spreads = [], []
    for step in range(4):
        states[step] = (base + prefix[step]).astype(BF16)
        tiles = [states[step, a:b].astype(F32) for a, b in ((0, 256), (256, 512), (512, 640))]
        mean = dup_third(jnp.broadcast_to(group_sum(position_sum(tiles), members) * (1.0 / 2560), (8, 384)))[0:1]
        centered = [tile - mean[:, 128 * i : 128 * i + 128] for i, tile in enumerate(tiles)]
        spread = group_sum(position_sum([c * c for c in centered]), members)
        means.append(mean)
        spreads.append(dup_third(jnp.broadcast_to(spread, (8, 384)))[0:1])
        for i, (first, last) in enumerate(((0, 224), (256, 480), (512, 608))):
            at = step * 96 + i * 32
            up[at : at + 32] = states[step, last : last + 32]
            down[at : at + 32] = states[step, first : first + 32]
    rest = jnp.concatenate(means + spreads, axis=0)
    for part in range(3):
        piece = rest.astype(BF16)
        rest = rest - piece.astype(F32)
        for tile in range(3):
            at = (part * 3 + tile) * 8
            value = piece[:, tile * 128 : tile * 128 + 128]
            far[at : at + 8] = value
            up[384 + at : 392 + at] = value
            down[384 + at : 392 + at] = value


def stats_of(ref, base):
    total = None
    for part in range(3):
        piece = jnp.concatenate(
            [ref[base + (part * 3 + t) * 8 : base + (part * 3 + t) * 8 + 8].astype(F32) for t in range(3)], axis=1
        )
        total = piece if total is None else total + piece
    return total[0:4], total[4:8]


def second_sweep_kernel(states, above, below, far, mine, gain, bias, wp, tb, out, taps, scales):
    x = lax.axis_index("x")
    parts = [stats_of(mine, 0), stats_of(above, 384), stats_of(below, 384), stats_of(far, 0)]
    mean = (parts[0][0] + parts[1][0] + parts[2][0] + parts[3][0]) * 0.25
    spread = parts[0][1] + parts[1][1] + parts[2][1] + parts[3][1]
    for one in parts:
        spread = spread + 2560.0 * (one[0] - mean) * (one[0] - mean)
    rstd = lax.rsqrt(spread * (1.0 / 10240) + 1e-05)
    for step in range(4):
        scales[step, 0:1] = mean[step : step + 1]
        scales[step, 1:2] = rstd[step : step + 1]

    def one_step(step, carry):
        here = scales[step]

        def normed(value, tile):
            lanes = slice(tile * 128, tile * 128 + 128)
            value = (value.astype(F32) - here[0:1, lanes]) * here[1:2, lanes]
            return silu(value * gain[:, lanes] + bias[:, lanes])

        edge = pl.multiple_of(step * 96, 32)
        tiles = []
        low = low_lanes(32)
        for tile in range(3):
            top = normed(above[pl.ds(edge + 32 * tile, 32)], tile)
            bottom = normed(below[pl.ds(edge + 32 * tile, 32)], tile)
            if tile < 2:
                middle = normed(states[step, 256 * tile : 256 * tile + 256], tile)
            else:
                middle = spread_tail(normed(states[step, 512:640], 2))
                top = jnp.where(low, swapped(top), top)
                bottom = jnp.where(low, bottom, swapped(bottom))
            top = jnp.where(x > 0, top, 0.0)
            bottom = jnp.where(x < 3, bottom, 0.0)
            tiles.append(jnp.concatenate([top, middle, bottom], axis=0))
        store_taps(taps, tiles)
        activated = silu(conv_rows(taps, wp) + tb[step][0:1])
        out[step, 0:256] = activated[:, 0:128].astype(BF16)
        out[step, 256:512] = activated[:, 128:256].astype(BF16)
        out[step, 512:640] = pack_tail(activated[:, 256:320]).astype(BF16)
        return carry

    lax.fori_loop(0, 4, one_step, 0)


def second_drift_kernel(own, before, after, tp, noise, rt, prefix, a3, run):
    run[...] = jnp.zeros_like(run)
    low = low_lanes(POS)

    def one_step(step, carry):
        tails = []
        for place, one in enumerate((before, own, after)):
            a3[:, place * 256 : place * 256 + 128] = one[step, 0:256]
            a3[:, place * 256 + 128 : place * 256 + 256] = one[step, 256:512]
            tails.append(spread_tail(one[step, 512:640].astype(F32)))
        a3[:, 768:896] = jnp.where(low, tails[0], tails[1]).astype(BF16)
        a3[:, 896:1024] = jnp.where(low, tails[2], 0.0).astype(BF16)
        for a, b, drift in drift_of(a3, tp, noise, step):
            now = run[a:b] + drift
            prefix[step, a:b] = now
            run[a:b] = now
        return carry

    lax.fori_loop(0, 4, one_step, 0)
    rt[...] = run[...].astype(BF16)


def result_kernel(sp, prefix, r1, r2, r3, *outs):
    x = lax.axis_index("x")
    base = sp[...].astype(F32) + (r1[...].astype(F32) + r2[...].astype(F32) + r3[...].astype(F32))
    for hop, out in enumerate(outs):
        out[...] = (base + prefix[lax.rem(x + hop, 4)]).astype(BF16)


def unpack_kernel(r0, r1, r2, r3, out):
    x = lax.axis_index("x")
    for hop, one in enumerate((r0, r1, r2, r3)):
        start = pl.multiple_of(lax.rem(x + 4 - hop, 4) * POS, POS)
        out[pl.ds(start, POS), 0:128] = one[0:256]
        out[pl.ds(start, POS), 128:256] = one[256:512]
        tail = spread_tail(one[512:640].astype(F32))
        out[pl.ds(start, POS), 256:320] = tail[:, 0:64].astype(BF16)


def call(body, name, outs, *args, scratch=(), flops=0, limit=24):
    shapes = [jax.ShapeDtypeStruct(shape, kind) for shape, kind in outs]
    vmem = pl.BlockSpec(memory_space=pltpu.VMEM)
    nbytes = sum(a.size * a.dtype.itemsize for a in args) + sum(s.size * s.dtype.itemsize for s in shapes)
    return pl.pallas_call(
        body,
        name=name,
        out_shape=shapes,
        in_specs=[vmem] * len(args),
        out_specs=[vmem] * len(shapes),
        scratch_shapes=[pltpu.VMEM(shape, kind) for shape, kind in scratch],
        compiler_params=pltpu.CompilerParams(vmem_limit_bytes=limit << 20),
        cost_estimate=pl.CostEstimate(flops=flops, bytes_accessed=nbytes, transcendentals=0),
    )(*args)


def moved(value, place):
    pairs = []
    for y in range(4):
        for x in range(4):
            for z in range(8):
                for core in range(2):
                    to = place(y, x, z * 2 + core)
                    if to is not None:
                        ty, tx, frame = to
                        pairs.append(((y * 4 + x) * 16 + z * 2 + core, (ty * 4 + tx) * 16 + frame))
    return lax.ppermute(value, AXES, pairs)


def along_x(value, hop):
    return moved(value, lambda y, x, frame: (y, (x + hop) % 4, frame))


def along_y(value, hop):
    return moved(value, lambda y, x, frame: (y + hop, x, frame) if y + hop < 4 else None)


def along_frame(value, hop):
    return moved(value, lambda y, x, frame: (y, x, frame + hop) if 0 <= frame + hop < 16 else None)


def embedding_of(step_index, half_dim):
    frequencies = jnp.exp(-math.log(10000.0) * jnp.arange(half_dim, dtype=F32) / half_dim)
    angles = step_index.astype(F32) * frequencies
    return jnp.concatenate([jnp.cos(angles), jnp.sin(angles)]).astype(BF16)


def local(start_state, step_noise, timesteps, gn_gain, gn_bias, spatial_weight, temporal_weight, temb_weight):
    start = start_state.reshape(1024, 320)
    noise = step_noise.reshape(1024, 320)
    emb = embedding_of(timesteps[0], temb_weight.shape[0] // 2)
    emb = jnp.broadcast_to(jnp.pad(emb, (0, 64))[None], (16, 384))
    wide_gain = jnp.concatenate([gn_gain, gn_gain[256:]])[None]
    wide_bias = jnp.concatenate([gn_bias, gn_bias[256:]])[None]
    packed = (ROWS, LANES)
    four = (4, ROWS, LANES)

    outgoing = call(pack_noise_kernel, "pack_noise", [((688, 128), BF16)] * 4, noise, emb)
    arrived = [outgoing[0]] + [along_x(outgoing[hop], hop) for hop in (1, 2, 3)]
    nq, sp = call(
        norm_start_kernel, "norm_start", [((3, 320, 128), BF16), (packed, BF16)], start, gn_gain[None], gn_bias[None]
    )
    before, after = along_frame(nq, 1), along_frame(nq, -1)
    wp, tp = call(
        weights_kernel, "weights", [((3, 1024, 320), BF16), ((1024, 320), BF16)], spatial_weight, temporal_weight
    )
    a3 = ((256, 1024), BF16)
    taps = ((320, 1024), BF16)
    run = (packed, F32)
    rt, prefix, noises, tb = call(
        first_sweep_kernel,
        "first_sweep",
        [(packed, BF16), (four, F32), (four, BF16), ((4, 16, 320), F32)],
        nq, before, after, wp, tp, temb_weight, *arrived,
        scratch=(taps, ((3, 256, 320), F32), a3, run),
        flops=2 * 1024 * 320 * 3200,
    )
    totals = [along_y(rt, hop) for hop in (1, 2, 3)]
    states, up, down, far = call(
        states_kernel,
        "states",
        [(four, BF16), ((464, 128), BF16), ((464, 128), BF16), ((72, 128), BF16)],
        sp, prefix, *totals,
    )
    activated = call(
        second_sweep_kernel,
        "second_sweep",
        [(four, BF16)],
        states, along_x(up, 1), along_x(down, -1), along_x(far, 2), far, wide_gain, wide_bias, wp, tb,
        scratch=(taps, ((4, 8, 384), F32)),
        flops=2 * 1024 * 320 * 2880,
    )[0]
    rt, prefix = call(
        second_drift_kernel,
        "second_drift",
        [(packed, BF16), (four, F32)],
        activated, along_frame(activated, 1), along_frame(activated, -1), tp, noises,
        scratch=(a3, run),
        flops=2 * 1024 * 320 * 960,
    )
    totals = [along_y(rt, hop) for hop in (1, 2, 3)]
    results = call(result_kernel, "result", [(packed, BF16)] * 4, sp, prefix, *totals)
    back = [results[0]] + [along_x(results[hop], hop) for hop in (1, 2, 3)]
    out = call(unpack_kernel, "unpack", [((1024, 320), BF16)], *back)[0]
    return out.reshape(1, 1, 32, 32, 320)


def solution(mesh):
    split = Mesh(mesh.devices.reshape(4, 4, 8, 2), AXES)
    steps, frames = ("y", "x"), ("z", "core")
    placed = (
        P(frames, None, None, None),
        P(steps, frames, None, None, None),
        P(steps),
        P(),
        P(),
        P(),
        P(),
        P(),
    )
    return jax.shard_map(
        local,
        mesh=split,
        in_specs=placed,
        out_specs=P(steps, frames, None, None, None),
        check_vma=False,
    )
```

```python
import math

import jax
import jax.numpy as jnp
from jax import lax
from jax.experimental import pallas as pl
from jax.experimental.pallas import tpu as pltpu
from jax.sharding import Mesh, PartitionSpec as P


F32, BF16 = jnp.float32, jnp.bfloat16
AXES = ("y", "x", "z", "core")
HIGHEST = lax.Precision.HIGHEST

POS, ROWS, LANES = 256, 640, 128


def silu(a):
    half = 0.5 * a
    return half + half * jnp.tanh(half)


def low_lanes(rows):
    return lax.broadcasted_iota(jnp.int32, (rows, LANES), 1) < 64


def swapped(tile):
    return pltpu.roll(tile, 64, 1)


def pack_tail(tail):
    return jnp.concatenate([tail[:128], tail[128:]], axis=1)


def twice(tail):
    return jnp.concatenate([tail, tail], axis=1)


def spread_tail(tile):
    low, other = low_lanes(128), swapped(tile)
    return jnp.concatenate([jnp.where(low, tile, other), jnp.where(low, other, tile)], axis=0)


def same_group(size):
    rows = lax.broadcasted_iota(jnp.int32, (size, size), 0)
    columns = lax.broadcasted_iota(jnp.int32, (size, size), 1)
    return (((rows * 6554) >> 16) == ((columns * 6554) >> 16)).astype(F32)


def group_sum(sums, members):
    return jnp.dot(sums, members, precision=HIGHEST, preferred_element_type=F32)


def store_taps(taps, tiles):
    column = lax.broadcasted_iota(jnp.int32, (320, LANES), 0) & 31
    low = low_lanes(320)
    shifted = []
    for place, step in enumerate((-1, 0, 1)):
        moved = []
        for tile in tiles:
            if step:
                tile = pltpu.roll(tile, -step % 320, 0)
                tile = jnp.where(column == (0 if step < 0 else 31), 0.0, tile)
            moved.append(tile)
        taps[:, place * 256 : place * 256 + 128] = moved[0].astype(BF16)
        taps[:, place * 256 + 128 : place * 256 + 256] = moved[1].astype(BF16)
        shifted.append(moved[2])
    taps[:, 768:896] = jnp.where(low, shifted[0], shifted[1]).astype(BF16)
    taps[:, 896:1024] = jnp.where(low, shifted[2], 0.0).astype(BF16)


def conv_rows(taps, wp):
    total = None
    for row in range(3):
        term = jnp.dot(taps[row * 32 : row * 32 + POS, :], wp[row], preferred_element_type=F32)
        total = term if total is None else total + term
    return total


def hop_of(slot):
    return jnp.where(lax.axis_index("core") == 0, slot, (4 - slot) % 4)


def prologue_kernel(
    noise_hbm, start_hbm, sw, tw, tew_hbm, gain_hbm, bias_hbm, emb,
    o0, o1, o2, o3, start, wp, tp, tew, gain, bias, noise, sems,
):
    x = lax.axis_index("x")
    frame = lax.axis_index("z") * 2 + lax.axis_index("core")
    moves = [(noise_hbm, noise), (start_hbm, start), (gain_hbm, gain), (bias_hbm, bias)]
    for row in range(4):
        out = tp if row == 3 else wp.at[row]
        for place in range(3):
            one = tw.at[place] if row == 3 else sw.at[row, place]
            moves.append((one.at[0:256], out.at[place * 256 : place * 256 + 256]))
            moves.append((one.at[256:320], out.at[768 + 64 * place : 832 + 64 * place]))
    moves.append((tew_hbm, tew))
    copies = [pltpu.make_async_copy(source, target, sems.at[i]) for i, (source, target) in enumerate(moves)]
    for copy in copies:
        copy.start()
    for row in range(3):
        wp[row, 960:1024] = jnp.zeros((64, 320), BF16)
    tp[960:1024] = jnp.zeros((64, 320), BF16)
    copies[0].wait()
    for slot, out in enumerate((o0, o1, o2, o3)):
        at = pl.multiple_of(lax.rem(x + hop_of(slot), 4) * POS, POS)
        out[0:256] = noise[pl.ds(at, POS), 0:128]
        out[256:512] = noise[pl.ds(at, POS), 128:256]
        out[512:640] = pack_tail(noise[pl.ds(at, POS), 256:320].astype(F32)).astype(BF16)
        for tile in range(3):
            out[640 + 16 * tile : 656 + 16 * tile] = emb[:, tile * 128 : tile * 128 + 128]
    for copy in copies[1:]:
        copy.wait()
    for place, missing in ((0, frame == 0), (2, frame == 15)):

        @pl.when(missing)
        def _():
            tp[place * 256 : place * 256 + 256] = jnp.zeros((256, 320), BF16)
            tp[768 + 64 * place : 832 + 64 * place] = jnp.zeros((64, 320), BF16)


def norm_start_kernel(start, gain_ref, bias_ref, nq, sp):
    x = lax.axis_index("x")
    members = same_group(320)
    values = start[...].astype(F32)
    mean = group_sum(jnp.broadcast_to(jnp.sum(values, axis=0, keepdims=True), (8, 320)), members)[0:1] * (1.0 / 10240)
    centered = start[...].astype(F32) - mean
    spread = jnp.sum(centered * centered, axis=0, keepdims=True)
    var = group_sum(jnp.broadcast_to(spread, (8, 320)), members)[0:1] * (1.0 / 10240)
    scale = lax.rsqrt(var + 1e-05)
    gain, bias = gain_ref[...].reshape(1, 320), bias_ref[...].reshape(1, 320)
    first = pl.multiple_of(x * POS, POS)
    above = pl.multiple_of(jnp.maximum(x * POS - 32, 0), 32)
    below = pl.multiple_of(jnp.minimum(x * POS + POS, 992), 32)
    for at, size, rows, kept in (
        (above, 32, 0, x > 0),
        (first, POS, 32, None),
        (below, 32, 288, x < 3),
    ):
        block = start[pl.ds(at, size), :].astype(F32)
        normed = silu((block - mean) * scale * gain + bias)
        if kept is not None:
            normed = jnp.where(kept, normed, 0.0)
        nq[0, rows : rows + size] = normed[:, 0:128].astype(BF16)
        nq[1, rows : rows + size] = normed[:, 128:256].astype(BF16)
        nq[2, rows : rows + size] = twice(normed[:, 256:320]).astype(BF16)
    sp[0:256] = start[pl.ds(first, POS), 0:128]
    sp[256:512] = start[pl.ds(first, POS), 128:256]
    sp[512:640] = pack_tail(start[pl.ds(first, POS), 256:320].astype(F32)).astype(BF16)


def drift_of(a3, tp, noise, step):
    update = jnp.dot(a3[...], tp[...], preferred_element_type=F32)
    packed = (update[:, 0:128], update[:, 128:256], pack_tail(update[:, 256:320]))
    spans = ((0, 256), (256, 512), (512, 640))
    return [(a, b, 0.25 * (u + noise[step, a:b].astype(F32))) for u, (a, b) in zip(packed, spans)]


def first_sweep_kernel(own, before, after, wp, tp, tew, n0, n1, n2, n3, rt, prefix, noise, tb, taps, pre, a3, run):
    x = lax.axis_index("x")
    for slot, one in enumerate((n0, n1, n2, n3)):
        step = lax.rem(x + 4 - hop_of(slot), 4)
        noise[step] = one[0:640]
        bias = (
            jnp.dot(one[640:656], tew[0:128], preferred_element_type=F32)
            + jnp.dot(one[656:672], tew[128:256], preferred_element_type=F32)
            + jnp.dot(one[672:688, 0:64], tew[256:320], preferred_element_type=F32)
        )
        tb[step] = bias / (1.0 + jnp.exp(-bias))
    for place, normed in enumerate((before, own, after)):
        store_taps(taps, [normed[i].astype(F32) for i in range(3)])
        pre[place] = conv_rows(taps, wp)
    run[...] = jnp.zeros_like(run)

    def one_step(step, carry):
        bias = tb[step][0:1]
        tails = []
        for place in range(3):
            activated = silu(pre[place] + bias)
            a3[:, place * 256 : place * 256 + 256] = activated[:, 0:256].astype(BF16)
            tails.append(activated[:, 256:320])
        a3[:, 768:896] = jnp.concatenate(tails[:2], axis=1).astype(BF16)
        a3[:, 896:1024] = jnp.concatenate([tails[2], jnp.zeros_like(tails[2])], axis=1).astype(BF16)
        for a, b, drift in drift_of(a3, tp, noise, step):
            earlier = run[a:b]
            prefix[step, a:b] = earlier
            run[a:b] = earlier + drift
        return carry

    lax.fori_loop(0, 4, one_step, 0)
    rt[...] = run[...].astype(BF16)


def dup_third(parts):
    third = parts[:, 256:384]
    third = jnp.where(low_lanes(third.shape[0]), third, swapped(third))
    return jnp.concatenate([parts[:, 0:256], third], axis=1)


def offset_of(totals):
    y = lax.axis_index("y")
    kept = [jnp.where(y >= hop_of(slot), one[...].astype(F32), 0.0) for slot, one in enumerate(totals, 1)]
    return kept[0] + kept[1] + kept[2]


def position_sum(tiles):
    sums = [jnp.sum(tile, axis=0, keepdims=True) for tile in tiles]
    third = jnp.broadcast_to(sums[2], (8, LANES))
    return jnp.concatenate(sums[:2] + [(third + swapped(third))[0:1]], axis=1)


def states_kernel(sp, prefix, r1, r2, r3, states, up, down, far):
    members = same_group(384)
    base = sp[...].astype(F32) + offset_of((r1, r2, r3))
    spans = ((0, 256), (256, 512), (512, 640))
    sums = []
    for step in range(4):
        states[step] = (base + prefix[step]).astype(BF16)
        sums.append(position_sum([states[step, a:b].astype(F32) for a, b in spans]))
        for i, (first, last) in enumerate(((0, 224), (256, 480), (512, 608))):
            at = step * 96 + i * 32
            up[at : at + 32] = states[step, last : last + 32]
            down[at : at + 32] = states[step, first : first + 32]
    means = dup_third(group_sum(jnp.concatenate(sums + sums, axis=0), members) * (1.0 / 2560))
    spreads = []
    for step in range(4):
        mean = means[step : step + 1]
        centered = [states[step, a:b].astype(F32) - mean[:, 128 * i : 128 * i + 128] for i, (a, b) in enumerate(spans)]
        spreads.append(position_sum([c * c for c in centered]))
    spread = dup_third(group_sum(jnp.concatenate(spreads + spreads, axis=0), members))
    rest = jnp.concatenate([means[0:4], spread[0:4]], axis=0)
    for part in range(3):
        piece = rest.astype(BF16)
        rest = rest - piece.astype(F32)
        for tile in range(3):
            at = (part * 3 + tile) * 8
            value = piece[:, tile * 128 : tile * 128 + 128]
            far[at : at + 8] = value
            up[384 + at : 392 + at] = value
            down[384 + at : 392 + at] = value


def stats_of(ref, base):
    total = None
    for part in range(3):
        piece = jnp.concatenate(
            [ref[base + (part * 3 + t) * 8 : base + (part * 3 + t) * 8 + 8].astype(F32) for t in range(3)], axis=1
        )
        total = piece if total is None else total + piece
    return total[0:4], total[4:8]


def wide(vector):
    vector = vector[...].reshape(1, 320)
    return jnp.concatenate([vector, vector[:, 256:320]], axis=1)


def second_sweep_kernel(states, above, below, far, mine, gain_ref, bias_ref, wp, tb, out, taps, scales):
    gain, bias = wide(gain_ref), wide(bias_ref)
    x = lax.axis_index("x")
    parts = [stats_of(mine, 0), stats_of(above, 384), stats_of(below, 384), stats_of(far, 0)]
    mean = (parts[0][0] + parts[1][0] + parts[2][0] + parts[3][0]) * 0.25
    spread = parts[0][1] + parts[1][1] + parts[2][1] + parts[3][1]
    for one in parts:
        spread = spread + 2560.0 * (one[0] - mean) * (one[0] - mean)
    rstd = lax.rsqrt(spread * (1.0 / 10240) + 1e-05)
    for step in range(4):
        scales[step, 0:1] = mean[step : step + 1]
        scales[step, 1:2] = rstd[step : step + 1]

    def one_step(step, carry):
        here = scales[step]

        def normed(value, tile):
            lanes = slice(tile * 128, tile * 128 + 128)
            value = (value.astype(F32) - here[0:1, lanes]) * here[1:2, lanes]
            return silu(value * gain[:, lanes] + bias[:, lanes])

        edge = pl.multiple_of(step * 96, 32)
        tiles = []
        low = low_lanes(32)
        for tile in range(3):
            top = normed(above[pl.ds(edge + 32 * tile, 32)], tile)
            bottom = normed(below[pl.ds(edge + 32 * tile, 32)], tile)
            if tile < 2:
                middle = normed(states[step, 256 * tile : 256 * tile + 256], tile)
            else:
                middle = spread_tail(normed(states[step, 512:640], 2))
                top = jnp.where(low, swapped(top), top)
                bottom = jnp.where(low, bottom, swapped(bottom))
            top = jnp.where(x > 0, top, 0.0)
            bottom = jnp.where(x < 3, bottom, 0.0)
            tiles.append(jnp.concatenate([top, middle, bottom], axis=0))
        store_taps(taps, tiles)
        activated = silu(conv_rows(taps, wp) + tb[step][0:1])
        out[step, 0:256] = activated[:, 0:128].astype(BF16)
        out[step, 256:512] = activated[:, 128:256].astype(BF16)
        out[step, 512:640] = pack_tail(activated[:, 256:320]).astype(BF16)
        return carry

    lax.fori_loop(0, 4, one_step, 0)


def second_drift_kernel(own, before, after, tp, noise, rt, prefix, a3, run):
    run[...] = jnp.zeros_like(run)
    low = low_lanes(POS)

    def one_step(step, carry):
        tails = []
        for place, one in enumerate((before, own, after)):
            a3[:, place * 256 : place * 256 + 128] = one[step, 0:256]
            a3[:, place * 256 + 128 : place * 256 + 256] = one[step, 256:512]
            tails.append(spread_tail(one[step, 512:640].astype(F32)))
        a3[:, 768:896] = jnp.where(low, tails[0], tails[1]).astype(BF16)
        a3[:, 896:1024] = jnp.where(low, tails[2], 0.0).astype(BF16)
        for a, b, drift in drift_of(a3, tp, noise, step):
            now = run[a:b] + drift
            prefix[step, a:b] = now
            run[a:b] = now
        return carry

    lax.fori_loop(0, 4, one_step, 0)
    rt[...] = run[...].astype(BF16)


def result_kernel(sp, prefix, r1, r2, r3, *outs):
    x = lax.axis_index("x")
    base = sp[...].astype(F32) + offset_of((r1, r2, r3))
    for slot, out in enumerate(outs):
        out[...] = (base + prefix[lax.rem(x + hop_of(slot), 4)]).astype(BF16)


def unpack_kernel(r0, r1, r2, r3, out):
    x = lax.axis_index("x")
    for slot, one in enumerate((r0, r1, r2, r3)):
        start = pl.multiple_of(lax.rem(x + 4 - hop_of(slot), 4) * POS, POS)
        out[pl.ds(start, POS), 0:128] = one[0:256]
        out[pl.ds(start, POS), 128:256] = one[256:512]
        tail = spread_tail(one[512:640].astype(F32))
        out[pl.ds(start, POS), 256:320] = tail[:, 0:64].astype(BF16)


def call(body, outs, *args, scratch=(), flops=0, limit=24, hbm=0, sems=0):
    shapes = [jax.ShapeDtypeStruct(shape, kind) for shape, kind in outs]
    vmem = pl.BlockSpec(memory_space=pltpu.VMEM)
    nbytes = sum(a.size * a.dtype.itemsize for a in args) + sum(s.size * s.dtype.itemsize for s in shapes)
    scratch_shapes = [pltpu.VMEM(shape, kind) for shape, kind in scratch]
    if sems:
        scratch_shapes.append(pltpu.SemaphoreType.DMA((sems,)))
    return pl.pallas_call(
        body,
        out_shape=shapes,
        in_specs=[pl.BlockSpec(memory_space=pltpu.HBM)] * hbm + [vmem] * (len(args) - hbm),
        out_specs=[vmem] * len(shapes),
        scratch_shapes=scratch_shapes,
        compiler_params=pltpu.CompilerParams(vmem_limit_bytes=limit << 20),
        cost_estimate=pl.CostEstimate(flops=flops, bytes_accessed=nbytes, transcendentals=0),
    )(*(pltpu.with_memory_space_constraint(a, pltpu.HBM) if i < hbm else a for i, a in enumerate(args)))


def moved(value, place):
    pairs = []
    for y in range(4):
        for x in range(4):
            for z in range(8):
                for core in range(2):
                    ty, tx, frame = place(y, x, z * 2 + core)
                    pairs.append(((y * 4 + x) * 16 + z * 2 + core, (ty * 4 + tx) * 16 + frame))
    return lax.ppermute(value, AXES, pairs)


def hop_on(slot, core):
    return slot if core == 0 else 4 - slot


def swap_x(values):
    out = [values[0]]
    for slot in (1, 2, 3):
        out.append(moved(values[slot], lambda y, x, frame: (y, (x + hop_on(slot, frame % 2)) % 4, frame)))
    return out


def gather_y(value):
    out = []
    for slot in (1, 2, 3):
        out.append(moved(value, lambda y, x, frame: ((y + hop_on(slot, frame % 2)) % 4, x, frame)))
    return out


def along_x(value, hop):
    return moved(value, lambda y, x, frame: (y, (x + hop) % 4, frame))


def along_frame(value, hop):
    return moved(value, lambda y, x, frame: (y, x, (frame + hop) % 16))


def embedding_of(step_index, half_dim):
    frequencies = jnp.exp(-math.log(10000.0) * jnp.arange(half_dim, dtype=F32) / half_dim)
    angles = step_index.astype(F32) * frequencies
    return jnp.concatenate([jnp.cos(angles), jnp.sin(angles)]).astype(BF16)


def local(start_state, step_noise, timesteps, gn_gain, gn_bias, spatial_weight, temporal_weight, temb_weight):
    start = start_state.reshape(1024, 320)
    noise = step_noise.reshape(1024, 320)
    emb = embedding_of(timesteps[0], temb_weight.shape[0] // 2)
    emb = jnp.broadcast_to(jnp.pad(emb, (0, 64))[None], (16, 384))
    packed = (ROWS, LANES)
    four = (4, ROWS, LANES)

    *outgoing, start, wp, tp, tew, gain, bias = call(
        prologue_kernel,
        [((688, 128), BF16)] * 4
        + [((1024, 320), BF16), ((3, 1024, 320), BF16), ((1024, 320), BF16), ((320, 320), BF16), ((320,), F32), ((320,), F32)],
        noise, start, spatial_weight, temporal_weight, temb_weight, gn_gain, gn_bias, emb,
        scratch=(((1024, 320), BF16),),
        hbm=7,
        sems=29,
    )
    arrived = swap_x(outgoing)
    nq, sp = call(norm_start_kernel, [((3, 320, 128), BF16), (packed, BF16)], start, gain, bias)
    before, after = along_frame(nq, 1), along_frame(nq, -1)
    a3 = ((256, 1024), BF16)
    taps = ((320, 1024), BF16)
    run = (packed, F32)
    rt, prefix, noises, tb = call(
        first_sweep_kernel,
        [(packed, BF16), (four, F32), (four, BF16), ((4, 16, 320), F32)],
        nq, before, after, wp, tp, tew, *arrived,
        scratch=(taps, ((3, 256, 320), F32), a3, run),
        flops=2 * 1024 * 320 * 3200,
    )
    totals = gather_y(rt)
    states, up, down, far = call(
        states_kernel,
        [(four, BF16), ((464, 128), BF16), ((464, 128), BF16), ((72, 128), BF16)],
        sp, prefix, *totals,
    )
    activated = call(
        second_sweep_kernel,
        [(four, BF16)],
        states, along_x(up, 1), along_x(down, -1), along_x(far, 2), far, gain, bias, wp, tb,
        scratch=(taps, ((4, 8, 384), F32)),
        flops=2 * 1024 * 320 * 2880,
    )[0]
    rt, prefix = call(
        second_drift_kernel,
        [(packed, BF16), (four, F32)],
        activated, along_frame(activated, 1), along_frame(activated, -1), tp, noises,
        scratch=(a3, run),
        flops=2 * 1024 * 320 * 960,
    )
    totals = gather_y(rt)
    results = call(result_kernel, [(packed, BF16)] * 4, sp, prefix, *totals)
    out = call(unpack_kernel, [((1024, 320), BF16)], *swap_x(results))[0]
    return out.reshape(1, 1, 32, 32, 320)


def solution(mesh):
    split = Mesh(mesh.devices.reshape(4, 4, 8, 2), AXES)
    steps, frames = ("y", "x"), ("z", "core")
    placed = (
        P(frames, None, None, None),
        P(steps, frames, None, None, None),
        P(steps),
        P(),
        P(),
        P(),
        P(),
        P(),
    )
    return jax.shard_map(
        local,
        mesh=split,
        in_specs=placed,
        out_specs=P(steps, frames, None, None, None),
        check_vma=False,
    )
```

```python
import functools
import math

import jax
import jax.numpy as jnp
from jax import lax
from jax.experimental import pallas as pl
from jax.experimental.pallas import tpu as pltpu
from jax.sharding import Mesh, PartitionSpec as P


F32, BF16 = jnp.float32, jnp.bfloat16
AXES = ("y", "x", "z", "core")
HIGHEST = lax.Precision.HIGHEST

POS, ROWS, LANES = 256, 640, 128


def silu(a):
    half = 0.5 * a
    return half + half * jnp.tanh(half)


def low_lanes(rows):
    return lax.broadcasted_iota(jnp.int32, (rows, LANES), 1) < 64


def swapped(tile):
    return pltpu.roll(tile, 64, 1)


def pack_tail(tail):
    return jnp.concatenate([tail[:128], tail[128:]], axis=1)


def twice(tail):
    return jnp.concatenate([tail, tail], axis=1)


def spread_tail(tile):
    low, other = low_lanes(128), swapped(tile)
    return jnp.concatenate([jnp.where(low, tile, other), jnp.where(low, other, tile)], axis=0)


def same_group(size):
    rows = lax.broadcasted_iota(jnp.int32, (size, size), 0)
    columns = lax.broadcasted_iota(jnp.int32, (size, size), 1)
    return (((rows * 6554) >> 16) == ((columns * 6554) >> 16)).astype(F32)


def group_sum(sums, members):
    return jnp.dot(sums, members, precision=HIGHEST, preferred_element_type=F32)


def store_taps(taps, tiles):
    column = lax.broadcasted_iota(jnp.int32, (320, LANES), 0) & 31
    low = low_lanes(320)
    shifted = []
    for place, step in enumerate((-1, 0, 1)):
        moved = []
        for tile in tiles:
            if step:
                tile = pltpu.roll(tile, -step % 320, 0)
                tile = jnp.where(column == (0 if step < 0 else 31), 0.0, tile)
            moved.append(tile)
        taps[:, place * 256 : place * 256 + 128] = moved[0].astype(BF16)
        taps[:, place * 256 + 128 : place * 256 + 256] = moved[1].astype(BF16)
        shifted.append(moved[2])
    taps[:, 768:896] = jnp.where(low, shifted[0], shifted[1]).astype(BF16)
    taps[:, 896:1024] = jnp.where(low, shifted[2], 0.0).astype(BF16)


def conv_rows(taps, wp):
    total = None
    for row in range(3):
        term = jnp.dot(taps[row * 32 : row * 32 + POS, :], wp[row], preferred_element_type=F32)
        total = term if total is None else total + term
    return total


def hop_of(slot):
    return jnp.where(lax.axis_index("core") == 0, slot, (4 - slot) % 4)


def pack_kernel(noise_hbm, emb, o0, o1, o2, o3, noise, sems):
    x = lax.axis_index("x")
    outs = {0: o0, 1: o1, 2: o2, 3: o3}
    copies = {}
    for slot in (1, 3, 2, 0):
        at = pl.multiple_of(lax.rem(x + hop_of(slot), 4) * POS, POS)
        copies[slot] = pltpu.make_async_copy(noise_hbm.at[pl.ds(at, POS)], noise.at[slot], sems.at[slot])
        copies[slot].start()
    for slot, copy in copies.items():
        out = outs[slot]
        copy.wait()
        out[0:256] = noise[slot, :, 0:128]
        out[256:512] = noise[slot, :, 128:256]
        out[512:640] = pack_tail(noise[slot, :, 256:320].astype(F32)).astype(BF16)
        for tile in range(3):
            out[640 + 16 * tile : 656 + 16 * tile] = emb[:, tile * 128 : tile * 128 + 128]


def norm_start_kernel(
    start_hbm, gain_hbm, bias_hbm, sw, tw, tew_hbm, nq, sp, wp, tp, tew, gain_ref, bias_ref, start, sems
):
    x = lax.axis_index("x")
    frame = lax.axis_index("z") * 2 + lax.axis_index("core")
    moves = [(start_hbm, start), (gain_hbm, gain_ref), (bias_hbm, bias_ref)]
    for row in range(4):
        out = tp if row == 3 else wp.at[row]
        for place in range(3):
            one = tw.at[place] if row == 3 else sw.at[row, place]
            moves.append((one.at[0:256], out.at[place * 256 : place * 256 + 256]))
            moves.append((one.at[256:320], out.at[768 + 64 * place : 832 + 64 * place]))
    moves.append((tew_hbm, tew))
    copies = [pltpu.make_async_copy(source, target, sems.at[i]) for i, (source, target) in enumerate(moves)]
    for copy in copies:
        copy.start()
    members = same_group(320)
    for row in range(3):
        wp[row, 960:1024] = jnp.zeros((64, 320), BF16)
    tp[960:1024] = jnp.zeros((64, 320), BF16)
    for copy in copies[:3]:
        copy.wait()
    values = start[...].astype(F32)
    mean = group_sum(jnp.broadcast_to(jnp.sum(values, axis=0, keepdims=True), (8, 320)), members)[0:1] * (1.0 / 10240)
    centered = start[...].astype(F32) - mean
    spread = jnp.sum(centered * centered, axis=0, keepdims=True)
    var = group_sum(jnp.broadcast_to(spread, (8, 320)), members)[0:1] * (1.0 / 10240)
    scale = lax.rsqrt(var + 1e-05)
    gain, bias = gain_ref[...].reshape(1, 320), bias_ref[...].reshape(1, 320)
    first = pl.multiple_of(x * POS, POS)
    above = pl.multiple_of(jnp.maximum(x * POS - 32, 0), 32)
    below = pl.multiple_of(jnp.minimum(x * POS + POS, 992), 32)
    for at, size, rows, kept in (
        (above, 32, 0, x > 0),
        (first, POS, 32, None),
        (below, 32, 288, x < 3),
    ):
        block = start[pl.ds(at, size), :].astype(F32)
        normed = silu((block - mean) * scale * gain + bias)
        if kept is not None:
            normed = jnp.where(kept, normed, 0.0)
        nq[0, rows : rows + size] = normed[:, 0:128].astype(BF16)
        nq[1, rows : rows + size] = normed[:, 128:256].astype(BF16)
        nq[2, rows : rows + size] = twice(normed[:, 256:320]).astype(BF16)
    sp[0:256] = start[pl.ds(first, POS), 0:128]
    sp[256:512] = start[pl.ds(first, POS), 128:256]
    sp[512:640] = pack_tail(start[pl.ds(first, POS), 256:320].astype(F32)).astype(BF16)
    for copy in copies[3:]:
        copy.wait()
    for place, missing in ((0, frame == 0), (2, frame == 15)):

        @pl.when(missing)
        def _():
            tp[place * 256 : place * 256 + 256] = jnp.zeros((256, 320), BF16)
            tp[768 + 64 * place : 832 + 64 * place] = jnp.zeros((64, 320), BF16)


def first_conv_kernel(*refs):
    *normed, wp, pre, taps = refs
    for place, one in enumerate(normed):
        store_taps(taps, [one[i].astype(F32) for i in range(3)])
        pre[place] = conv_rows(taps, wp)


SPANS = ((0, 256), (256, 512), (512, 640))


def packed_update(a3, tp):
    update = jnp.dot(a3, tp[...], preferred_element_type=F32)
    return update[:, 0:128], update[:, 128:256], pack_tail(update[:, 256:320])


def store_frames(a3, parts):
    for place, part in enumerate(parts):
        a3[:, place * 256 : place * 256 + 256] = part[:, 0:256].astype(BF16)
    a3[:, 768:896] = jnp.concatenate([parts[0][:, 256:320], parts[1][:, 256:320]], axis=1).astype(BF16)
    last = parts[2][:, 256:320]
    a3[:, 896:1024] = jnp.concatenate([last, jnp.zeros_like(last)], axis=1).astype(BF16)


def first_total_kernel(here, sides, tp, tew, n0, n1, n2, n3, rt, noise, tb, a3s, sums, a3):
    x = lax.axis_index("x")
    for slot, one in enumerate((n0, n1, n2, n3)):
        step = lax.rem(x + 4 - hop_of(slot), 4)
        noise[step] = one[0:640]
        bias = (
            jnp.dot(one[640:656], tew[0:128], preferred_element_type=F32)
            + jnp.dot(one[656:672], tew[128:256], preferred_element_type=F32)
            + jnp.dot(one[672:688, 0:64], tew[256:320], preferred_element_type=F32)
        )
        tb[step] = bias / (1.0 + jnp.exp(-bias))
    sums[...] = jnp.zeros_like(sums)

    def one_step(step, carry):
        bias = tb[step][0:1]
        parts = []
        for place, pre in enumerate((sides.at[0], here.at[0], sides.at[1])):
            activated = silu(pre[...] + bias)
            sums[place] += activated
            parts.append(activated)
        store_frames(a3s.at[step], parts)
        return carry

    lax.fori_loop(0, 4, one_step, 0)
    store_frames(a3, [sums[place] for place in range(3)])
    for update, (a, b) in zip(packed_update(a3[...], tp), SPANS):
        total = update
        for step in range(4):
            total = total + noise[step, a:b].astype(F32)
        rt[a:b] = (0.25 * total).astype(BF16)


def first_prefix_kernel(a3s, tp, noise, prefix):
    prefix[0] = jnp.zeros((ROWS, LANES), F32)

    def one_step(step, carry):
        for update, (a, b) in zip(packed_update(a3s[step], tp), SPANS):
            prefix[step + 1, a:b] = prefix[step, a:b] + 0.25 * (update + noise[step, a:b].astype(F32))
        return carry

    lax.fori_loop(0, 3, one_step, 0)


def dup_third(parts):
    third = parts[:, 256:384]
    third = jnp.where(low_lanes(third.shape[0]), third, swapped(third))
    return jnp.concatenate([parts[:, 0:256], third], axis=1)


def offset_of(totals):
    y = lax.axis_index("y")
    kept = [jnp.where(y >= hop_of(slot), one[...].astype(F32), 0.0) for slot, one in enumerate(totals, 1)]
    return kept[0] + kept[1] + kept[2]


def position_sum(tiles):
    sums = [jnp.sum(tile, axis=0, keepdims=True) for tile in tiles]
    third = jnp.broadcast_to(sums[2], (8, LANES))
    return jnp.concatenate(sums[:2] + [(third + swapped(third))[0:1]], axis=1)


def states_kernel(sp, prefix, r1, r2, r3, states, up, down, far):
    members = same_group(384)
    base = sp[...].astype(F32) + offset_of((r1, r2, r3))
    spans = ((0, 256), (256, 512), (512, 640))
    sums = []
    for step in range(4):
        states[step] = (base + prefix[step]).astype(BF16)
        sums.append(position_sum([states[step, a:b].astype(F32) for a, b in spans]))
        for i, (first, last) in enumerate(((0, 224), (256, 480), (512, 608))):
            at = step * 96 + i * 32
            up[at : at + 32] = states[step, last : last + 32]
            down[at : at + 32] = states[step, first : first + 32]
    means = dup_third(group_sum(jnp.concatenate(sums + sums, axis=0), members) * (1.0 / 2560))
    spreads = []
    for step in range(4):
        mean = means[step : step + 1]
        centered = [states[step, a:b].astype(F32) - mean[:, 128 * i : 128 * i + 128] for i, (a, b) in enumerate(spans)]
        spreads.append(position_sum([c * c for c in centered]))
    spread = dup_third(group_sum(jnp.concatenate(spreads + spreads, axis=0), members))
    rest = jnp.concatenate([means[0:4], spread[0:4]], axis=0)
    for part in range(3):
        piece = rest.astype(BF16)
        rest = rest - piece.astype(F32)
        for tile in range(3):
            at = (part * 3 + tile) * 8
            value = piece[:, tile * 128 : tile * 128 + 128]
            far[at : at + 8] = value
            up[384 + at : 392 + at] = value
            down[384 + at : 392 + at] = value


def stats_of(ref, base):
    total = None
    for part in range(3):
        piece = jnp.concatenate(
            [ref[base + (part * 3 + t) * 8 : base + (part * 3 + t) * 8 + 8].astype(F32) for t in range(3)], axis=1
        )
        total = piece if total is None else total + piece
    return total[0:4], total[4:8]


def wide(vector):
    vector = vector[...].reshape(1, 320)
    return jnp.concatenate([vector, vector[:, 256:320]], axis=1)


def second_sweep_kernel(first, states, above, below, far, mine, gain_ref, bias_ref, wp, tb, out, taps, scales):
    gain, bias = wide(gain_ref), wide(bias_ref)
    x = lax.axis_index("x")
    parts = [stats_of(mine, 0), stats_of(above, 384), stats_of(below, 384), stats_of(far, 0)]
    mean = (parts[0][0] + parts[1][0] + parts[2][0] + parts[3][0]) * 0.25
    spread = parts[0][1] + parts[1][1] + parts[2][1] + parts[3][1]
    for one in parts:
        spread = spread + 2560.0 * (one[0] - mean) * (one[0] - mean)
    rstd = lax.rsqrt(spread * (1.0 / 10240) + 1e-05)
    for step in range(4):
        scales[step, 0:1] = mean[step : step + 1]
        scales[step, 1:2] = rstd[step : step + 1]

    def one_step(local_step, carry):
        step = local_step + first
        here = scales[step]

        def normed(value, tile):
            lanes = slice(tile * 128, tile * 128 + 128)
            value = (value.astype(F32) - here[0:1, lanes]) * here[1:2, lanes]
            return silu(value * gain[:, lanes] + bias[:, lanes])

        edge = pl.multiple_of(step * 96, 32)
        tiles = []
        low = low_lanes(32)
        for tile in range(3):
            top = normed(above[pl.ds(edge + 32 * tile, 32)], tile)
            bottom = normed(below[pl.ds(edge + 32 * tile, 32)], tile)
            if tile < 2:
                middle = normed(states[step, 256 * tile : 256 * tile + 256], tile)
            else:
                middle = spread_tail(normed(states[step, 512:640], 2))
                top = jnp.where(low, swapped(top), top)
                bottom = jnp.where(low, bottom, swapped(bottom))
            top = jnp.where(x > 0, top, 0.0)
            bottom = jnp.where(x < 3, bottom, 0.0)
            tiles.append(jnp.concatenate([top, middle, bottom], axis=0))
        store_taps(taps, tiles)
        activated = silu(conv_rows(taps, wp) + tb[step][0:1])
        out[local_step, 0:256] = activated[:, 0:128].astype(BF16)
        out[local_step, 256:512] = activated[:, 128:256].astype(BF16)
        out[local_step, 512:640] = pack_tail(activated[:, 256:320]).astype(BF16)
        return carry

    lax.fori_loop(0, 2, one_step, 0)


def store_packed_frames(a3, tiles):
    low = low_lanes(POS)
    tails = []
    for place, (first, second, tail) in enumerate(tiles):
        a3[:, place * 256 : place * 256 + 128] = first.astype(BF16)
        a3[:, place * 256 + 128 : place * 256 + 256] = second.astype(BF16)
        tails.append(spread_tail(tail))
    a3[:, 768:896] = jnp.where(low, tails[0], tails[1]).astype(BF16)
    a3[:, 896:1024] = jnp.where(low, tails[2], 0.0).astype(BF16)


def second_total_kernel(own0, own1, before0, before1, after0, after1, tp, noise, rt, a3):
    tiles = []
    for pair in ((before0, before1), (own0, own1), (after0, after1)):
        parts = []
        for a, b in SPANS:
            ones = [half[step, a:b].astype(F32) for half in pair for step in range(2)]
            parts.append((ones[0] + ones[1]) + (ones[2] + ones[3]))
        tiles.append(parts)
    store_packed_frames(a3, tiles)
    for update, (a, b) in zip(packed_update(a3[...], tp), SPANS):
        total = update
        for step in range(4):
            total = total + noise[step, a:b].astype(F32)
        rt[a:b] = (0.25 * total).astype(BF16)


def second_prefix_kernel(own0, own1, before0, before1, after0, after1, tp, noise, prefix, a3):
    for step in range(4):
        tiles = []
        for pair in ((before0, before1), (own0, own1), (after0, after1)):
            half = pair[step // 2]
            tiles.append([half[step % 2, a:b].astype(F32) for a, b in SPANS])
        store_packed_frames(a3, tiles)
        for update, (a, b) in zip(packed_update(a3[...], tp), SPANS):
            now = 0.25 * (update + noise[step, a:b].astype(F32))
            prefix[step, a:b] = now if step == 0 else prefix[step - 1, a:b] + now


def result_kernel(sp, prefix, r1, r2, r3, *outs):
    x = lax.axis_index("x")
    base = sp[...].astype(F32) + offset_of((r1, r2, r3))
    for slot, out in enumerate(outs):
        out[...] = (base + prefix[lax.rem(x + hop_of(slot), 4)]).astype(BF16)


def unpack_kernel(r0, r1, r2, r3, out):
    x = lax.axis_index("x")
    for slot, one in enumerate((r0, r1, r2, r3)):
        start = pl.multiple_of(lax.rem(x + 4 - hop_of(slot), 4) * POS, POS)
        out[pl.ds(start, POS), 0:128] = one[0:256]
        out[pl.ds(start, POS), 128:256] = one[256:512]
        tail = spread_tail(one[512:640].astype(F32))
        out[pl.ds(start, POS), 256:320] = tail[:, 0:64].astype(BF16)


def call(body, outs, *args, scratch=(), flops=0, limit=24, hbm=0, sems=0):
    shapes = [jax.ShapeDtypeStruct(shape, kind) for shape, kind in outs]
    vmem = pl.BlockSpec(memory_space=pltpu.VMEM)
    nbytes = sum(a.size * a.dtype.itemsize for a in args) + sum(s.size * s.dtype.itemsize for s in shapes)
    scratch_shapes = [pltpu.VMEM(shape, kind) for shape, kind in scratch]
    if sems:
        scratch_shapes.append(pltpu.SemaphoreType.DMA((sems,)))
    return pl.pallas_call(
        body,
        out_shape=shapes,
        in_specs=[pl.BlockSpec(memory_space=pltpu.HBM)] * hbm + [vmem] * (len(args) - hbm),
        out_specs=[vmem] * len(shapes),
        scratch_shapes=scratch_shapes,
        compiler_params=pltpu.CompilerParams(vmem_limit_bytes=limit << 20),
        cost_estimate=pl.CostEstimate(flops=flops, bytes_accessed=nbytes, transcendentals=0),
    )(*(pltpu.with_memory_space_constraint(a, pltpu.HBM) if i < hbm else a for i, a in enumerate(args)))


def moved(value, place):
    pairs = []
    for y in range(4):
        for x in range(4):
            for z in range(8):
                for core in range(2):
                    ty, tx, frame = place(y, x, z * 2 + core)
                    pairs.append(((y * 4 + x) * 16 + z * 2 + core, (ty * 4 + tx) * 16 + frame))
    return lax.ppermute(value, AXES, pairs)


def hop_on(slot, core):
    return slot if core == 0 else 4 - slot


def swap_x(values):
    out = [values[0]]
    for slot in (1, 2, 3):
        out.append(moved(values[slot], lambda y, x, frame: (y, (x + hop_on(slot, frame % 2)) % 4, frame)))
    return out


def gather_y(value):
    out = []
    for slot in (1, 2, 3):
        out.append(moved(value, lambda y, x, frame: ((y + hop_on(slot, frame % 2)) % 4, x, frame)))
    return out


def along_x(value, hop):
    return moved(value, lambda y, x, frame: (y, (x + hop) % 4, frame))


def along_frame(value, hop):
    return moved(value, lambda y, x, frame: (y, x, (frame + hop) % 16))


def embedding_of(step_index, half_dim):
    frequencies = jnp.exp(-math.log(10000.0) * jnp.arange(half_dim, dtype=F32) / half_dim)
    angles = step_index.astype(F32) * frequencies
    return jnp.concatenate([jnp.cos(angles), jnp.sin(angles)]).astype(BF16)


def local(start_state, step_noise, timesteps, gn_gain, gn_bias, spatial_weight, temporal_weight, temb_weight):
    start = start_state.reshape(1024, 320)
    noise = step_noise.reshape(1024, 320)
    emb = embedding_of(timesteps[0], temb_weight.shape[0] // 2)
    emb = jnp.broadcast_to(jnp.pad(emb, (0, 64))[None], (16, 384))
    packed = (ROWS, LANES)
    four = (4, ROWS, LANES)

    *outgoing, = call(
        pack_kernel, [((688, 128), BF16)] * 4, noise, emb, scratch=(((4, 256, 320), BF16),), hbm=1, sems=4
    )
    arrived = swap_x(outgoing)
    nq, sp, wp, tp, tew, gain, bias = call(
        norm_start_kernel,
        [((3, 320, 128), BF16), (packed, BF16), ((3, 1024, 320), BF16), ((1024, 320), BF16), ((320, 320), BF16)]
        + [((320,), F32)] * 2,
        start, gn_gain, gn_bias, spatial_weight, temporal_weight, temb_weight,
        scratch=(((1024, 320), BF16),),
        hbm=6,
        sems=28,
    )
    before, after = along_frame(nq, 1), along_frame(nq, -1)
    taps = ((320, 1024), BF16)
    a3 = ((256, 1024), BF16)
    pre = (256, 320)
    here = call(first_conv_kernel, [((1,) + pre, F32)], nq, wp, scratch=(taps,), flops=512 * 320 * 2880)[0]
    sides = call(first_conv_kernel, [((2,) + pre, F32)], before, after, wp, scratch=(taps,), flops=1024 * 320 * 2880)[0]
    rt, noises, tb, a3s = call(
        first_total_kernel,
        [(packed, BF16), (four, BF16), ((4, 16, 320), F32), ((4, 256, 1024), BF16)],
        here, sides, tp, tew, *arrived,
        scratch=(((3, 256, 320), F32), a3),
        flops=512 * 320 * 960,
    )
    totals = gather_y(rt)
    prefix = call(first_prefix_kernel, [(four, F32)], a3s, tp, noises, flops=3 * 512 * 320 * 960)[0]
    states, up, down, far = call(
        states_kernel,
        [(four, BF16), ((464, 128), BF16), ((464, 128), BF16), ((72, 128), BF16)],
        sp, prefix, *totals,
    )
    edges = along_x(up, 1), along_x(down, -1), along_x(far, 2), far
    halves = []
    for half in (0, 1):
        own = call(
            functools.partial(second_sweep_kernel, 2 * half),
            [((2, ROWS, LANES), BF16)],
            states, *edges, gain, bias, wp, tb,
            scratch=(taps, ((4, 8, 384), F32)),
            flops=1024 * 320 * 2880,
        )[0]
        halves.append((own, along_frame(own, 1), along_frame(own, -1)))
    parts = [half[i] for i in range(3) for half in halves]
    rt = call(second_total_kernel, [(packed, BF16)], *parts, tp, noises, scratch=(a3,), flops=512 * 320 * 960)[0]
    totals = gather_y(rt)
    prefix = call(second_prefix_kernel, [(four, F32)], *parts, tp, noises, scratch=(a3,), flops=2048 * 320 * 960)[0]
    results = call(result_kernel, [(packed, BF16)] * 4, sp, prefix, *totals)
    out = call(unpack_kernel, [((1024, 320), BF16)], *swap_x(results))[0]
    return out.reshape(1, 1, 32, 32, 320)


def solution(mesh):
    split = Mesh(mesh.devices.reshape(4, 4, 8, 2), AXES)
    steps, frames = ("y", "x"), ("z", "core")
    placed = (
        P(frames, None, None, None),
        P(steps, frames, None, None, None),
        P(steps),
        P(),
        P(),
        P(),
        P(),
        P(),
    )
    return jax.shard_map(
        local,
        mesh=split,
        in_specs=placed,
        out_specs=P(steps, frames, None, None, None),
        check_vma=False,
    )
```

```python
import functools
import math

import jax
import jax.numpy as jnp
from jax import lax
from jax.experimental import pallas as pl
from jax.experimental.pallas import tpu as pltpu
from jax.sharding import Mesh, PartitionSpec as P


F32, BF16 = jnp.float32, jnp.bfloat16
AXES = ("y", "x", "z", "core")
HIGHEST = lax.Precision.HIGHEST

POS, ROWS, LANES = 256, 640, 128


def silu(a):
    half = 0.5 * a
    return half + half * jnp.tanh(half)


def low_lanes(rows):
    return lax.broadcasted_iota(jnp.int32, (rows, LANES), 1) < 64


def swapped(tile):
    return pltpu.roll(tile, 64, 1)


def pack_tail(tail):
    half = tail.shape[0] // 2
    return jnp.concatenate([tail[:half], tail[half:]], axis=1)


def spread_tail(tile):
    low, other = low_lanes(tile.shape[0]), swapped(tile)
    return jnp.concatenate([jnp.where(low, tile, other), jnp.where(low, other, tile)], axis=0)


def same_group(size):
    rows = lax.broadcasted_iota(jnp.int32, (size, size), 0)
    columns = lax.broadcasted_iota(jnp.int32, (size, size), 1)
    return (((rows * 6554) >> 16) == ((columns * 6554) >> 16)).astype(F32)


def group_sum(sums, members):
    return jnp.dot(sums, members, precision=HIGHEST, preferred_element_type=F32)


def store_taps(taps, tiles):
    column = lax.broadcasted_iota(jnp.int32, (320, LANES), 0) & 31
    low = low_lanes(320)
    shifted = []
    for place, step in enumerate((-1, 0, 1)):
        moved = []
        for tile in tiles:
            if step:
                tile = pltpu.roll(tile, -step % 320, 0)
                tile = jnp.where(column == (0 if step < 0 else 31), 0.0, tile)
            moved.append(tile)
        taps[:, place * 256 : place * 256 + 128] = moved[0].astype(BF16)
        taps[:, place * 256 + 128 : place * 256 + 256] = moved[1].astype(BF16)
        shifted.append(moved[2])
    taps[:, 768:896] = jnp.where(low, shifted[0], shifted[1]).astype(BF16)
    taps[:, 896:1024] = jnp.where(low, shifted[2], 0.0).astype(BF16)


def conv_rows(taps, wp):
    total = None
    for row in range(3):
        term = jnp.dot(taps[row * 32 : row * 32 + POS, :], wp[row], preferred_element_type=F32)
        total = term if total is None else total + term
    return total


def hop_of(slot):
    return jnp.where(lax.axis_index("core") == 0, slot, (4 - slot) % 4)


def pack_kernel(noise_hbm, start_hbm, gain_hbm, bias_hbm, emb, o0, o1, o2, o3, start, gain, bias, noise, sems):
    x = lax.axis_index("x")
    outs = {0: o0, 1: o1, 2: o2, 3: o3}
    copies = {}
    for slot in (2, 1, 3, 0):
        at = pl.multiple_of(lax.rem(x + hop_of(slot), 4) * POS, POS)
        copies[slot] = pltpu.make_async_copy(noise_hbm.at[pl.ds(at, POS)], noise.at[slot], sems.at[slot])
        copies[slot].start()
    rest = [
        pltpu.make_async_copy(source, target, sems.at[4 + i])
        for i, (source, target) in enumerate(((start_hbm, start), (gain_hbm, gain), (bias_hbm, bias)))
    ]
    for copy in rest:
        copy.start()
    for slot, copy in copies.items():
        out = outs[slot]
        copy.wait()
        out[0:256] = noise[slot, :, 0:128]
        out[256:512] = noise[slot, :, 128:256]
        out[512:640] = pack_tail(noise[slot, :, 256:320].astype(F32)).astype(BF16)
        for tile in range(3):
            out[640 + 16 * tile : 656 + 16 * tile] = emb[:, tile * 128 : tile * 128 + 128]
    for copy in rest:
        copy.wait()


def norm_start_kernel(sw, tw, tew_hbm, start, gain_ref, bias_ref, nq, sp, wp, tp, tew, sems):
    x = lax.axis_index("x")
    frame = lax.axis_index("z") * 2 + lax.axis_index("core")
    moves = []
    for row in range(4):
        out = tp if row == 3 else wp.at[row]
        for place in range(3):
            one = tw.at[place] if row == 3 else sw.at[row, place]
            moves.append((one.at[0:256], out.at[place * 256 : place * 256 + 256]))
            moves.append((one.at[256:320], out.at[768 + 64 * place : 832 + 64 * place]))
    moves.append((tew_hbm, tew))
    copies = [pltpu.make_async_copy(source, target, sems.at[i]) for i, (source, target) in enumerate(moves)]
    for copy in copies:
        copy.start()
    members = same_group(320)
    for row in range(3):
        wp[row, 960:1024] = jnp.zeros((64, 320), BF16)
    tp[960:1024] = jnp.zeros((64, 320), BF16)
    values = start[...].astype(F32)
    mean = group_sum(jnp.broadcast_to(jnp.sum(values, axis=0, keepdims=True), (8, 320)), members)[0:1] * (1.0 / 10240)
    centered = start[...].astype(F32) - mean
    spread = jnp.sum(centered * centered, axis=0, keepdims=True)
    var = group_sum(jnp.broadcast_to(spread, (8, 320)), members)[0:1] * (1.0 / 10240)
    scale = lax.rsqrt(var + 1e-05)
    gain, bias = gain_ref[...].reshape(1, 320), bias_ref[...].reshape(1, 320)
    first = pl.multiple_of(x * POS, POS)
    above = pl.multiple_of(jnp.maximum(x * POS - 32, 0), 32)
    below = pl.multiple_of(jnp.minimum(x * POS + POS, 992), 32)
    pieces = []
    for at, size, kept in ((above, 32, x > 0), (first, POS, None), (below, 32, x < 3)):
        block = start[pl.ds(at, size), :].astype(F32)
        normed = silu((block - mean) * scale * gain + bias)
        pieces.append(normed if kept is None else jnp.where(kept, normed, 0.0))
    normed = jnp.concatenate(pieces, axis=0)
    nq[0:320] = normed[:, 0:128].astype(BF16)
    nq[320:640] = normed[:, 128:256].astype(BF16)
    nq[640:800] = pack_tail(normed[:, 256:320]).astype(BF16)
    sp[0:256] = start[pl.ds(first, POS), 0:128]
    sp[256:512] = start[pl.ds(first, POS), 128:256]
    sp[512:640] = pack_tail(start[pl.ds(first, POS), 256:320].astype(F32)).astype(BF16)
    for copy in copies:
        copy.wait()
    for place, missing in ((0, frame == 0), (2, frame == 15)):

        @pl.when(missing)
        def _():
            tp[place * 256 : place * 256 + 256] = jnp.zeros((256, 320), BF16)
            tp[768 + 64 * place : 832 + 64 * place] = jnp.zeros((64, 320), BF16)


def first_conv_kernel(*refs):
    *normed, wp, pre, taps = refs
    for place, one in enumerate(normed):
        store_taps(taps, [one[0:320].astype(F32), one[320:640].astype(F32), spread_tail(one[640:800].astype(F32))])
        pre[place] = conv_rows(taps, wp)


SPANS = ((0, 256), (256, 512), (512, 640))


def packed_update(a3, tp):
    update = jnp.dot(a3, tp[...], preferred_element_type=F32)
    return update[:, 0:128], update[:, 128:256], pack_tail(update[:, 256:320])


def store_frames(a3, parts):
    for place, part in enumerate(parts):
        a3[:, place * 256 : place * 256 + 256] = part[:, 0:256].astype(BF16)
    a3[:, 768:896] = jnp.concatenate([parts[0][:, 256:320], parts[1][:, 256:320]], axis=1).astype(BF16)
    last = parts[2][:, 256:320]
    a3[:, 896:1024] = jnp.concatenate([last, jnp.zeros_like(last)], axis=1).astype(BF16)


def first_total_kernel(here, sides, tp, tew, n0, n1, n2, n3, rt, noise, tb, a3s, sums, a3):
    x = lax.axis_index("x")
    arrived = (n0, n1, n2, n3)
    bias = None
    for at, rows in ((640, slice(0, 128)), (656, slice(128, 256)), (672, slice(256, 320))):
        emb = jnp.concatenate([one[at : at + 16, 0 : rows.stop - rows.start] for one in arrived], axis=0)
        term = jnp.dot(emb, tew[rows], preferred_element_type=F32)
        bias = term if bias is None else bias + term
    bias = bias / (1.0 + jnp.exp(-bias))
    for slot, one in enumerate(arrived):
        step = lax.rem(x + 4 - hop_of(slot), 4)
        noise[step] = one[0:640]
        tb[step] = bias[slot * 16 : slot * 16 + 16]
    sums[...] = jnp.zeros_like(sums)

    def one_step(step, carry):
        bias = tb[step][0:1]
        parts = []
        for place, pre in enumerate((sides.at[0], here.at[0], sides.at[1])):
            activated = silu(pre[...] + bias)
            sums[place] += activated
            parts.append(activated)
        store_frames(a3s.at[step], parts)
        return carry

    lax.fori_loop(0, 4, one_step, 0)
    store_frames(a3, [sums[place] for place in range(3)])
    for update, (a, b) in zip(packed_update(a3[...], tp), SPANS):
        total = update
        for step in range(4):
            total = total + noise[step, a:b].astype(F32)
        rt[a:b] = (0.25 * total).astype(BF16)


def first_prefix_kernel(a3s, tp, noise, prefix):
    prefix[0] = jnp.zeros((ROWS, LANES), F32)

    def one_step(step, carry):
        for update, (a, b) in zip(packed_update(a3s[step], tp), SPANS):
            prefix[step + 1, a:b] = prefix[step, a:b] + 0.25 * (update + noise[step, a:b].astype(F32))
        return carry

    lax.fori_loop(0, 3, one_step, 0)


def dup_third(parts):
    third = parts[:, 256:384]
    third = jnp.where(low_lanes(third.shape[0]), third, swapped(third))
    return jnp.concatenate([parts[:, 0:256], third], axis=1)


def offset_of(totals):
    y = lax.axis_index("y")
    kept = [jnp.where(y >= hop_of(slot), one[...].astype(F32), 0.0) for slot, one in enumerate(totals, 1)]
    return kept[0] + kept[1] + kept[2]


def position_sum(tiles):
    sums = [jnp.sum(tile, axis=0, keepdims=True) for tile in tiles]
    third = jnp.broadcast_to(sums[2], (8, LANES))
    return jnp.concatenate(sums[:2] + [(third + swapped(third))[0:1]], axis=1)


def states_kernel(sp, prefix, r1, r2, r3, states, up, down, far):
    members = same_group(384)
    base = sp[...].astype(F32) + offset_of((r1, r2, r3))
    spans = ((0, 256), (256, 512), (512, 640))
    sums = []
    for step in range(4):
        states[step] = (base + prefix[step]).astype(BF16)
        sums.append(position_sum([states[step, a:b].astype(F32) for a, b in spans]))
        for i, (first, last) in enumerate(((0, 224), (256, 480), (512, 608))):
            at = step * 96 + i * 32
            up[at : at + 32] = states[step, last : last + 32]
            down[at : at + 32] = states[step, first : first + 32]
    means = dup_third(group_sum(jnp.concatenate(sums + sums, axis=0), members) * (1.0 / 2560))
    spreads = []
    for step in range(4):
        mean = means[step : step + 1]
        centered = [states[step, a:b].astype(F32) - mean[:, 128 * i : 128 * i + 128] for i, (a, b) in enumerate(spans)]
        spreads.append(position_sum([c * c for c in centered]))
    spread = dup_third(group_sum(jnp.concatenate(spreads + spreads, axis=0), members))
    rest = jnp.concatenate([means[0:4], spread[0:4]], axis=0)
    for part in range(3):
        piece = rest.astype(BF16)
        rest = rest - piece.astype(F32)
        for tile in range(3):
            at = (part * 3 + tile) * 8
            value = piece[:, tile * 128 : tile * 128 + 128]
            far[at : at + 8] = value
            up[384 + at : 392 + at] = value
            down[384 + at : 392 + at] = value


def stats_of(ref, base):
    total = None
    for part in range(3):
        piece = jnp.concatenate(
            [ref[base + (part * 3 + t) * 8 : base + (part * 3 + t) * 8 + 8].astype(F32) for t in range(3)], axis=1
        )
        total = piece if total is None else total + piece
    return total[0:4], total[4:8]


def wide(vector):
    vector = vector[...].reshape(1, 320)
    return jnp.concatenate([vector, vector[:, 256:320]], axis=1)


def second_sweep_kernel(first, states, above, below, far, mine, gain_ref, bias_ref, wp, tb, *refs):
    if first:
        earlier, out, total, taps, scales = refs
    else:
        out, taps, scales = refs
    gain, bias = wide(gain_ref), wide(bias_ref)
    x = lax.axis_index("x")
    parts = [stats_of(mine, 0), stats_of(above, 384), stats_of(below, 384), stats_of(far, 0)]
    mean = (parts[0][0] + parts[1][0] + parts[2][0] + parts[3][0]) * 0.25
    spread = parts[0][1] + parts[1][1] + parts[2][1] + parts[3][1]
    for one in parts:
        spread = spread + 2560.0 * (one[0] - mean) * (one[0] - mean)
    rstd = lax.rsqrt(spread * (1.0 / 10240) + 1e-05)
    for step in range(4):
        scales[step, 0:1] = mean[step : step + 1]
        scales[step, 1:2] = rstd[step : step + 1]

    def one_step(local_step, carry):
        step = local_step + first
        here = scales[step]

        def normed(value, tile):
            lanes = slice(tile * 128, tile * 128 + 128)
            value = (value.astype(F32) - here[0:1, lanes]) * here[1:2, lanes]
            return silu(value * gain[:, lanes] + bias[:, lanes])

        edge = pl.multiple_of(step * 96, 32)
        tiles = []
        low = low_lanes(32)
        for tile in range(3):
            top = normed(above[pl.ds(edge + 32 * tile, 32)], tile)
            bottom = normed(below[pl.ds(edge + 32 * tile, 32)], tile)
            if tile < 2:
                middle = normed(states[step, 256 * tile : 256 * tile + 256], tile)
            else:
                middle = spread_tail(normed(states[step, 512:640], 2))
                top = jnp.where(low, swapped(top), top)
                bottom = jnp.where(low, bottom, swapped(bottom))
            top = jnp.where(x > 0, top, 0.0)
            bottom = jnp.where(x < 3, bottom, 0.0)
            tiles.append(jnp.concatenate([top, middle, bottom], axis=0))
        store_taps(taps, tiles)
        activated = silu(conv_rows(taps, wp) + tb[step][0:1])
        out[local_step, 0:256] = activated[:, 0:128].astype(BF16)
        out[local_step, 256:512] = activated[:, 128:256].astype(BF16)
        out[local_step, 512:640] = pack_tail(activated[:, 256:320]).astype(BF16)
        return carry

    lax.fori_loop(0, 2, one_step, 0)
    if first:
        ones = [half[step].astype(F32) for half in (earlier, out) for step in range(2)]
        total[...] = ((ones[0] + ones[1]) + (ones[2] + ones[3])).astype(BF16)


def store_packed_frames(a3, tiles):
    low = low_lanes(POS)
    tails = []
    for place, (first, second, tail) in enumerate(tiles):
        a3[:, place * 256 : place * 256 + 128] = first.astype(BF16)
        a3[:, place * 256 + 128 : place * 256 + 256] = second.astype(BF16)
        tails.append(spread_tail(tail))
    a3[:, 768:896] = jnp.where(low, tails[0], tails[1]).astype(BF16)
    a3[:, 896:1024] = jnp.where(low, tails[2], 0.0).astype(BF16)


def second_total_kernel(own, before, after, tp, noise, rt, a3):
    store_packed_frames(a3, [[one[a:b].astype(F32) for a, b in SPANS] for one in (before, own, after)])
    for update, (a, b) in zip(packed_update(a3[...], tp), SPANS):
        total = update
        for step in range(4):
            total = total + noise[step, a:b].astype(F32)
        rt[a:b] = (0.25 * total).astype(BF16)


def second_prefix_kernel(own0, own1, before0, before1, after0, after1, tp, noise, prefix, a3):
    for step in range(4):
        tiles = []
        for pair in ((before0, before1), (own0, own1), (after0, after1)):
            half = pair[step // 2]
            tiles.append([half[step % 2, a:b].astype(F32) for a, b in SPANS])
        store_packed_frames(a3, tiles)
        for update, (a, b) in zip(packed_update(a3[...], tp), SPANS):
            now = 0.25 * (update + noise[step, a:b].astype(F32))
            prefix[step, a:b] = now if step == 0 else prefix[step - 1, a:b] + now


def result_kernel(sp, prefix, r1, r2, r3, *outs):
    x = lax.axis_index("x")
    base = sp[...].astype(F32) + offset_of((r1, r2, r3))
    for slot, out in enumerate(outs):
        out[...] = (base + prefix[lax.rem(x + hop_of(slot), 4)]).astype(BF16)


def unpack_kernel(r0, r1, r2, r3, out):
    x = lax.axis_index("x")
    for slot, one in enumerate((r0, r1, r2, r3)):
        start = pl.multiple_of(lax.rem(x + 4 - hop_of(slot), 4) * POS, POS)
        out[pl.ds(start, POS), 0:128] = one[0:256]
        out[pl.ds(start, POS), 128:256] = one[256:512]
        tail = spread_tail(one[512:640].astype(F32))
        out[pl.ds(start, POS), 256:320] = tail[:, 0:64].astype(BF16)


def call(body, outs, *args, scratch=(), flops=0, limit=24, hbm=0, sems=0):
    shapes = [jax.ShapeDtypeStruct(shape, kind) for shape, kind in outs]
    vmem = pl.BlockSpec(memory_space=pltpu.VMEM)
    nbytes = sum(a.size * a.dtype.itemsize for a in args) + sum(s.size * s.dtype.itemsize for s in shapes)
    scratch_shapes = [pltpu.VMEM(shape, kind) for shape, kind in scratch]
    if sems:
        scratch_shapes.append(pltpu.SemaphoreType.DMA((sems,)))
    return pl.pallas_call(
        body,
        out_shape=shapes,
        in_specs=[pl.BlockSpec(memory_space=pltpu.HBM)] * hbm + [vmem] * (len(args) - hbm),
        out_specs=[vmem] * len(shapes),
        scratch_shapes=scratch_shapes,
        compiler_params=pltpu.CompilerParams(vmem_limit_bytes=limit << 20),
        cost_estimate=pl.CostEstimate(flops=flops, bytes_accessed=nbytes, transcendentals=0),
    )(*(pltpu.with_memory_space_constraint(a, pltpu.HBM) if i < hbm else a for i, a in enumerate(args)))


def moved(value, place):
    pairs = []
    for y in range(4):
        for x in range(4):
            for z in range(8):
                for core in range(2):
                    ty, tx, frame = place(y, x, z * 2 + core)
                    pairs.append(((y * 4 + x) * 16 + z * 2 + core, (ty * 4 + tx) * 16 + frame))
    return lax.ppermute(value, AXES, pairs)


def hop_on(slot, core):
    return slot if core == 0 else 4 - slot


def swap_x(values):
    out = [values[0]]
    for slot in (1, 2, 3):
        out.append(moved(values[slot], lambda y, x, frame: (y, (x + hop_on(slot, frame % 2)) % 4, frame)))
    return out


def gather_y(value):
    out = []
    for slot in (1, 2, 3):
        out.append(moved(value, lambda y, x, frame: ((y + hop_on(slot, frame % 2)) % 4, x, frame)))
    return out


def along_x(value, hop):
    return moved(value, lambda y, x, frame: (y, (x + hop) % 4, frame))


def along_frame(value, hop):
    return moved(value, lambda y, x, frame: (y, x, (frame + hop) % 16))


def embedding_of(step_index, half_dim):
    frequencies = jnp.exp(-math.log(10000.0) * jnp.arange(half_dim, dtype=F32) / half_dim)
    angles = step_index.astype(F32) * frequencies
    return jnp.concatenate([jnp.cos(angles), jnp.sin(angles)]).astype(BF16)


def local(start_state, step_noise, timesteps, gn_gain, gn_bias, spatial_weight, temporal_weight, temb_weight):
    start = start_state.reshape(1024, 320)
    noise = step_noise.reshape(1024, 320)
    emb = embedding_of(timesteps[0], temb_weight.shape[0] // 2)
    emb = jnp.broadcast_to(jnp.pad(emb, (0, 64))[None], (16, 384))
    packed = (ROWS, LANES)
    four = (4, ROWS, LANES)

    *outgoing, start, gain, bias = call(
        pack_kernel,
        [((688, 128), BF16)] * 4 + [((1024, 320), BF16), ((320,), F32), ((320,), F32)],
        noise, start, gn_gain, gn_bias, emb,
        scratch=(((4, 256, 320), BF16),),
        hbm=4,
        sems=7,
    )
    arrived = swap_x(outgoing)
    nq, sp, wp, tp, tew = call(
        norm_start_kernel,
        [((800, 128), BF16), (packed, BF16), ((3, 1024, 320), BF16), ((1024, 320), BF16), ((320, 320), BF16)],
        spatial_weight, temporal_weight, temb_weight, start, gain, bias,
        hbm=3,
        sems=25,
    )
    before, after = along_frame(nq, 1), along_frame(nq, -1)
    taps = ((320, 1024), BF16)
    a3 = ((256, 1024), BF16)
    pre = (256, 320)
    here = call(first_conv_kernel, [((1,) + pre, F32)], nq, wp, scratch=(taps,), flops=512 * 320 * 2880)[0]
    sides = call(first_conv_kernel, [((2,) + pre, F32)], before, after, wp, scratch=(taps,), flops=1024 * 320 * 2880)[0]
    rt, noises, tb, a3s = call(
        first_total_kernel,
        [(packed, BF16), (four, BF16), ((4, 16, 320), F32), ((4, 256, 1024), BF16)],
        here, sides, tp, tew, *arrived,
        scratch=(((3, 256, 320), F32), a3),
        flops=512 * 320 * 960,
    )
    totals = gather_y(rt)
    prefix = call(first_prefix_kernel, [(four, F32)], a3s, tp, noises, flops=3 * 512 * 320 * 960)[0]
    states, up, down, far = call(
        states_kernel,
        [(four, BF16), ((464, 128), BF16), ((464, 128), BF16), ((72, 128), BF16)],
        sp, prefix, *totals,
    )
    edges = along_x(up, 1), along_x(down, -1), along_x(far, 2), far
    halves, earlier, outs = [], (), [((2, ROWS, LANES), BF16)]
    for half in (0, 1):
        own, *total = call(
            functools.partial(second_sweep_kernel, 2 * half),
            outs + [(packed, BF16)] * half,
            states, *edges, gain, bias, wp, tb, *earlier,
            scratch=(taps, ((4, 8, 384), F32)),
            flops=1024 * 320 * 2880,
        )
        halves.append((own, along_frame(own, 1), along_frame(own, -1)))
        earlier = (own,)
    parts = [half[i] for i in range(3) for half in halves]
    sums = total[0], along_frame(total[0], 1), along_frame(total[0], -1)
    rt = call(second_total_kernel, [(packed, BF16)], *sums, tp, noises, scratch=(a3,), flops=512 * 320 * 960)[0]
    totals = gather_y(rt)
    prefix = call(second_prefix_kernel, [(four, F32)], *parts, tp, noises, scratch=(a3,), flops=2048 * 320 * 960)[0]
    results = call(result_kernel, [(packed, BF16)] * 4, sp, prefix, *totals)
    out = call(unpack_kernel, [((1024, 320), BF16)], *swap_x(results))[0]
    return out.reshape(1, 1, 32, 32, 320)


def solution(mesh):
    split = Mesh(mesh.devices.reshape(4, 4, 8, 2), AXES)
    steps, frames = ("y", "x"), ("z", "core")
    placed = (
        P(frames, None, None, None),
        P(steps, frames, None, None, None),
        P(steps),
        P(),
        P(),
        P(),
        P(),
        P(),
    )
    return jax.shard_map(
        local,
        mesh=split,
        in_specs=placed,
        out_specs=P(steps, frames, None, None, None),
        check_vma=False,
    )
```

```python
import functools
import math

import jax
import jax.numpy as jnp
from jax import lax
from jax.experimental import pallas as pl
from jax.experimental.pallas import tpu as pltpu
from jax.sharding import Mesh, PartitionSpec as P


F32, BF16 = jnp.float32, jnp.bfloat16
AXES = ("y", "x", "z", "core")

POS, ROWS, LANES = 256, 640, 128


def silu(a):
    half = 0.5 * a
    return half + half * jnp.tanh(half)


def low_lanes(rows):
    return lax.broadcasted_iota(jnp.int32, (rows, LANES), 1) < 64


def swapped(tile):
    return pltpu.roll(tile, 64, 1)


def pack_tail(tail):
    half = tail.shape[0] // 2
    return jnp.concatenate([tail[:half], tail[half:]], axis=1)


def spread_tail(tile):
    low, other = low_lanes(tile.shape[0]), swapped(tile)
    return jnp.concatenate([jnp.where(low, tile, other), jnp.where(low, other, tile)], axis=0)


def same_group(size):
    rows = lax.broadcasted_iota(jnp.int32, (size, size), 0)
    columns = lax.broadcasted_iota(jnp.int32, (size, size), 1)
    return (((rows * 6554) >> 16) == ((columns * 6554) >> 16)).astype(F32).astype(BF16)


def thirds(value):
    parts = []
    for _ in range(3):
        part = value.astype(BF16).astype(F32)
        value = value - part
        parts.append(part)
    return parts


def group_sum(sums, members):
    wide = jnp.dot(jnp.concatenate(thirds(sums), axis=0).astype(BF16), members, preferred_element_type=F32)
    return (wide[0:8] + wide[8:16]) + wide[16:24]


def store_taps(taps, tiles):
    column = lax.broadcasted_iota(jnp.int32, (320, LANES), 0) & 31
    low = low_lanes(320)
    shifted = []
    for place, step in enumerate((-1, 0, 1)):
        moved = []
        for tile in tiles:
            if step:
                tile = pltpu.roll(tile, -step % 320, 0)
                tile = jnp.where(column == (0 if step < 0 else 31), 0.0, tile)
            moved.append(tile)
        taps[:, place * 256 : place * 256 + 128] = moved[0].astype(BF16)
        taps[:, place * 256 + 128 : place * 256 + 256] = moved[1].astype(BF16)
        shifted.append(moved[2])
    taps[:, 768:896] = jnp.where(low, shifted[0], shifted[1]).astype(BF16)
    taps[:, 896:1024] = jnp.where(low, shifted[2], 0.0).astype(BF16)


def conv_tail(taps, wt):
    wide = jnp.dot(taps[...], wt[...], preferred_element_type=F32)
    return (wide[0:256, 0:64] + wide[32:288, 64:128]) + wide[64:320, 128:192]


def conv_row(taps, wp, row):
    return jnp.dot(taps[row * 32 : row * 32 + POS, :], wp[row, :, 0:256], preferred_element_type=F32)


def hop_of(slot):
    return jnp.where(lax.axis_index("core") == 0, slot, (4 - slot) % 4)


def pack_kernel(noise_hbm, start_hbm, gain_hbm, bias_hbm, emb, o0, o1, o2, o3, start, gain, bias, noise, sems):
    x = lax.axis_index("x")
    outs = {0: o0, 1: o1, 2: o2, 3: o3}
    copies = {}
    for slot in (2, 1, 3, 0):
        at = pl.multiple_of(lax.rem(x + hop_of(slot), 4) * POS, POS)
        copies[slot] = pltpu.make_async_copy(noise_hbm.at[pl.ds(at, POS)], noise.at[slot], sems.at[slot])
        copies[slot].start()
    rest = [
        pltpu.make_async_copy(source, target, sems.at[4 + i])
        for i, (source, target) in enumerate(((start_hbm, start), (gain_hbm, gain), (bias_hbm, bias)))
    ]
    for copy in rest:
        copy.start()
    for slot, copy in copies.items():
        out = outs[slot]
        copy.wait()
        out[0:256] = noise[slot, :, 0:128]
        out[256:512] = noise[slot, :, 128:256]
        out[512:640] = pack_tail(noise[slot, :, 256:320].astype(F32)).astype(BF16)
        for tile in range(3):
            out[640 + 16 * tile : 656 + 16 * tile] = emb[:, tile * 128 : tile * 128 + 128]
    for copy in rest:
        copy.wait()


def norm_start_kernel(start, gain_ref, bias_ref, nq, sp):
    x = lax.axis_index("x")
    members = same_group(320)
    values = start[...].astype(F32)
    mean = group_sum(jnp.broadcast_to(jnp.sum(values, axis=0, keepdims=True), (8, 320)), members)[0:1] * (1.0 / 10240)
    centered = start[...].astype(F32) - mean
    spread = jnp.sum(centered * centered, axis=0, keepdims=True)
    var = group_sum(jnp.broadcast_to(spread, (8, 320)), members)[0:1] * (1.0 / 10240)
    scale = lax.rsqrt(var + 1e-05)
    gain, bias = gain_ref[...].reshape(1, 320), bias_ref[...].reshape(1, 320)
    first = pl.multiple_of(x * POS, POS)
    above = pl.multiple_of(jnp.maximum(x * POS - 32, 0), 32)
    below = pl.multiple_of(jnp.minimum(x * POS + POS, 992), 32)
    pieces = []
    for at, size, kept in ((above, 32, x > 0), (first, POS, None), (below, 32, x < 3)):
        block = start[pl.ds(at, size), :].astype(F32)
        normed = silu((block - mean) * scale * gain + bias)
        pieces.append(normed if kept is None else jnp.where(kept, normed, 0.0))
    normed = jnp.concatenate(pieces, axis=0)
    nq[0:320] = normed[:, 0:128].astype(BF16)
    nq[320:640] = normed[:, 128:256].astype(BF16)
    nq[640:800] = pack_tail(normed[:, 256:320]).astype(BF16)
    sp[0:256] = start[pl.ds(first, POS), 0:128]
    sp[256:512] = start[pl.ds(first, POS), 128:256]
    sp[512:640] = pack_tail(start[pl.ds(first, POS), 256:320].astype(F32)).astype(BF16)


def conv_frame(normed, wp, wt, pre, taps, before_row=None):
    store_taps(taps, [normed[0:320].astype(F32), normed[320:640].astype(F32), spread_tail(normed[640:800].astype(F32))])
    main = None
    for row in range(3):
        if before_row is not None:
            before_row(row)
        term = conv_row(taps, wp, row)
        main = term if main is None else main + term
    if before_row is not None:
        before_row(3)
    pre[:, 0:256] = 0.5 * main
    pre[:, 256:320] = 0.5 * conv_tail(taps, wt)


def first_own_kernel(sw, tw, tew_hbm, normed, pre, wp, wt, tp, tew, taps, sems):
    frame = lax.axis_index("z") * 2 + lax.axis_index("core")
    copies = []
    for row in range(4):
        out = tp if row == 3 else wp.at[row]
        for place in range(3):
            one = tw.at[place] if row == 3 else sw.at[row, place]
            for source, target in (
                (one.at[0:256], out.at[place * 256 : place * 256 + 256]),
                (one.at[256:320], out.at[768 + 64 * place : 832 + 64 * place]),
            ):
                copies.append(pltpu.make_async_copy(source, target, sems.at[len(copies)]))
    copies.append(pltpu.make_async_copy(tew_hbm, tew, sems.at[24]))
    for copy in copies:
        copy.start()
    for row in range(3):
        wp[row, 960:1024] = jnp.zeros((64, 320), BF16)
    tp[960:1024] = jnp.zeros((64, 320), BF16)

    def before_row(row):
        if row < 3:
            for copy in copies[6 * row : 6 * row + 6]:
                copy.wait()
        else:
            wt[...] = jnp.concatenate([wp[i, :, 256:320].astype(F32) for i in range(3)], axis=1).astype(BF16)

    conv_frame(normed, wp, wt, pre.at[0], taps, before_row)
    for copy in copies[18:]:
        copy.wait()
    for place, missing in ((0, frame == 0), (2, frame == 15)):

        @pl.when(missing)
        def _():
            tp[place * 256 : place * 256 + 256] = jnp.zeros((256, 320), BF16)
            tp[768 + 64 * place : 832 + 64 * place] = jnp.zeros((64, 320), BF16)


def first_sides_kernel(before, after, wp, wt, pre, taps):
    for place, normed in enumerate((before, after)):
        conv_frame(normed, wp, wt, pre.at[place], taps)


def silu_half(half):
    return half + half * jnp.tanh(half)


SPANS = ((0, 256), (256, 512), (512, 640))


def packed_update(a3, tp):
    update = jnp.dot(a3, tp[...], preferred_element_type=F32)
    return update[:, 0:128], update[:, 128:256], pack_tail(update[:, 256:320])


def store_frames(a3, parts):
    for place, part in enumerate(parts):
        a3[:, place * 256 : place * 256 + 256] = part[:, 0:256].astype(BF16)
    a3[:, 768:896] = jnp.concatenate([parts[0][:, 256:320], parts[1][:, 256:320]], axis=1).astype(BF16)
    last = parts[2][:, 256:320]
    a3[:, 896:1024] = jnp.concatenate([last, jnp.zeros_like(last)], axis=1).astype(BF16)


def first_total_kernel(here, sides, tp, tew, n0, n1, n2, n3, rt, noise, tb, a3, tails):
    x = lax.axis_index("x")
    arrived = (n0, n1, n2, n3)
    bias = None
    for at, rows in ((640, slice(0, 128)), (656, slice(128, 256)), (672, slice(256, 320))):
        emb = jnp.concatenate([one[at : at + 16, 0 : rows.stop - rows.start] for one in arrived], axis=0)
        term = jnp.dot(emb, tew[rows], preferred_element_type=F32)
        bias = term if bias is None else bias + term
    bias = bias / (1.0 + jnp.exp(-bias))
    for slot, one in enumerate(arrived):
        step = lax.rem(x + 4 - hop_of(slot), 4)
        noise[step] = one[0:640]
        tb[step] = bias[slot * 16 : slot * 16 + 16]
    halves = [0.5 * bias[slot * 16 : slot * 16 + 1] for slot in range(4)]

    def some_rows(block, carry):
        rows = pl.ds(pl.multiple_of(block * 32, 32), 32)
        for place, pre in enumerate((sides.at[0], here.at[0], sides.at[1])):
            half = pre[rows, :]
            ones = [silu_half(half + one) for one in halves]
            total = (ones[0] + ones[1]) + (ones[2] + ones[3])
            a3[rows, place * 256 : place * 256 + 256] = total[:, 0:256].astype(BF16)
            tails[place, rows, :] = total[:, 256:320]
        return carry

    lax.fori_loop(0, 8, some_rows, 0)
    a3[:, 768:896] = jnp.concatenate([tails[0], tails[1]], axis=1).astype(BF16)
    a3[:, 896:1024] = jnp.concatenate([tails[2], jnp.zeros((POS, 64), F32)], axis=1).astype(BF16)
    for update, (a, b) in zip(packed_update(a3[...], tp), SPANS):
        total = update
        for step in range(4):
            total = total + noise[step, a:b].astype(F32)
        rt[a:b] = (0.25 * total).astype(BF16)


def first_prefix_kernel(here, sides, tb, tp, noise, prefix, a3):
    prefix[0] = jnp.zeros((ROWS, LANES), F32)

    def one_step(step, carry):
        half = 0.5 * tb[step][0:1]
        store_frames(a3, [silu_half(pre[...] + half) for pre in (sides.at[0], here.at[0], sides.at[1])])
        for update, (a, b) in zip(packed_update(a3[...], tp), SPANS):
            prefix[step + 1, a:b] = prefix[step, a:b] + 0.25 * (update + noise[step, a:b].astype(F32))
        return carry

    lax.fori_loop(0, 3, one_step, 0)


def dup_third(parts):
    third = parts[:, 256:384]
    third = jnp.where(low_lanes(third.shape[0]), third, swapped(third))
    return jnp.concatenate([parts[:, 0:256], third], axis=1)


def offset_of(totals):
    y = lax.axis_index("y")
    kept = [jnp.where(y >= hop_of(slot), one[...].astype(F32), 0.0) for slot, one in enumerate(totals, 1)]
    return kept[0] + kept[1] + kept[2]


def position_sum(tiles):
    sums = [jnp.sum(tile, axis=0, keepdims=True) for tile in tiles]
    third = jnp.broadcast_to(sums[2], (8, LANES))
    return jnp.concatenate(sums[:2] + [(third + swapped(third))[0:1]], axis=1)


def states_kernel(sp, prefix, r1, r2, r3, states, up, down, far):
    members = same_group(384)
    base = sp[...].astype(F32) + offset_of((r1, r2, r3))
    spans = ((0, 256), (256, 512), (512, 640))
    sums = []
    for step in range(4):
        states[step] = (base + prefix[step]).astype(BF16)
        sums.append(position_sum([states[step, a:b].astype(F32) for a, b in spans]))
        for i, (first, last) in enumerate(((0, 224), (256, 480), (512, 608))):
            at = step * 96 + i * 32
            up[at : at + 32] = states[step, last : last + 32]
            down[at : at + 32] = states[step, first : first + 32]
    means = dup_third(group_sum(jnp.concatenate(sums + sums, axis=0), members) * (1.0 / 2560))
    spreads = []
    for step in range(4):
        mean = means[step : step + 1]
        centered = [states[step, a:b].astype(F32) - mean[:, 128 * i : 128 * i + 128] for i, (a, b) in enumerate(spans)]
        spreads.append(position_sum([c * c for c in centered]))
    spread = dup_third(group_sum(jnp.concatenate(spreads + spreads, axis=0), members))
    rest = jnp.concatenate([means[0:4], spread[0:4]], axis=0)
    for part in range(3):
        piece = rest.astype(BF16)
        rest = rest - piece.astype(F32)
        for tile in range(3):
            at = (part * 3 + tile) * 8
            value = piece[:, tile * 128 : tile * 128 + 128]
            far[at : at + 8] = value
            up[384 + at : 392 + at] = value
            down[384 + at : 392 + at] = value


def stats_of(ref, base):
    total = None
    for part in range(3):
        piece = jnp.concatenate(
            [ref[base + (part * 3 + t) * 8 : base + (part * 3 + t) * 8 + 8].astype(F32) for t in range(3)], axis=1
        )
        total = piece if total is None else total + piece
    return total[0:4], total[4:8]


def wide(vector):
    vector = vector[...].reshape(1, 320)
    return jnp.concatenate([vector, vector[:, 256:320]], axis=1)


def second_sweep_kernel(first, states, above, below, far, mine, gain_ref, bias_ref, wp, wt, tb, *refs):
    if first:
        earlier, out, total, taps, scales = refs
    else:
        out, taps, scales = refs
    gain, bias = wide(gain_ref), wide(bias_ref)
    x = lax.axis_index("x")
    parts = [stats_of(mine, 0), stats_of(above, 384), stats_of(below, 384), stats_of(far, 0)]
    mean = (parts[0][0] + parts[1][0] + parts[2][0] + parts[3][0]) * 0.25
    spread = parts[0][1] + parts[1][1] + parts[2][1] + parts[3][1]
    for one in parts:
        spread = spread + 2560.0 * (one[0] - mean) * (one[0] - mean)
    rstd = lax.rsqrt(spread * (1.0 / 10240) + 1e-05)
    for step in range(4):
        scales[step, 0:1] = mean[step : step + 1]
        scales[step, 1:2] = rstd[step : step + 1]

    def one_step(local_step, carry):
        step = local_step + first
        here = scales[step]

        def normed(value, tile):
            lanes = slice(tile * 128, tile * 128 + 128)
            value = (value.astype(F32) - here[0:1, lanes]) * here[1:2, lanes]
            return silu(value * gain[:, lanes] + bias[:, lanes])

        edge = pl.multiple_of(step * 96, 32)
        tiles = []
        low = low_lanes(32)
        for tile in range(3):
            top = normed(above[pl.ds(edge + 32 * tile, 32)], tile)
            bottom = normed(below[pl.ds(edge + 32 * tile, 32)], tile)
            if tile < 2:
                middle = normed(states[step, 256 * tile : 256 * tile + 256], tile)
            else:
                middle = spread_tail(normed(states[step, 512:640], 2))
                top = jnp.where(low, swapped(top), top)
                bottom = jnp.where(low, bottom, swapped(bottom))
            top = jnp.where(x > 0, top, 0.0)
            bottom = jnp.where(x < 3, bottom, 0.0)
            tiles.append(jnp.concatenate([top, middle, bottom], axis=0))
        store_taps(taps, tiles)
        bias_here = tb[step][0:1]
        main = (conv_row(taps, wp, 0) + conv_row(taps, wp, 1)) + conv_row(taps, wp, 2)
        activated = silu(main + bias_here[:, 0:256])
        tail = silu(conv_tail(taps, wt) + bias_here[:, 256:320])
        out[local_step, 0:256] = activated[:, 0:128].astype(BF16)
        out[local_step, 256:512] = activated[:, 128:256].astype(BF16)
        out[local_step, 512:640] = pack_tail(tail).astype(BF16)
        return carry

    lax.fori_loop(0, 2, one_step, 0)
    if first:
        ones = [half[step].astype(F32) for half in (earlier, out) for step in range(2)]
        total[...] = ((ones[0] + ones[1]) + (ones[2] + ones[3])).astype(BF16)


def store_packed_frames(a3, tiles):
    low = low_lanes(POS)
    tails = []
    for place, (first, second, tail) in enumerate(tiles):
        a3[:, place * 256 : place * 256 + 128] = first.astype(BF16)
        a3[:, place * 256 + 128 : place * 256 + 256] = second.astype(BF16)
        tails.append(spread_tail(tail))
    a3[:, 768:896] = jnp.where(low, tails[0], tails[1]).astype(BF16)
    a3[:, 896:1024] = jnp.where(low, tails[2], 0.0).astype(BF16)


def second_total_kernel(own, before, after, tp, noise, rt, a3):
    store_packed_frames(a3, [[one[a:b].astype(F32) for a, b in SPANS] for one in (before, own, after)])
    for update, (a, b) in zip(packed_update(a3[...], tp), SPANS):
        total = update
        for step in range(4):
            total = total + noise[step, a:b].astype(F32)
        rt[a:b] = (0.25 * total).astype(BF16)


def second_prefix_kernel(own0, own1, before0, before1, after0, after1, tp, noise, prefix, a3):
    for step in range(4):
        tiles = []
        for pair in ((before0, before1), (own0, own1), (after0, after1)):
            half = pair[step // 2]
            tiles.append([half[step % 2, a:b].astype(F32) for a, b in SPANS])
        store_packed_frames(a3, tiles)
        for update, (a, b) in zip(packed_update(a3[...], tp), SPANS):
            now = 0.25 * (update + noise[step, a:b].astype(F32))
            prefix[step, a:b] = now if step == 0 else prefix[step - 1, a:b] + now


def result_kernel(sp, prefix, r1, r2, r3, *outs):
    x = lax.axis_index("x")
    base = sp[...].astype(F32) + offset_of((r1, r2, r3))
    for slot, out in enumerate(outs):
        out[...] = (base + prefix[lax.rem(x + hop_of(slot), 4)]).astype(BF16)


def unpack_kernel(r0, r1, r2, r3, out):
    x = lax.axis_index("x")
    for slot, one in enumerate((r0, r1, r2, r3)):
        start = pl.multiple_of(lax.rem(x + 4 - hop_of(slot), 4) * POS, POS)
        out[pl.ds(start, POS), 0:128] = one[0:256]
        out[pl.ds(start, POS), 128:256] = one[256:512]
        tail = spread_tail(one[512:640].astype(F32))
        out[pl.ds(start, POS), 256:320] = tail[:, 0:64].astype(BF16)


def call(body, outs, *args, scratch=(), flops=0, limit=24, hbm=0, sems=0):
    shapes = [jax.ShapeDtypeStruct(shape, kind) for shape, kind in outs]
    vmem = pl.BlockSpec(memory_space=pltpu.VMEM)
    nbytes = sum(a.size * a.dtype.itemsize for a in args) + sum(s.size * s.dtype.itemsize for s in shapes)
    scratch_shapes = [pltpu.VMEM(shape, kind) for shape, kind in scratch]
    if sems:
        scratch_shapes.append(pltpu.SemaphoreType.DMA((sems,)))
    return pl.pallas_call(
        body,
        out_shape=shapes,
        in_specs=[pl.BlockSpec(memory_space=pltpu.HBM)] * hbm + [vmem] * (len(args) - hbm),
        out_specs=[vmem] * len(shapes),
        scratch_shapes=scratch_shapes,
        compiler_params=pltpu.CompilerParams(vmem_limit_bytes=limit << 20),
        cost_estimate=pl.CostEstimate(flops=flops, bytes_accessed=nbytes, transcendentals=0),
    )(*(pltpu.with_memory_space_constraint(a, pltpu.HBM) if i < hbm else a for i, a in enumerate(args)))


def moved(value, place):
    pairs = []
    for y in range(4):
        for x in range(4):
            for z in range(8):
                for core in range(2):
                    ty, tx, frame = place(y, x, z * 2 + core)
                    pairs.append(((y * 4 + x) * 16 + z * 2 + core, (ty * 4 + tx) * 16 + frame))
    return lax.ppermute(value, AXES, pairs)


def hop_on(slot, core):
    return slot if core == 0 else 4 - slot


def swap_x(values):
    out = [values[0]]
    for slot in (1, 2, 3):
        out.append(moved(values[slot], lambda y, x, frame: (y, (x + hop_on(slot, frame % 2)) % 4, frame)))
    return out


def gather_y(value):
    out = []
    for slot in (1, 2, 3):
        out.append(moved(value, lambda y, x, frame: ((y + hop_on(slot, frame % 2)) % 4, x, frame)))
    return out


def along_x(value, hop):
    return moved(value, lambda y, x, frame: (y, (x + hop) % 4, frame))


def along_frame(value, hop):
    return moved(value, lambda y, x, frame: (y, x, (frame + hop) % 16))


def embedding_of(step_index, half_dim):
    frequencies = jnp.exp(-math.log(10000.0) * jnp.arange(half_dim, dtype=F32) / half_dim)
    angles = step_index.astype(F32) * frequencies
    return jnp.concatenate([jnp.cos(angles), jnp.sin(angles)]).astype(BF16)


def local(start_state, step_noise, timesteps, gn_gain, gn_bias, spatial_weight, temporal_weight, temb_weight):
    start = start_state.reshape(1024, 320)
    noise = step_noise.reshape(1024, 320)
    emb = embedding_of(timesteps[0], temb_weight.shape[0] // 2)
    emb = jnp.broadcast_to(jnp.pad(emb, (0, 64))[None], (16, 384))
    packed = (ROWS, LANES)
    four = (4, ROWS, LANES)

    *outgoing, start, gain, bias = call(
        pack_kernel,
        [((688, 128), BF16)] * 4 + [((1024, 320), BF16), ((320,), F32), ((320,), F32)],
        noise, start, gn_gain, gn_bias, emb,
        scratch=(((4, 256, 320), BF16),),
        hbm=4,
        sems=7,
    )
    arrived = swap_x(outgoing)
    nq, sp = call(norm_start_kernel, [((800, 128), BF16), (packed, BF16)], start, gain, bias)
    before, after = along_frame(nq, 1), along_frame(nq, -1)
    taps = ((320, 1024), BF16)
    a3 = ((256, 1024), BF16)
    pre = (256, 320)
    here, wp, wt, tp, tew = call(
        first_own_kernel,
        [((1,) + pre, F32), ((3, 1024, 320), BF16), ((1024, 192), BF16), ((1024, 320), BF16), ((320, 320), BF16)],
        spatial_weight, temporal_weight, temb_weight, nq,
        scratch=(taps,),
        flops=512 * 320 * 2880,
        hbm=3,
        sems=25,
    )
    sides = call(
        first_sides_kernel, [((2,) + pre, F32)], before, after, wp, wt, scratch=(taps,), flops=1024 * 320 * 2880
    )[0]
    rt, noises, tb = call(
        first_total_kernel,
        [(packed, BF16), (four, BF16), ((4, 16, 320), F32)],
        here, sides, tp, tew, *arrived,
        scratch=(a3, ((3, 256, 64), F32)),
        flops=512 * 320 * 960,
    )
    totals = gather_y(rt)
    prefix = call(
        first_prefix_kernel, [(four, F32)], here, sides, tb, tp, noises, scratch=(a3,), flops=1536 * 320 * 960
    )[0]
    states, up, down, far = call(
        states_kernel,
        [(four, BF16), ((464, 128), BF16), ((464, 128), BF16), ((72, 128), BF16)],
        sp, prefix, *totals,
    )
    edges = along_x(up, 1), along_x(down, -1), along_x(far, 2), far
    halves, earlier, outs = [], (), [((2, ROWS, LANES), BF16)]
    for half in (0, 1):
        own, *total = call(
            functools.partial(second_sweep_kernel, 2 * half),
            outs + [(packed, BF16)] * half,
            states, *edges, gain, bias, wp, wt, tb, *earlier,
            scratch=(taps, ((4, 8, 384), F32)),
            flops=1024 * 320 * 2880,
        )
        halves.append((own, along_frame(own, 1), along_frame(own, -1)))
        earlier = (own,)
    parts = [half[i] for i in range(3) for half in halves]
    sums = total[0], along_frame(total[0], 1), along_frame(total[0], -1)
    rt = call(second_total_kernel, [(packed, BF16)], *sums, tp, noises, scratch=(a3,), flops=512 * 320 * 960)[0]
    totals = gather_y(rt)
    prefix = call(second_prefix_kernel, [(four, F32)], *parts, tp, noises, scratch=(a3,), flops=2048 * 320 * 960)[0]
    results = call(result_kernel, [(packed, BF16)] * 4, sp, prefix, *totals)
    out = call(unpack_kernel, [((1024, 320), BF16)], *swap_x(results))[0]
    return out.reshape(1, 1, 32, 32, 320)


def solution(mesh):
    split = Mesh(mesh.devices.reshape(4, 4, 8, 2), AXES)
    steps, frames = ("y", "x"), ("z", "core")
    placed = (
        P(frames, None, None, None),
        P(steps, frames, None, None, None),
        P(steps),
        P(),
        P(),
        P(),
        P(),
        P(),
    )
    return jax.shard_map(
        local,
        mesh=split,
        in_specs=placed,
        out_specs=P(steps, frames, None, None, None),
        check_vma=False,
    )
```

```python
import math

import jax
import jax.numpy as jnp
from jax import lax
from jax.experimental import pallas as pl
from jax.experimental.pallas import tpu as pltpu
from jax.sharding import Mesh, PartitionSpec as P


F32, BF16 = jnp.float32, jnp.bfloat16
AXES = ("y", "x", "z", "core")

POS, ROWS, LANES = 256, 640, 128


def silu(a):
    half = 0.5 * a
    return half + half * jnp.tanh(half)


def low_lanes(rows):
    return lax.broadcasted_iota(jnp.int32, (rows, LANES), 1) < 64


def swapped(tile):
    return pltpu.roll(tile, 64, 1)


def pack_tail(tail):
    half = tail.shape[0] // 2
    return jnp.concatenate([tail[:half], tail[half:]], axis=1)


def spread_tail(tile):
    low, other = low_lanes(tile.shape[0]), swapped(tile)
    return jnp.concatenate([jnp.where(low, tile, other), jnp.where(low, other, tile)], axis=0)


def same_group(size):
    rows = lax.broadcasted_iota(jnp.int32, (size, size), 0)
    columns = lax.broadcasted_iota(jnp.int32, (size, size), 1)
    return (((rows * 6554) >> 16) == ((columns * 6554) >> 16)).astype(F32).astype(BF16)


def thirds(value):
    parts = []
    for _ in range(3):
        part = value.astype(BF16).astype(F32)
        value = value - part
        parts.append(part)
    return parts


def group_sum(sums, members):
    wide = jnp.dot(jnp.concatenate(thirds(sums), axis=0).astype(BF16), members, preferred_element_type=F32)
    return (wide[0:8] + wide[8:16]) + wide[16:24]


def store_taps(taps, tiles):
    column = lax.broadcasted_iota(jnp.int32, (320, LANES), 0) & 31
    low = low_lanes(320)
    shifted = []
    for place, step in enumerate((-1, 0, 1)):
        moved = []
        for tile in tiles:
            if step:
                tile = pltpu.roll(tile, -step % 320, 0)
                tile = jnp.where(column == (0 if step < 0 else 31), 0.0, tile)
            moved.append(tile)
        taps[:, place * 256 : place * 256 + 128] = moved[0].astype(BF16)
        taps[:, place * 256 + 128 : place * 256 + 256] = moved[1].astype(BF16)
        shifted.append(moved[2])
    taps[:, 768:896] = jnp.where(low, shifted[0], shifted[1]).astype(BF16)
    taps[:, 896:1024] = jnp.where(low, shifted[2], 0.0).astype(BF16)


def conv_tail(taps, wt):
    wide = jnp.dot(taps[...], wt[...], preferred_element_type=F32)
    return (wide[0:256, 0:64] + wide[32:288, 64:128]) + wide[64:320, 128:192]


def conv_row(taps, wp, row):
    return jnp.dot(taps[row * 32 : row * 32 + POS, :], wp[row, :, 0:256], preferred_element_type=F32)


def hop_of(slot):
    return jnp.where(lax.axis_index("core") == 0, slot, (4 - slot) % 4)


def pack_kernel(noise_hbm, start_hbm, gain_hbm, bias_hbm, emb, o0, o1, o2, o3, start, gain, bias, noise, sems):
    x = lax.axis_index("x")
    outs = {0: o0, 1: o1, 2: o2, 3: o3}
    copies = {}
    for slot in (2, 1, 3, 0):
        at = pl.multiple_of(lax.rem(x + hop_of(slot), 4) * POS, POS)
        copies[slot] = pltpu.make_async_copy(noise_hbm.at[pl.ds(at, POS)], noise.at[slot], sems.at[slot])
        copies[slot].start()
    rest = [
        pltpu.make_async_copy(source, target, sems.at[4 + i])
        for i, (source, target) in enumerate(((start_hbm, start), (gain_hbm, gain), (bias_hbm, bias)))
    ]
    for copy in rest:
        copy.start()
    for slot, copy in copies.items():
        out = outs[slot]
        copy.wait()
        out[0:256] = noise[slot, :, 0:128]
        out[256:512] = noise[slot, :, 128:256]
        out[512:640] = pack_tail(noise[slot, :, 256:320].astype(F32)).astype(BF16)
        for tile in range(3):
            out[640 + 16 * tile : 656 + 16 * tile] = emb[:, tile * 128 : tile * 128 + 128]
    for copy in rest:
        copy.wait()


def norm_start_kernel(start, gain_ref, bias_ref, nq, sp):
    x = lax.axis_index("x")
    members = same_group(320)
    values = start[...].astype(F32)
    mean = group_sum(jnp.broadcast_to(jnp.sum(values, axis=0, keepdims=True), (8, 320)), members)[0:1] * (1.0 / 10240)
    centered = start[...].astype(F32) - mean
    spread = jnp.sum(centered * centered, axis=0, keepdims=True)
    var = group_sum(jnp.broadcast_to(spread, (8, 320)), members)[0:1] * (1.0 / 10240)
    scale = lax.rsqrt(var + 1e-05)
    gain, bias = gain_ref[...].reshape(1, 320), bias_ref[...].reshape(1, 320)
    first = pl.multiple_of(x * POS, POS)
    above = pl.multiple_of(jnp.maximum(x * POS - 32, 0), 32)
    below = pl.multiple_of(jnp.minimum(x * POS + POS, 992), 32)
    pieces = []
    for at, size, kept in ((above, 32, x > 0), (first, POS, None), (below, 32, x < 3)):
        block = start[pl.ds(at, size), :].astype(F32)
        normed = silu((block - mean) * scale * gain + bias)
        pieces.append(normed if kept is None else jnp.where(kept, normed, 0.0))
    normed = jnp.concatenate(pieces, axis=0)
    nq[0:320] = normed[:, 0:128].astype(BF16)
    nq[320:640] = normed[:, 128:256].astype(BF16)
    nq[640:800] = pack_tail(normed[:, 256:320]).astype(BF16)
    sp[0:256] = start[pl.ds(first, POS), 0:128]
    sp[256:512] = start[pl.ds(first, POS), 128:256]
    sp[512:640] = pack_tail(start[pl.ds(first, POS), 256:320].astype(F32)).astype(BF16)


def conv_frame(normed, wp, wt, pre, taps, before_row=None):
    store_taps(taps, [normed[0:320].astype(F32), normed[320:640].astype(F32), spread_tail(normed[640:800].astype(F32))])
    main = None
    for row in range(3):
        if before_row is not None:
            before_row(row)
        term = conv_row(taps, wp, row)
        main = term if main is None else main + term
    if before_row is not None:
        before_row(3)
    pre[:, 0:256] = 0.5 * main
    pre[:, 256:320] = 0.5 * conv_tail(taps, wt)


def first_own_kernel(sw, tw, tew_hbm, normed, pre, wp, wt, tp, tew, taps, sems):
    frame = lax.axis_index("z") * 2 + lax.axis_index("core")
    copies = []
    for row in range(4):
        out = tp if row == 3 else wp.at[row]
        for place in range(3):
            one = tw.at[place] if row == 3 else sw.at[row, place]
            for source, target in (
                (one.at[0:256], out.at[place * 256 : place * 256 + 256]),
                (one.at[256:320], out.at[768 + 64 * place : 832 + 64 * place]),
            ):
                copies.append(pltpu.make_async_copy(source, target, sems.at[len(copies)]))
    copies.append(pltpu.make_async_copy(tew_hbm, tew, sems.at[24]))
    for copy in copies:
        copy.start()
    for row in range(3):
        wp[row, 960:1024] = jnp.zeros((64, 320), BF16)
    tp[960:1024] = jnp.zeros((64, 320), BF16)

    def before_row(row):
        if row < 3:
            for copy in copies[6 * row : 6 * row + 6]:
                copy.wait()
        else:
            wt[...] = jnp.concatenate([wp[i, :, 256:320].astype(F32) for i in range(3)], axis=1).astype(BF16)

    conv_frame(normed, wp, wt, pre.at[0], taps, before_row)
    for copy in copies[18:]:
        copy.wait()
    for place, missing in ((0, frame == 0), (2, frame == 15)):

        @pl.when(missing)
        def _():
            tp[place * 256 : place * 256 + 256] = jnp.zeros((256, 320), BF16)
            tp[768 + 64 * place : 832 + 64 * place] = jnp.zeros((64, 320), BF16)


def first_sides_kernel(before, after, wp, wt, pre, taps):
    for place, normed in enumerate((before, after)):
        conv_frame(normed, wp, wt, pre.at[place], taps)


def silu_half(half):
    return half + half * jnp.tanh(half)


SPANS = ((0, 256), (256, 512), (512, 640))


def packed_update(a3, tp):
    update = jnp.dot(a3, tp[...], preferred_element_type=F32)
    return update[:, 0:128], update[:, 128:256], pack_tail(update[:, 256:320])


def store_frames(a3, parts):
    for place, part in enumerate(parts):
        a3[:, place * 256 : place * 256 + 256] = part[:, 0:256].astype(BF16)
    a3[:, 768:896] = jnp.concatenate([parts[0][:, 256:320], parts[1][:, 256:320]], axis=1).astype(BF16)
    last = parts[2][:, 256:320]
    a3[:, 896:1024] = jnp.concatenate([last, jnp.zeros_like(last)], axis=1).astype(BF16)


def first_total_kernel(here, sides, tp, tew, n0, n1, n2, n3, rt, noise, tb, a3, tails):
    x = lax.axis_index("x")
    arrived = (n0, n1, n2, n3)
    bias = None
    for at, rows in ((640, slice(0, 128)), (656, slice(128, 256)), (672, slice(256, 320))):
        emb = jnp.concatenate([one[at : at + 16, 0 : rows.stop - rows.start] for one in arrived], axis=0)
        term = jnp.dot(emb, tew[rows], preferred_element_type=F32)
        bias = term if bias is None else bias + term
    bias = bias / (1.0 + jnp.exp(-bias))
    for slot, one in enumerate(arrived):
        step = lax.rem(x + 4 - hop_of(slot), 4)
        noise[step] = one[0:640]
        tb[step] = bias[slot * 16 : slot * 16 + 16]
    halves = [0.5 * bias[slot * 16 : slot * 16 + 1] for slot in range(4)]

    def some_rows(block, carry):
        rows = pl.ds(pl.multiple_of(block * 32, 32), 32)
        for place, pre in enumerate((sides.at[0], here.at[0], sides.at[1])):
            half = pre[rows, :]
            ones = [silu_half(half + one) for one in halves]
            total = (ones[0] + ones[1]) + (ones[2] + ones[3])
            a3[rows, place * 256 : place * 256 + 256] = total[:, 0:256].astype(BF16)
            tails[place, rows, :] = total[:, 256:320]
        return carry

    lax.fori_loop(0, 8, some_rows, 0)
    a3[:, 768:896] = jnp.concatenate([tails[0], tails[1]], axis=1).astype(BF16)
    a3[:, 896:1024] = jnp.concatenate([tails[2], jnp.zeros((POS, 64), F32)], axis=1).astype(BF16)
    for update, (a, b) in zip(packed_update(a3[...], tp), SPANS):
        total = update
        for step in range(4):
            total = total + noise[step, a:b].astype(F32)
        rt[a:b] = (0.25 * total).astype(BF16)


def first_prefix_kernel(here, sides, tb, tp, noise, prefix, a3):
    prefix[0] = jnp.zeros((ROWS, LANES), F32)

    def one_step(step, carry):
        half = 0.5 * tb[step][0:1]
        store_frames(a3, [silu_half(pre[...] + half) for pre in (sides.at[0], here.at[0], sides.at[1])])
        for update, (a, b) in zip(packed_update(a3[...], tp), SPANS):
            prefix[step + 1, a:b] = prefix[step, a:b] + 0.25 * (update + noise[step, a:b].astype(F32))
        return carry

    lax.fori_loop(0, 3, one_step, 0)


def dup_third(parts):
    third = parts[:, 256:384]
    third = jnp.where(low_lanes(third.shape[0]), third, swapped(third))
    return jnp.concatenate([parts[:, 0:256], third], axis=1)


def offset_of(totals):
    y = lax.axis_index("y")
    kept = [jnp.where(y >= hop_of(slot), one[...].astype(F32), 0.0) for slot, one in enumerate(totals, 1)]
    return kept[0] + kept[1] + kept[2]


def position_sum(tiles):
    sums = [jnp.sum(tile, axis=0, keepdims=True) for tile in tiles]
    third = jnp.broadcast_to(sums[2], (8, LANES))
    return jnp.concatenate(sums[:2] + [(third + swapped(third))[0:1]], axis=1)


def states_kernel(sp, prefix, r1, r2, r3, states, up, down, far):
    members = same_group(384)
    base = sp[...].astype(F32) + offset_of((r1, r2, r3))
    spans = ((0, 256), (256, 512), (512, 640))
    sums = []
    for step in range(4):
        states[step] = (base + prefix[step]).astype(BF16)
        sums.append(position_sum([states[step, a:b].astype(F32) for a, b in spans]))
        for i, (first, last) in enumerate(((0, 224), (256, 480), (512, 608))):
            at = step * 96 + i * 32
            up[at : at + 32] = states[step, last : last + 32]
            down[at : at + 32] = states[step, first : first + 32]
    means = dup_third(group_sum(jnp.concatenate(sums + sums, axis=0), members) * (1.0 / 2560))
    spreads = []
    for step in range(4):
        mean = means[step : step + 1]
        centered = [states[step, a:b].astype(F32) - mean[:, 128 * i : 128 * i + 128] for i, (a, b) in enumerate(spans)]
        spreads.append(position_sum([c * c for c in centered]))
    spread = dup_third(group_sum(jnp.concatenate(spreads + spreads, axis=0), members))
    rest = jnp.concatenate([means[0:4], spread[0:4]], axis=0)
    for part in range(3):
        piece = rest.astype(BF16)
        rest = rest - piece.astype(F32)
        for tile in range(3):
            at = (part * 3 + tile) * 8
            value = piece[:, tile * 128 : tile * 128 + 128]
            far[at : at + 8] = value
            up[384 + at : 392 + at] = value
            down[384 + at : 392 + at] = value


def stats_of(ref, base):
    total = None
    for part in range(3):
        piece = jnp.concatenate(
            [ref[base + (part * 3 + t) * 8 : base + (part * 3 + t) * 8 + 8].astype(F32) for t in range(3)], axis=1
        )
        total = piece if total is None else total + piece
    return total[0:4], total[4:8]


def wide(vector):
    vector = vector[...].reshape(1, 320)
    return jnp.concatenate([vector, vector[:, 256:320]], axis=1)


def second_sweep_kernel(states, above, below, far, mine, gain_ref, bias_ref, wp, wt, tb, out, total, taps, scales):
    gain, bias = wide(gain_ref), wide(bias_ref)
    x = lax.axis_index("x")
    parts = [stats_of(mine, 0), stats_of(above, 384), stats_of(below, 384), stats_of(far, 0)]
    mean = (parts[0][0] + parts[1][0] + parts[2][0] + parts[3][0]) * 0.25
    spread = parts[0][1] + parts[1][1] + parts[2][1] + parts[3][1]
    for one in parts:
        spread = spread + 2560.0 * (one[0] - mean) * (one[0] - mean)
    rstd = lax.rsqrt(spread * (1.0 / 10240) + 1e-05)
    for step in range(4):
        scales[step, 0:1] = mean[step : step + 1]
        scales[step, 1:2] = rstd[step : step + 1]

    def one_step(step, carry):
        here = scales[step]

        def normed(value, tile):
            lanes = slice(tile * 128, tile * 128 + 128)
            value = (value.astype(F32) - here[0:1, lanes]) * here[1:2, lanes]
            return silu(value * gain[:, lanes] + bias[:, lanes])

        edge = pl.multiple_of(step * 96, 32)
        tiles = []
        low = low_lanes(32)
        for tile in range(3):
            top = normed(above[pl.ds(edge + 32 * tile, 32)], tile)
            bottom = normed(below[pl.ds(edge + 32 * tile, 32)], tile)
            if tile < 2:
                middle = normed(states[step, 256 * tile : 256 * tile + 256], tile)
            else:
                middle = spread_tail(normed(states[step, 512:640], 2))
                top = jnp.where(low, swapped(top), top)
                bottom = jnp.where(low, bottom, swapped(bottom))
            top = jnp.where(x > 0, top, 0.0)
            bottom = jnp.where(x < 3, bottom, 0.0)
            tiles.append(jnp.concatenate([top, middle, bottom], axis=0))
        store_taps(taps, tiles)
        bias_here = tb[step][0:1]
        main = (conv_row(taps, wp, 0) + conv_row(taps, wp, 1)) + conv_row(taps, wp, 2)
        activated = silu(main + bias_here[:, 0:256])
        tail = silu(conv_tail(taps, wt) + bias_here[:, 256:320])
        out[step, 0:256] = activated[:, 0:128].astype(BF16)
        out[step, 256:512] = activated[:, 128:256].astype(BF16)
        out[step, 512:640] = pack_tail(tail).astype(BF16)
        return carry

    lax.fori_loop(0, 4, one_step, 0)
    ones = [out[step].astype(F32) for step in range(4)]
    total[...] = ((ones[0] + ones[1]) + (ones[2] + ones[3])).astype(BF16)


def store_packed_frames(a3, tiles):
    low = low_lanes(POS)
    tails = []
    for place, (first, second, tail) in enumerate(tiles):
        a3[:, place * 256 : place * 256 + 128] = first.astype(BF16)
        a3[:, place * 256 + 128 : place * 256 + 256] = second.astype(BF16)
        tails.append(spread_tail(tail))
    a3[:, 768:896] = jnp.where(low, tails[0], tails[1]).astype(BF16)
    a3[:, 896:1024] = jnp.where(low, tails[2], 0.0).astype(BF16)


def second_total_kernel(own, before, after, tp, noise, rt, a3):
    store_packed_frames(a3, [[one[a:b].astype(F32) for a, b in SPANS] for one in (before, own, after)])
    for update, (a, b) in zip(packed_update(a3[...], tp), SPANS):
        total = update
        for step in range(4):
            total = total + noise[step, a:b].astype(F32)
        rt[a:b] = (0.25 * total).astype(BF16)


def second_prefix_kernel(own, before, after, tp, noise, prefix, a3):
    for step in range(4):
        store_packed_frames(a3, [[one[step, a:b].astype(F32) for a, b in SPANS] for one in (before, own, after)])
        for update, (a, b) in zip(packed_update(a3[...], tp), SPANS):
            now = 0.25 * (update + noise[step, a:b].astype(F32))
            prefix[step, a:b] = now if step == 0 else prefix[step - 1, a:b] + now


def result_kernel(sp, prefix, r1, r2, r3, *outs):
    x = lax.axis_index("x")
    base = sp[...].astype(F32) + offset_of((r1, r2, r3))
    for slot, out in enumerate(outs):
        out[...] = (base + prefix[lax.rem(x + hop_of(slot), 4)]).astype(BF16)


def unpack_kernel(r0, r1, r2, r3, out):
    x = lax.axis_index("x")
    for slot, one in enumerate((r0, r1, r2, r3)):
        start = pl.multiple_of(lax.rem(x + 4 - hop_of(slot), 4) * POS, POS)
        out[pl.ds(start, POS), 0:128] = one[0:256]
        out[pl.ds(start, POS), 128:256] = one[256:512]
        tail = spread_tail(one[512:640].astype(F32))
        out[pl.ds(start, POS), 256:320] = tail[:, 0:64].astype(BF16)


def call(body, outs, *args, scratch=(), flops=0, limit=24, hbm=0, sems=0):
    shapes = [jax.ShapeDtypeStruct(shape, kind) for shape, kind in outs]
    vmem = pl.BlockSpec(memory_space=pltpu.VMEM)
    nbytes = sum(a.size * a.dtype.itemsize for a in args) + sum(s.size * s.dtype.itemsize for s in shapes)
    scratch_shapes = [pltpu.VMEM(shape, kind) for shape, kind in scratch]
    if sems:
        scratch_shapes.append(pltpu.SemaphoreType.DMA((sems,)))
    return pl.pallas_call(
        body,
        out_shape=shapes,
        in_specs=[pl.BlockSpec(memory_space=pltpu.HBM)] * hbm + [vmem] * (len(args) - hbm),
        out_specs=[vmem] * len(shapes),
        scratch_shapes=scratch_shapes,
        compiler_params=pltpu.CompilerParams(vmem_limit_bytes=limit << 20),
        cost_estimate=pl.CostEstimate(flops=flops, bytes_accessed=nbytes, transcendentals=0),
    )(*(pltpu.with_memory_space_constraint(a, pltpu.HBM) if i < hbm else a for i, a in enumerate(args)))


def moved(value, place):
    pairs = []
    for y in range(4):
        for x in range(4):
            for z in range(8):
                for core in range(2):
                    ty, tx, frame = place(y, x, z * 2 + core)
                    pairs.append(((y * 4 + x) * 16 + z * 2 + core, (ty * 4 + tx) * 16 + frame))
    return lax.ppermute(value, AXES, pairs)


def hop_on(slot, core):
    return slot if core == 0 else 4 - slot


def swap_x(values):
    out = [values[0]]
    for slot in (1, 2, 3):
        out.append(moved(values[slot], lambda y, x, frame: (y, (x + hop_on(slot, frame % 2)) % 4, frame)))
    return out


def gather_y(value):
    out = []
    for slot in (1, 2, 3):
        out.append(moved(value, lambda y, x, frame: ((y + hop_on(slot, frame % 2)) % 4, x, frame)))
    return out


def along_x(value, hop):
    return moved(value, lambda y, x, frame: (y, (x + hop) % 4, frame))


def along_frame(value, hop):
    return moved(value, lambda y, x, frame: (y, x, (frame + hop) % 16))


def embedding_of(step_index, half_dim):
    frequencies = jnp.exp(-math.log(10000.0) * jnp.arange(half_dim, dtype=F32) / half_dim)
    angles = step_index.astype(F32) * frequencies
    return jnp.concatenate([jnp.cos(angles), jnp.sin(angles)]).astype(BF16)


def local(start_state, step_noise, timesteps, gn_gain, gn_bias, spatial_weight, temporal_weight, temb_weight):
    start = start_state.reshape(1024, 320)
    noise = step_noise.reshape(1024, 320)
    emb = embedding_of(timesteps[0], temb_weight.shape[0] // 2)
    emb = jnp.broadcast_to(jnp.pad(emb, (0, 64))[None], (16, 384))
    packed = (ROWS, LANES)
    four = (4, ROWS, LANES)

    *outgoing, start, gain, bias = call(
        pack_kernel,
        [((688, 128), BF16)] * 4 + [((1024, 320), BF16), ((320,), F32), ((320,), F32)],
        noise, start, gn_gain, gn_bias, emb,
        scratch=(((4, 256, 320), BF16),),
        hbm=4,
        sems=7,
    )
    arrived = swap_x(outgoing)
    nq, sp = call(norm_start_kernel, [((800, 128), BF16), (packed, BF16)], start, gain, bias)
    before, after = along_frame(nq, 1), along_frame(nq, -1)
    taps = ((320, 1024), BF16)
    a3 = ((256, 1024), BF16)
    pre = (256, 320)
    here, wp, wt, tp, tew = call(
        first_own_kernel,
        [((1,) + pre, F32), ((3, 1024, 320), BF16), ((1024, 192), BF16), ((1024, 320), BF16), ((320, 320), BF16)],
        spatial_weight, temporal_weight, temb_weight, nq,
        scratch=(taps,),
        flops=512 * 320 * 2880,
        hbm=3,
        sems=25,
    )
    sides = call(
        first_sides_kernel, [((2,) + pre, F32)], before, after, wp, wt, scratch=(taps,), flops=1024 * 320 * 2880
    )[0]
    rt, noises, tb = call(
        first_total_kernel,
        [(packed, BF16), (four, BF16), ((4, 16, 320), F32)],
        here, sides, tp, tew, *arrived,
        scratch=(a3, ((3, 256, 64), F32)),
        flops=512 * 320 * 960,
    )
    totals = gather_y(rt)
    prefix = call(
        first_prefix_kernel, [(four, F32)], here, sides, tb, tp, noises, scratch=(a3,), flops=1536 * 320 * 960
    )[0]
    states, up, down, far = call(
        states_kernel,
        [(four, BF16), ((464, 128), BF16), ((464, 128), BF16), ((72, 128), BF16)],
        sp, prefix, *totals,
    )
    edges = along_x(up, 1), along_x(down, -1), along_x(far, 2), far
    own, total = call(
        second_sweep_kernel,
        [(four, BF16), (packed, BF16)],
        states, *edges, gain, bias, wp, wt, tb,
        scratch=(taps, ((4, 8, 384), F32)),
        flops=2048 * 320 * 2880,
    )
    sums = total, along_frame(total, 1), along_frame(total, -1)
    parts = own, along_frame(own, 1), along_frame(own, -1)
    rt = call(second_total_kernel, [(packed, BF16)], *sums, tp, noises, scratch=(a3,), flops=512 * 320 * 960)[0]
    totals = gather_y(rt)
    prefix = call(second_prefix_kernel, [(four, F32)], *parts, tp, noises, scratch=(a3,), flops=2048 * 320 * 960)[0]
    results = call(result_kernel, [(packed, BF16)] * 4, sp, prefix, *totals)
    out = call(unpack_kernel, [((1024, 320), BF16)], *swap_x(results))[0]
    return out.reshape(1, 1, 32, 32, 320)


def solution(mesh):
    split = Mesh(mesh.devices.reshape(4, 4, 8, 2), AXES)
    steps, frames = ("y", "x"), ("z", "core")
    placed = (
        P(frames, None, None, None),
        P(steps, frames, None, None, None),
        P(steps),
        P(),
        P(),
        P(),
        P(),
        P(),
    )
    return jax.shard_map(
        local,
        mesh=split,
        in_specs=placed,
        out_specs=P(steps, frames, None, None, None),
        check_vma=False,
    )
```

```python
import math

import jax
import jax.numpy as jnp
from jax import lax
from jax.experimental import pallas as pl
from jax.experimental.pallas import tpu as pltpu
from jax.sharding import Mesh, PartitionSpec as P


F32, BF16 = jnp.float32, jnp.bfloat16
AXES = ("y", "x", "z", "core")

POS, ROWS, LANES = 256, 640, 128


def silu(a):
    half = 0.5 * a
    return half + half * jnp.tanh(half)


def low_lanes(rows):
    return lax.broadcasted_iota(jnp.int32, (rows, LANES), 1) < 64


def swapped(tile):
    return pltpu.roll(tile, 64, 1)


def pack_tail(tail):
    half = tail.shape[0] // 2
    return jnp.concatenate([tail[:half], tail[half:]], axis=1)


def spread_tail(tile):
    low, other = low_lanes(tile.shape[0]), swapped(tile)
    return jnp.concatenate([jnp.where(low, tile, other), jnp.where(low, other, tile)], axis=0)


def same_group(size):
    rows = lax.broadcasted_iota(jnp.int32, (size, size), 0)
    columns = lax.broadcasted_iota(jnp.int32, (size, size), 1)
    return (((rows * 6554) >> 16) == ((columns * 6554) >> 16)).astype(F32).astype(BF16)


def thirds(value):
    parts = []
    for _ in range(3):
        part = value.astype(BF16).astype(F32)
        value = value - part
        parts.append(part)
    return parts


def group_sum(sums, members):
    wide = jnp.dot(jnp.concatenate(thirds(sums), axis=0).astype(BF16), members, preferred_element_type=F32)
    return (wide[0:8] + wide[8:16]) + wide[16:24]


def store_taps(taps, tiles):
    column = lax.broadcasted_iota(jnp.int32, (320, LANES), 0) & 31
    low = low_lanes(320)
    shifted = []
    for place, step in enumerate((-1, 0, 1)):
        moved = []
        for tile in tiles:
            if step:
                tile = pltpu.roll(tile, -step % 320, 0)
                tile = jnp.where(column == (0 if step < 0 else 31), 0.0, tile)
            moved.append(tile)
        taps[:, place * 256 : place * 256 + 128] = moved[0].astype(BF16)
        taps[:, place * 256 + 128 : place * 256 + 256] = moved[1].astype(BF16)
        shifted.append(moved[2])
    taps[:, 768:896] = jnp.where(low, shifted[0], shifted[1]).astype(BF16)
    taps[:, 896:1024] = jnp.where(low, shifted[2], 0.0).astype(BF16)


def conv_tail(taps, wt):
    wide = jnp.dot(taps[...], wt[...], preferred_element_type=F32)
    return (wide[0:256, 0:64] + wide[32:288, 64:128]) + wide[64:320, 128:192]


def conv_row(taps, wp, row):
    return jnp.dot(taps[row * 32 : row * 32 + POS, :], wp[row, :, 0:256], preferred_element_type=F32)


def hop_of(slot):
    return jnp.where(lax.axis_index("core") == 0, slot, (4 - slot) % 4)


def pack_kernel(noise_hbm, start_hbm, gain_hbm, bias_hbm, emb, o0, o1, o2, o3, start, gain, bias, noise, sems):
    x = lax.axis_index("x")
    outs = {0: o0, 1: o1, 2: o2, 3: o3}
    copies = {}
    for slot in (2, 1, 3, 0):
        at = pl.multiple_of((x ^ hop_of(slot)) * POS, POS)
        copies[slot] = pltpu.make_async_copy(noise_hbm.at[pl.ds(at, POS)], noise.at[slot], sems.at[slot])
        copies[slot].start()
    rest = [
        pltpu.make_async_copy(source, target, sems.at[4 + i])
        for i, (source, target) in enumerate(((start_hbm, start), (gain_hbm, gain), (bias_hbm, bias)))
    ]
    for copy in rest:
        copy.start()
    for slot, copy in copies.items():
        out = outs[slot]
        copy.wait()
        out[0:256] = noise[slot, :, 0:128]
        out[256:512] = noise[slot, :, 128:256]
        out[512:640] = pack_tail(noise[slot, :, 256:320].astype(F32)).astype(BF16)
        for tile in range(3):
            out[640 + 16 * tile : 656 + 16 * tile] = emb[:, tile * 128 : tile * 128 + 128]
    for copy in rest:
        copy.wait()


def norm_start_kernel(start, gain_ref, bias_ref, nq, sp):
    x = lax.axis_index("x")
    members = same_group(320)
    values = start[...].astype(F32)
    mean = group_sum(jnp.broadcast_to(jnp.sum(values, axis=0, keepdims=True), (8, 320)), members)[0:1] * (1.0 / 10240)
    centered = start[...].astype(F32) - mean
    spread = jnp.sum(centered * centered, axis=0, keepdims=True)
    var = group_sum(jnp.broadcast_to(spread, (8, 320)), members)[0:1] * (1.0 / 10240)
    scale = lax.rsqrt(var + 1e-05)
    gain, bias = gain_ref[...].reshape(1, 320), bias_ref[...].reshape(1, 320)
    first = pl.multiple_of(x * POS, POS)
    above = pl.multiple_of(jnp.maximum(x * POS - 32, 0), 32)
    below = pl.multiple_of(jnp.minimum(x * POS + POS, 992), 32)
    pieces = []
    for at, size, kept in ((above, 32, x > 0), (first, POS, None), (below, 32, x < 3)):
        block = start[pl.ds(at, size), :].astype(F32)
        normed = silu((block - mean) * scale * gain + bias)
        pieces.append(normed if kept is None else jnp.where(kept, normed, 0.0))
    normed = jnp.concatenate(pieces, axis=0)
    nq[0:320] = normed[:, 0:128].astype(BF16)
    nq[320:640] = normed[:, 128:256].astype(BF16)
    nq[640:800] = pack_tail(normed[:, 256:320]).astype(BF16)
    sp[0:256] = start[pl.ds(first, POS), 0:128]
    sp[256:512] = start[pl.ds(first, POS), 128:256]
    sp[512:640] = pack_tail(start[pl.ds(first, POS), 256:320].astype(F32)).astype(BF16)


def conv_frame(normed, wp, wt, pre, taps, before_row=None):
    store_taps(taps, [normed[0:320].astype(F32), normed[320:640].astype(F32), spread_tail(normed[640:800].astype(F32))])
    main = None
    for row in range(3):
        if before_row is not None:
            before_row(row)
        term = conv_row(taps, wp, row)
        main = term if main is None else main + term
    if before_row is not None:
        before_row(3)
    pre[:, 0:256] = 0.5 * main
    pre[:, 256:320] = 0.5 * conv_tail(taps, wt)


def first_own_kernel(sw, tw, tew_hbm, normed, pre, wp, wt, tp, tew, taps, sems):
    core = lax.axis_index("core")
    frame = lax.axis_index("z") * 2 + core
    copies = []
    for row in range(4):
        out = tp if row == 3 else wp.at[row]
        for place in range(3):
            one = tw.at[place + core * (2 - 2 * place)] if row == 3 else sw.at[row, place]
            for source, target in (
                (one.at[0:256], out.at[place * 256 : place * 256 + 256]),
                (one.at[256:320], out.at[768 + 64 * place : 832 + 64 * place]),
            ):
                copies.append(pltpu.make_async_copy(source, target, sems.at[len(copies)]))
    copies.append(pltpu.make_async_copy(tew_hbm, tew, sems.at[24]))
    for copy in copies:
        copy.start()
    for row in range(3):
        wp[row, 960:1024] = jnp.zeros((64, 320), BF16)
    tp[960:1024] = jnp.zeros((64, 320), BF16)

    def before_row(row):
        if row < 3:
            for copy in copies[6 * row : 6 * row + 6]:
                copy.wait()
        else:
            wt[...] = jnp.concatenate([wp[i, :, 256:320].astype(F32) for i in range(3)], axis=1).astype(BF16)

    conv_frame(normed, wp, wt, pre.at[0], taps, before_row)
    for copy in copies[18:]:
        copy.wait()

    @pl.when((frame == 0) | (frame == 15))
    def _():
        tp[0:256] = jnp.zeros((256, 320), BF16)
        tp[768:832] = jnp.zeros((64, 320), BF16)


def first_sides_kernel(before, after, wp, wt, pre, taps):
    for place, normed in enumerate((before, after)):
        conv_frame(normed, wp, wt, pre.at[place], taps)


def silu_half(half):
    return half + half * jnp.tanh(half)


SPANS = ((0, 256), (256, 512), (512, 640))


def packed_update(a3, tp):
    update = jnp.dot(a3, tp[...], preferred_element_type=F32)
    return update[:, 0:128], update[:, 128:256], pack_tail(update[:, 256:320])


def store_frames(a3, parts):
    for place, part in enumerate(parts):
        a3[:, place * 256 : place * 256 + 256] = part[:, 0:256].astype(BF16)
    a3[:, 768:896] = jnp.concatenate([parts[0][:, 256:320], parts[1][:, 256:320]], axis=1).astype(BF16)
    last = parts[2][:, 256:320]
    a3[:, 896:1024] = jnp.concatenate([last, jnp.zeros_like(last)], axis=1).astype(BF16)


def first_total_kernel(here, sides, tp, tew, n0, n1, n2, n3, rt, noise, tb, a3, tails):
    x = lax.axis_index("x")
    arrived = (n0, n1, n2, n3)
    bias = None
    for at, rows in ((640, slice(0, 128)), (656, slice(128, 256)), (672, slice(256, 320))):
        emb = jnp.concatenate([one[at : at + 16, 0 : rows.stop - rows.start] for one in arrived], axis=0)
        term = jnp.dot(emb, tew[rows], preferred_element_type=F32)
        bias = term if bias is None else bias + term
    bias = bias / (1.0 + jnp.exp(-bias))
    for slot, one in enumerate(arrived):
        step = x ^ hop_of(slot)
        noise[step] = one[0:640]
        tb[step] = bias[slot * 16 : slot * 16 + 16]
    halves = [0.5 * bias[slot * 16 : slot * 16 + 1] for slot in range(4)]

    def some_rows(block, carry):
        rows = pl.ds(pl.multiple_of(block * 32, 32), 32)
        for place, pre in enumerate((sides.at[0], here.at[0], sides.at[1])):
            half = pre[rows, :]
            ones = [silu_half(half + one) for one in halves]
            total = (ones[0] + ones[1]) + (ones[2] + ones[3])
            a3[rows, place * 256 : place * 256 + 256] = total[:, 0:256].astype(BF16)
            tails[place, rows, :] = total[:, 256:320]
        return carry

    lax.fori_loop(0, 8, some_rows, 0)
    a3[:, 768:896] = jnp.concatenate([tails[0], tails[1]], axis=1).astype(BF16)
    a3[:, 896:1024] = jnp.concatenate([tails[2], jnp.zeros((POS, 64), F32)], axis=1).astype(BF16)
    for update, (a, b) in zip(packed_update(a3[...], tp), SPANS):
        total = update
        for step in range(4):
            total = total + noise[step, a:b].astype(F32)
        rt[a:b] = (0.25 * total).astype(BF16)


def first_prefix_kernel(here, sides, tb, tp, noise, prefix, a3):
    prefix[0] = jnp.zeros((ROWS, LANES), F32)

    def one_step(step, carry):
        half = 0.5 * tb[step][0:1]
        store_frames(a3, [silu_half(pre[...] + half) for pre in (sides.at[0], here.at[0], sides.at[1])])
        for update, (a, b) in zip(packed_update(a3[...], tp), SPANS):
            prefix[step + 1, a:b] = prefix[step, a:b] + 0.25 * (update + noise[step, a:b].astype(F32))
        return carry

    lax.fori_loop(0, 3, one_step, 0)


def dup_third(parts):
    third = parts[:, 256:384]
    third = jnp.where(low_lanes(third.shape[0]), third, swapped(third))
    return jnp.concatenate([parts[:, 0:256], third], axis=1)


def slot_1_is_ahead():
    return ((lax.axis_index("x") + lax.axis_index("core")) & 1) == 0


def offset_of(totals):
    y = lax.axis_index("y")
    kept = [jnp.where((y ^ hop_of(slot)) < y, one[...].astype(F32), 0.0) for slot, one in enumerate(totals, 1)]
    return kept[0] + kept[1] + kept[2]


def position_sum(tiles):
    sums = [jnp.sum(tile, axis=0, keepdims=True) for tile in tiles]
    third = jnp.broadcast_to(sums[2], (8, LANES))
    return jnp.concatenate(sums[:2] + [(third + swapped(third))[0:1]], axis=1)


def states_kernel(sp, prefix, r1, r2, r3, states, halo1, halo3, far):
    ahead = slot_1_is_ahead()
    members = same_group(384)
    base = sp[...].astype(F32) + offset_of((r1, r2, r3))
    spans = ((0, 256), (256, 512), (512, 640))
    sums = []
    for step in range(4):
        states[step] = (base + prefix[step]).astype(BF16)
        sums.append(position_sum([states[step, a:b].astype(F32) for a, b in spans]))
        for i, (first, last) in enumerate(((0, 224), (256, 480), (512, 608))):
            at = step * 96 + i * 32
            for halo, row in ((halo1, jnp.where(ahead, last, first)), (halo3, jnp.where(ahead, first, last))):
                halo[at : at + 32] = states[step, pl.ds(pl.multiple_of(row, 32), 32)]
    means = dup_third(group_sum(jnp.concatenate(sums + sums, axis=0), members) * (1.0 / 2560))
    spreads = []
    for step in range(4):
        mean = means[step : step + 1]
        centered = [states[step, a:b].astype(F32) - mean[:, 128 * i : 128 * i + 128] for i, (a, b) in enumerate(spans)]
        spreads.append(position_sum([c * c for c in centered]))
    spread = dup_third(group_sum(jnp.concatenate(spreads + spreads, axis=0), members))
    rest = jnp.concatenate([means[0:4], spread[0:4]], axis=0)
    for part in range(3):
        piece = rest.astype(BF16)
        rest = rest - piece.astype(F32)
        for tile in range(3):
            at = (part * 3 + tile) * 8
            value = piece[:, tile * 128 : tile * 128 + 128]
            far[at : at + 8] = value
            halo1[384 + at : 392 + at] = value
            halo3[384 + at : 392 + at] = value


def stats_of(ref, base):
    total = None
    for part in range(3):
        piece = jnp.concatenate(
            [ref[base + (part * 3 + t) * 8 : base + (part * 3 + t) * 8 + 8].astype(F32) for t in range(3)], axis=1
        )
        total = piece if total is None else total + piece
    return total[0:4], total[4:8]


def wide(vector):
    vector = vector[...].reshape(1, 320)
    return jnp.concatenate([vector, vector[:, 256:320]], axis=1)


def second_sweep_kernel(states, halo1, halo3, far, mine, gain_ref, bias_ref, wp, wt, tb, out, total, taps, scales):
    gain, bias = wide(gain_ref), wide(bias_ref)
    x = lax.axis_index("x")
    ahead = slot_1_is_ahead()
    parts = [stats_of(mine, 0), stats_of(halo1, 384), stats_of(halo3, 384), stats_of(far, 0)]
    mean = (parts[0][0] + parts[1][0] + parts[2][0] + parts[3][0]) * 0.25
    spread = parts[0][1] + parts[1][1] + parts[2][1] + parts[3][1]
    for one in parts:
        spread = spread + 2560.0 * (one[0] - mean) * (one[0] - mean)
    rstd = lax.rsqrt(spread * (1.0 / 10240) + 1e-05)
    for step in range(4):
        scales[step, 0:1] = mean[step : step + 1]
        scales[step, 1:2] = rstd[step : step + 1]

    def one_step(step, carry):
        here = scales[step]

        def normed(value, tile):
            lanes = slice(tile * 128, tile * 128 + 128)
            value = (value.astype(F32) - here[0:1, lanes]) * here[1:2, lanes]
            return silu(value * gain[:, lanes] + bias[:, lanes])

        edge = pl.multiple_of(step * 96, 32)
        tiles = []
        low = low_lanes(32)
        for tile in range(3):
            one = halo1[pl.ds(edge + 32 * tile, 32)].astype(F32)
            three = halo3[pl.ds(edge + 32 * tile, 32)].astype(F32)
            top = normed(jnp.where(ahead, three, one), tile)
            bottom = normed(jnp.where(ahead, one, three), tile)
            if tile < 2:
                middle = normed(states[step, 256 * tile : 256 * tile + 256], tile)
            else:
                middle = spread_tail(normed(states[step, 512:640], 2))
                top = jnp.where(low, swapped(top), top)
                bottom = jnp.where(low, bottom, swapped(bottom))
            top = jnp.where(x > 0, top, 0.0)
            bottom = jnp.where(x < 3, bottom, 0.0)
            tiles.append(jnp.concatenate([top, middle, bottom], axis=0))
        store_taps(taps, tiles)
        bias_here = tb[step][0:1]
        main = (conv_row(taps, wp, 0) + conv_row(taps, wp, 1)) + conv_row(taps, wp, 2)
        activated = silu(main + bias_here[:, 0:256])
        tail = silu(conv_tail(taps, wt) + bias_here[:, 256:320])
        out[step, 0:256] = activated[:, 0:128].astype(BF16)
        out[step, 256:512] = activated[:, 128:256].astype(BF16)
        out[step, 512:640] = pack_tail(tail).astype(BF16)
        return carry

    lax.fori_loop(0, 4, one_step, 0)
    ones = [out[step].astype(F32) for step in range(4)]
    total[...] = ((ones[0] + ones[1]) + (ones[2] + ones[3])).astype(BF16)


def store_packed_frames(a3, tiles):
    low = low_lanes(POS)
    tails = []
    for place, (first, second, tail) in enumerate(tiles):
        a3[:, place * 256 : place * 256 + 128] = first.astype(BF16)
        a3[:, place * 256 + 128 : place * 256 + 256] = second.astype(BF16)
        tails.append(spread_tail(tail))
    a3[:, 768:896] = jnp.where(low, tails[0], tails[1]).astype(BF16)
    a3[:, 896:1024] = jnp.where(low, tails[2], 0.0).astype(BF16)


def second_total_kernel(own, before, after, tp, noise, rt, a3):
    store_packed_frames(a3, [[one[a:b].astype(F32) for a, b in SPANS] for one in (before, own, after)])
    for update, (a, b) in zip(packed_update(a3[...], tp), SPANS):
        total = update
        for step in range(4):
            total = total + noise[step, a:b].astype(F32)
        rt[a:b] = (0.25 * total).astype(BF16)


def second_prefix_kernel(own, before, after, tp, noise, prefix, a3):
    for step in range(4):
        store_packed_frames(a3, [[one[step, a:b].astype(F32) for a, b in SPANS] for one in (before, own, after)])
        for update, (a, b) in zip(packed_update(a3[...], tp), SPANS):
            now = 0.25 * (update + noise[step, a:b].astype(F32))
            prefix[step, a:b] = now if step == 0 else prefix[step - 1, a:b] + now


def result_kernel(sp, prefix, r1, r2, r3, *outs):
    x = lax.axis_index("x")
    base = sp[...].astype(F32) + offset_of((r1, r2, r3))
    for slot, out in enumerate(outs):
        out[...] = (base + prefix[x ^ hop_of(slot)]).astype(BF16)


def unpack_kernel(r0, r1, r2, r3, out):
    x = lax.axis_index("x")
    for slot, one in enumerate((r0, r1, r2, r3)):
        start = pl.multiple_of((x ^ hop_of(slot)) * POS, POS)
        out[pl.ds(start, POS), 0:128] = one[0:256]
        out[pl.ds(start, POS), 128:256] = one[256:512]
        tail = spread_tail(one[512:640].astype(F32))
        out[pl.ds(start, POS), 256:320] = tail[:, 0:64].astype(BF16)


def call(body, outs, *args, scratch=(), flops=0, limit=24, hbm=0, sems=0):
    shapes = [jax.ShapeDtypeStruct(shape, kind) for shape, kind in outs]
    vmem = pl.BlockSpec(memory_space=pltpu.VMEM)
    nbytes = sum(a.size * a.dtype.itemsize for a in args) + sum(s.size * s.dtype.itemsize for s in shapes)
    scratch_shapes = [pltpu.VMEM(shape, kind) for shape, kind in scratch]
    if sems:
        scratch_shapes.append(pltpu.SemaphoreType.DMA((sems,)))
    return pl.pallas_call(
        body,
        out_shape=shapes,
        in_specs=[pl.BlockSpec(memory_space=pltpu.HBM)] * hbm + [vmem] * (len(args) - hbm),
        out_specs=[vmem] * len(shapes),
        scratch_shapes=scratch_shapes,
        compiler_params=pltpu.CompilerParams(vmem_limit_bytes=limit << 20),
        cost_estimate=pl.CostEstimate(flops=flops, bytes_accessed=nbytes, transcendentals=0),
    )(*(pltpu.with_memory_space_constraint(a, pltpu.HBM) if i < hbm else a for i, a in enumerate(args)))


def moved(value, place):
    pairs = []
    for y in range(4):
        for x in range(4):
            for z in range(8):
                for core in range(2):
                    ty, tx, frame = place(y, x, z * 2 + core)
                    pairs.append(((y * 4 + x) * 16 + z * 2 + core, (ty * 4 + tx) * 16 + frame))
    return lax.ppermute(value, AXES, pairs)


def hop_on(slot, core):
    return slot if core == 0 else 4 - slot


def swap_x(values):
    out = [values[0]]
    for slot in (1, 2, 3):
        out.append(moved(values[slot], lambda y, x, frame: (y, x ^ hop_on(slot, frame % 2), frame)))
    return out


def gather_y(value):
    out = []
    for slot in (1, 2, 3):
        out.append(moved(value, lambda y, x, frame: (y ^ hop_on(slot, frame % 2), x, frame)))
    return out


def beside(value):
    there = moved(value, lambda y, x, frame: (y, x, (frame + (1 if frame % 2 else 15)) % 16))
    return there, moved(value, lambda y, x, frame: (y, x, frame ^ 1))


def embedding_of(step_index, half_dim):
    frequencies = jnp.exp(-math.log(10000.0) * jnp.arange(half_dim, dtype=F32) / half_dim)
    angles = step_index.astype(F32) * frequencies
    return jnp.concatenate([jnp.cos(angles), jnp.sin(angles)]).astype(BF16)


def local(start_state, step_noise, timesteps, gn_gain, gn_bias, spatial_weight, temporal_weight, temb_weight):
    start = start_state.reshape(1024, 320)
    noise = step_noise.reshape(1024, 320)
    emb = embedding_of(timesteps[0], temb_weight.shape[0] // 2)
    emb = jnp.broadcast_to(jnp.pad(emb, (0, 64))[None], (16, 384))
    packed = (ROWS, LANES)
    four = (4, ROWS, LANES)

    *outgoing, start, gain, bias = call(
        pack_kernel,
        [((688, 128), BF16)] * 4 + [((1024, 320), BF16), ((320,), F32), ((320,), F32)],
        noise, start, gn_gain, gn_bias, emb,
        scratch=(((4, 256, 320), BF16),),
        hbm=4,
        sems=7,
    )
    arrived = swap_x(outgoing)
    nq, sp = call(norm_start_kernel, [((800, 128), BF16), (packed, BF16)], start, gain, bias)
    there, mate = beside(nq)
    taps = ((320, 1024), BF16)
    a3 = ((256, 1024), BF16)
    pre = (256, 320)
    here, wp, wt, tp, tew = call(
        first_own_kernel,
        [((1,) + pre, F32), ((3, 1024, 320), BF16), ((1024, 192), BF16), ((1024, 320), BF16), ((320, 320), BF16)],
        spatial_weight, temporal_weight, temb_weight, nq,
        scratch=(taps,),
        flops=512 * 320 * 2880,
        hbm=3,
        sems=25,
    )
    sides = call(
        first_sides_kernel, [((2,) + pre, F32)], there, mate, wp, wt, scratch=(taps,), flops=1024 * 320 * 2880
    )[0]
    rt, noises, tb = call(
        first_total_kernel,
        [(packed, BF16), (four, BF16), ((4, 16, 320), F32)],
        here, sides, tp, tew, *arrived,
        scratch=(a3, ((3, 256, 64), F32)),
        flops=512 * 320 * 960,
    )
    totals = gather_y(rt)
    prefix = call(
        first_prefix_kernel, [(four, F32)], here, sides, tb, tp, noises, scratch=(a3,), flops=1536 * 320 * 960
    )[0]
    states, *halos = call(
        states_kernel,
        [(four, BF16), ((464, 128), BF16), ((464, 128), BF16), ((72, 128), BF16)],
        sp, prefix, *totals,
    )
    _, halo1, far, halo3 = swap_x((None, halos[0], halos[2], halos[1]))
    own, total = call(
        second_sweep_kernel,
        [(four, BF16), (packed, BF16)],
        states, halo1, halo3, far, halos[2], gain, bias, wp, wt, tb,
        scratch=(taps, ((4, 8, 384), F32)),
        flops=2048 * 320 * 2880,
    )
    sums = total, *beside(total)
    parts = own, *beside(own)
    rt = call(second_total_kernel, [(packed, BF16)], *sums, tp, noises, scratch=(a3,), flops=512 * 320 * 960)[0]
    totals = gather_y(rt)
    prefix = call(second_prefix_kernel, [(four, F32)], *parts, tp, noises, scratch=(a3,), flops=2048 * 320 * 960)[0]
    results = call(result_kernel, [(packed, BF16)] * 4, sp, prefix, *totals)
    out = call(unpack_kernel, [((1024, 320), BF16)], *swap_x(results))[0]
    return out.reshape(1, 1, 32, 32, 320)


def solution(mesh):
    split = Mesh(mesh.devices.reshape(4, 4, 8, 2), AXES)
    steps, frames = ("y", "x"), ("z", "core")
    placed = (
        P(frames, None, None, None),
        P(steps, frames, None, None, None),
        P(steps),
        P(),
        P(),
        P(),
        P(),
        P(),
    )
    return jax.shard_map(
        local,
        mesh=split,
        in_specs=placed,
        out_specs=P(steps, frames, None, None, None),
        check_vma=False,
    )
```

```python
import math

import jax
import jax.numpy as jnp
from jax import lax
from jax.experimental import pallas as pl
from jax.experimental.pallas import tpu as pltpu
from jax.sharding import Mesh, PartitionSpec as P


F32, BF16 = jnp.float32, jnp.bfloat16
AXES = ("y", "x", "z", "core")

POS, ROWS, LANES = 256, 640, 128


def silu(a):
    half = 0.5 * a
    return half + half * jnp.tanh(half)


def low_lanes(rows):
    return lax.broadcasted_iota(jnp.int32, (rows, LANES), 1) < 64


def swapped(tile):
    return pltpu.roll(tile, 64, 1)


def pack_tail(tail):
    half = tail.shape[0] // 2
    return jnp.concatenate([tail[:half], tail[half:]], axis=1)


def spread_tail(tile):
    low, other = low_lanes(tile.shape[0]), swapped(tile)
    return jnp.concatenate([jnp.where(low, tile, other), jnp.where(low, other, tile)], axis=0)


def same_group(size):
    rows = lax.broadcasted_iota(jnp.int32, (size, size), 0)
    columns = lax.broadcasted_iota(jnp.int32, (size, size), 1)
    return (((rows * 6554) >> 16) == ((columns * 6554) >> 16)).astype(F32).astype(BF16)


def thirds(value):
    parts = []
    for _ in range(3):
        part = value.astype(BF16).astype(F32)
        value = value - part
        parts.append(part)
    return parts


def group_sum(sums, members):
    wide = jnp.dot(jnp.concatenate(thirds(sums), axis=0).astype(BF16), members, preferred_element_type=F32)
    return (wide[0:8] + wide[8:16]) + wide[16:24]


def store_taps(taps, tiles):
    column = lax.broadcasted_iota(jnp.int32, (320, LANES), 0) & 31
    low = low_lanes(320)
    shifted = []
    for place, step in enumerate((-1, 0, 1)):
        moved = []
        for tile in tiles:
            if step:
                tile = pltpu.roll(tile, -step % 320, 0)
                tile = jnp.where(column == (0 if step < 0 else 31), 0.0, tile)
            moved.append(tile)
        taps[:, place * 256 : place * 256 + 128] = moved[0].astype(BF16)
        taps[:, place * 256 + 128 : place * 256 + 256] = moved[1].astype(BF16)
        shifted.append(moved[2])
    taps[:, 768:896] = jnp.where(low, shifted[0], shifted[1]).astype(BF16)
    taps[:, 896:1024] = jnp.where(low, shifted[2], 0.0).astype(BF16)


def conv_tail(taps, wt):
    wide = jnp.dot(taps[...], wt[...], preferred_element_type=F32)
    return (wide[0:256, 0:64] + wide[32:288, 64:128]) + wide[64:320, 128:192]


def conv_row(taps, wp, row):
    return jnp.dot(taps[row * 32 : row * 32 + POS, :], wp[row][:, 0:256], preferred_element_type=F32)


def weight_copies(places, out, sems, first):
    copies = []
    for place, one in enumerate(places):
        for source, target in (
            (one.at[0:256], out.at[place * 256 : place * 256 + 256]),
            (one.at[256:320], out.at[768 + 64 * place : 832 + 64 * place]),
        ):
            copies.append(pltpu.make_async_copy(source, target, sems.at[first + len(copies)]))
    for copy in copies:
        copy.start()
    out[960:1024] = jnp.zeros((64, 320), BF16)
    return copies


def hop_of(slot):
    return jnp.where(lax.axis_index("core") == 0, slot, (4 - slot) % 4)


def pack_kernel(noise_hbm, start_hbm, gain_hbm, bias_hbm, emb, o0, o1, o2, o3, start, gain, bias, noise, sems):
    x = lax.axis_index("x")
    outs = {0: o0, 1: o1, 2: o2, 3: o3}
    copies = {}
    for slot in (2, 1, 3, 0):
        at = pl.multiple_of((x ^ hop_of(slot)) * POS, POS)
        copies[slot] = pltpu.make_async_copy(noise_hbm.at[pl.ds(at, POS)], noise.at[slot], sems.at[slot])
        copies[slot].start()
    rest = [
        pltpu.make_async_copy(source, target, sems.at[4 + i])
        for i, (source, target) in enumerate(((start_hbm, start), (gain_hbm, gain), (bias_hbm, bias)))
    ]
    for copy in rest:
        copy.start()
    for slot, copy in copies.items():
        out = outs[slot]
        copy.wait()
        out[0:256] = noise[slot, :, 0:128]
        out[256:512] = noise[slot, :, 128:256]
        out[512:640] = pack_tail(noise[slot, :, 256:320].astype(F32)).astype(BF16)
        for tile in range(3):
            out[640 + 16 * tile : 656 + 16 * tile] = emb[:, tile * 128 : tile * 128 + 128]
    for copy in rest:
        copy.wait()


def norm_start_kernel(sw, start, gain_ref, bias_ref, nq, sp, wp0, sems):
    x = lax.axis_index("x")
    copies = weight_copies([sw.at[0, place] for place in range(3)], wp0, sems, 0)
    members = same_group(320)
    values = start[...].astype(F32)
    mean = group_sum(jnp.broadcast_to(jnp.sum(values, axis=0, keepdims=True), (8, 320)), members)[0:1] * (1.0 / 10240)
    centered = start[...].astype(F32) - mean
    spread = jnp.sum(centered * centered, axis=0, keepdims=True)
    var = group_sum(jnp.broadcast_to(spread, (8, 320)), members)[0:1] * (1.0 / 10240)
    scale = lax.rsqrt(var + 1e-05)
    gain, bias = gain_ref[...].reshape(1, 320), bias_ref[...].reshape(1, 320)
    first = pl.multiple_of(x * POS, POS)
    above = pl.multiple_of(jnp.maximum(x * POS - 32, 0), 32)
    below = pl.multiple_of(jnp.minimum(x * POS + POS, 992), 32)
    pieces = []
    for at, size, kept in ((above, 32, x > 0), (first, POS, None), (below, 32, x < 3)):
        block = start[pl.ds(at, size), :].astype(F32)
        normed = silu((block - mean) * scale * gain + bias)
        pieces.append(normed if kept is None else jnp.where(kept, normed, 0.0))
    normed = jnp.concatenate(pieces, axis=0)
    nq[0:320] = normed[:, 0:128].astype(BF16)
    nq[320:640] = normed[:, 128:256].astype(BF16)
    nq[640:800] = pack_tail(normed[:, 256:320]).astype(BF16)
    sp[0:256] = start[pl.ds(first, POS), 0:128]
    sp[256:512] = start[pl.ds(first, POS), 128:256]
    sp[512:640] = pack_tail(start[pl.ds(first, POS), 256:320].astype(F32)).astype(BF16)
    for copy in copies:
        copy.wait()


def conv_frame(normed, wp, wt, pre, taps, before_row=None):
    store_taps(taps, [normed[0:320].astype(F32), normed[320:640].astype(F32), spread_tail(normed[640:800].astype(F32))])
    main = None
    for row in range(3):
        if before_row is not None:
            before_row(row)
        term = conv_row(taps, wp, row)
        main = term if main is None else main + term
    if before_row is not None:
        before_row(3)
    pre[:, 0:256] = 0.5 * main
    pre[:, 256:320] = 0.5 * conv_tail(taps, wt)


def first_own_kernel(sw, normed, wp0, pre, wp1, wp2, wt, taps, sems):
    wp = (wp0, wp1, wp2)
    copies = [weight_copies([sw.at[row, place] for place in range(3)], wp[row], sems, 6 * row - 6) for row in (1, 2)]

    def before_row(row):
        if row < 3:
            for copy in copies[row - 1] if row else ():
                copy.wait()
        else:
            wt[...] = jnp.concatenate([one[:, 256:320].astype(F32) for one in wp], axis=1).astype(BF16)

    conv_frame(normed, wp, wt, pre.at[0], taps, before_row)


def first_sides_kernel(tw, tew_hbm, there, mate, wp0, wp1, wp2, wt, pre, tp, tew, taps, sems):
    core = lax.axis_index("core")
    frame = lax.axis_index("z") * 2 + core
    copies = weight_copies([tw.at[place + core * (2 - 2 * place)] for place in range(3)], tp, sems, 0)
    copies.append(pltpu.make_async_copy(tew_hbm, tew, sems.at[6]))
    copies[-1].start()
    for place, normed in enumerate((there, mate)):
        conv_frame(normed, (wp0, wp1, wp2), wt, pre.at[place], taps)
    for copy in copies:
        copy.wait()

    @pl.when((frame == 0) | (frame == 15))
    def _():
        tp[0:256] = jnp.zeros((256, 320), BF16)
        tp[768:832] = jnp.zeros((64, 320), BF16)


def silu_half(half):
    return half + half * jnp.tanh(half)


SPANS = ((0, 256), (256, 512), (512, 640))


def packed_update(a3, tp):
    update = jnp.dot(a3, tp[...], preferred_element_type=F32)
    return update[:, 0:128], update[:, 128:256], pack_tail(update[:, 256:320])


def store_frames(a3, parts):
    for place, part in enumerate(parts):
        a3[:, place * 256 : place * 256 + 256] = part[:, 0:256].astype(BF16)
    a3[:, 768:896] = jnp.concatenate([parts[0][:, 256:320], parts[1][:, 256:320]], axis=1).astype(BF16)
    last = parts[2][:, 256:320]
    a3[:, 896:1024] = jnp.concatenate([last, jnp.zeros_like(last)], axis=1).astype(BF16)


def first_total_kernel(here, sides, tp, tew, n0, n1, n2, n3, rt, noise, tb, a3, tails):
    x = lax.axis_index("x")
    arrived = (n0, n1, n2, n3)
    bias = None
    for at, rows in ((640, slice(0, 128)), (656, slice(128, 256)), (672, slice(256, 320))):
        emb = jnp.concatenate([one[at : at + 16, 0 : rows.stop - rows.start] for one in arrived], axis=0)
        term = jnp.dot(emb, tew[rows], preferred_element_type=F32)
        bias = term if bias is None else bias + term
    bias = bias / (1.0 + jnp.exp(-bias))
    for slot, one in enumerate(arrived):
        step = x ^ hop_of(slot)
        noise[step] = one[0:640]
        tb[step] = bias[slot * 16 : slot * 16 + 16]
    halves = [0.5 * bias[slot * 16 : slot * 16 + 1] for slot in range(4)]

    def some_rows(block, carry):
        rows = pl.ds(pl.multiple_of(block * 32, 32), 32)
        for place, pre in enumerate((sides.at[0], here.at[0], sides.at[1])):
            half = pre[rows, :]
            ones = [silu_half(half + one) for one in halves]
            total = (ones[0] + ones[1]) + (ones[2] + ones[3])
            a3[rows, place * 256 : place * 256 + 256] = total[:, 0:256].astype(BF16)
            tails[place, rows, :] = total[:, 256:320]
        return carry

    lax.fori_loop(0, 8, some_rows, 0)
    a3[:, 768:896] = jnp.concatenate([tails[0], tails[1]], axis=1).astype(BF16)
    a3[:, 896:1024] = jnp.concatenate([tails[2], jnp.zeros((POS, 64), F32)], axis=1).astype(BF16)
    for update, (a, b) in zip(packed_update(a3[...], tp), SPANS):
        total = update
        for step in range(4):
            total = total + noise[step, a:b].astype(F32)
        rt[a:b] = (0.25 * total).astype(BF16)


def first_prefix_kernel(here, sides, tb, tp, noise, prefix, a3):
    prefix[0] = jnp.zeros((ROWS, LANES), F32)

    def one_step(step, carry):
        half = 0.5 * tb[step][0:1]
        store_frames(a3, [silu_half(pre[...] + half) for pre in (sides.at[0], here.at[0], sides.at[1])])
        for update, (a, b) in zip(packed_update(a3[...], tp), SPANS):
            prefix[step + 1, a:b] = prefix[step, a:b] + 0.25 * (update + noise[step, a:b].astype(F32))
        return carry

    lax.fori_loop(0, 3, one_step, 0)


def dup_third(parts):
    third = parts[:, 256:384]
    third = jnp.where(low_lanes(third.shape[0]), third, swapped(third))
    return jnp.concatenate([parts[:, 0:256], third], axis=1)


def slot_1_is_ahead():
    return ((lax.axis_index("x") + lax.axis_index("core")) & 1) == 0


def offset_of(totals):
    y = lax.axis_index("y")
    kept = [jnp.where((y ^ hop_of(slot)) < y, one[...].astype(F32), 0.0) for slot, one in enumerate(totals, 1)]
    return kept[0] + kept[1] + kept[2]


def position_sum(tiles):
    sums = [jnp.sum(tile, axis=0, keepdims=True) for tile in tiles]
    third = jnp.broadcast_to(sums[2], (8, LANES))
    return jnp.concatenate(sums[:2] + [(third + swapped(third))[0:1]], axis=1)


def states_kernel(sp, prefix, r1, r2, r3, states, halo1, halo3, far):
    ahead = slot_1_is_ahead()
    members = same_group(384)
    base = sp[...].astype(F32) + offset_of((r1, r2, r3))
    spans = ((0, 256), (256, 512), (512, 640))
    sums = []
    for step in range(4):
        states[step] = (base + prefix[step]).astype(BF16)
        sums.append(position_sum([states[step, a:b].astype(F32) for a, b in spans]))
        for i, (first, last) in enumerate(((0, 224), (256, 480), (512, 608))):
            at = step * 96 + i * 32
            for halo, row in ((halo1, jnp.where(ahead, last, first)), (halo3, jnp.where(ahead, first, last))):
                halo[at : at + 32] = states[step, pl.ds(pl.multiple_of(row, 32), 32)]
    means = dup_third(group_sum(jnp.concatenate(sums + sums, axis=0), members) * (1.0 / 2560))
    spreads = []
    for step in range(4):
        mean = means[step : step + 1]
        centered = [states[step, a:b].astype(F32) - mean[:, 128 * i : 128 * i + 128] for i, (a, b) in enumerate(spans)]
        spreads.append(position_sum([c * c for c in centered]))
    spread = dup_third(group_sum(jnp.concatenate(spreads + spreads, axis=0), members))
    rest = jnp.concatenate([means[0:4], spread[0:4]], axis=0)
    for part in range(3):
        piece = rest.astype(BF16)
        rest = rest - piece.astype(F32)
        for tile in range(3):
            at = (part * 3 + tile) * 8
            value = piece[:, tile * 128 : tile * 128 + 128]
            far[at : at + 8] = value
            halo1[384 + at : 392 + at] = value
            halo3[384 + at : 392 + at] = value


def stats_of(ref, base):
    total = None
    for part in range(3):
        piece = jnp.concatenate(
            [ref[base + (part * 3 + t) * 8 : base + (part * 3 + t) * 8 + 8].astype(F32) for t in range(3)], axis=1
        )
        total = piece if total is None else total + piece
    return total[0:4], total[4:8]


def wide(vector):
    vector = vector[...].reshape(1, 320)
    return jnp.concatenate([vector, vector[:, 256:320]], axis=1)


def second_sweep_kernel(states, halo1, halo3, far, mine, gain_ref, bias_ref, wp0, wp1, wp2, wt, tb, out, total, taps, scales):
    wp = (wp0, wp1, wp2)
    gain, bias = wide(gain_ref), wide(bias_ref)
    x = lax.axis_index("x")
    ahead = slot_1_is_ahead()
    parts = [stats_of(mine, 0), stats_of(halo1, 384), stats_of(halo3, 384), stats_of(far, 0)]
    mean = (parts[0][0] + parts[1][0] + parts[2][0] + parts[3][0]) * 0.25
    spread = parts[0][1] + parts[1][1] + parts[2][1] + parts[3][1]
    for one in parts:
        spread = spread + 2560.0 * (one[0] - mean) * (one[0] - mean)
    rstd = lax.rsqrt(spread * (1.0 / 10240) + 1e-05)
    for step in range(4):
        scales[step, 0:1] = mean[step : step + 1]
        scales[step, 1:2] = rstd[step : step + 1]

    def one_step(step, carry):
        here = scales[step]

        def normed(value, tile):
            lanes = slice(tile * 128, tile * 128 + 128)
            value = (value.astype(F32) - here[0:1, lanes]) * here[1:2, lanes]
            return silu(value * gain[:, lanes] + bias[:, lanes])

        edge = pl.multiple_of(step * 96, 32)
        tiles = []
        low = low_lanes(32)
        for tile in range(3):
            one = halo1[pl.ds(edge + 32 * tile, 32)].astype(F32)
            three = halo3[pl.ds(edge + 32 * tile, 32)].astype(F32)
            top = normed(jnp.where(ahead, three, one), tile)
            bottom = normed(jnp.where(ahead, one, three), tile)
            if tile < 2:
                middle = normed(states[step, 256 * tile : 256 * tile + 256], tile)
            else:
                middle = spread_tail(normed(states[step, 512:640], 2))
                top = jnp.where(low, swapped(top), top)
                bottom = jnp.where(low, bottom, swapped(bottom))
            top = jnp.where(x > 0, top, 0.0)
            bottom = jnp.where(x < 3, bottom, 0.0)
            tiles.append(jnp.concatenate([top, middle, bottom], axis=0))
        store_taps(taps, tiles)
        bias_here = tb[step][0:1]
        main = (conv_row(taps, wp, 0) + conv_row(taps, wp, 1)) + conv_row(taps, wp, 2)
        activated = silu(main + bias_here[:, 0:256])
        tail = silu(conv_tail(taps, wt) + bias_here[:, 256:320])
        out[step, 0:256] = activated[:, 0:128].astype(BF16)
        out[step, 256:512] = activated[:, 128:256].astype(BF16)
        out[step, 512:640] = pack_tail(tail).astype(BF16)
        return carry

    lax.fori_loop(0, 4, one_step, 0)
    ones = [out[step].astype(F32) for step in range(4)]
    total[...] = ((ones[0] + ones[1]) + (ones[2] + ones[3])).astype(BF16)


def store_packed_frames(a3, tiles):
    low = low_lanes(POS)
    tails = []
    for place, (first, second, tail) in enumerate(tiles):
        a3[:, place * 256 : place * 256 + 128] = first.astype(BF16)
        a3[:, place * 256 + 128 : place * 256 + 256] = second.astype(BF16)
        tails.append(spread_tail(tail))
    a3[:, 768:896] = jnp.where(low, tails[0], tails[1]).astype(BF16)
    a3[:, 896:1024] = jnp.where(low, tails[2], 0.0).astype(BF16)


def second_total_kernel(own, before, after, tp, noise, rt, a3):
    store_packed_frames(a3, [[one[a:b].astype(F32) for a, b in SPANS] for one in (before, own, after)])
    for update, (a, b) in zip(packed_update(a3[...], tp), SPANS):
        total = update
        for step in range(4):
            total = total + noise[step, a:b].astype(F32)
        rt[a:b] = (0.25 * total).astype(BF16)


def second_prefix_kernel(own, before, after, tp, noise, prefix, a3):
    for step in range(4):
        store_packed_frames(a3, [[one[step, a:b].astype(F32) for a, b in SPANS] for one in (before, own, after)])
        for update, (a, b) in zip(packed_update(a3[...], tp), SPANS):
            now = 0.25 * (update + noise[step, a:b].astype(F32))
            prefix[step, a:b] = now if step == 0 else prefix[step - 1, a:b] + now


def result_kernel(sp, prefix, r1, r2, r3, *outs):
    x = lax.axis_index("x")
    base = sp[...].astype(F32) + offset_of((r1, r2, r3))
    for slot, out in enumerate(outs):
        out[...] = (base + prefix[x ^ hop_of(slot)]).astype(BF16)


def unpack_kernel(r0, r1, r2, r3, out):
    x = lax.axis_index("x")
    for slot, one in enumerate((r0, r1, r2, r3)):
        start = pl.multiple_of((x ^ hop_of(slot)) * POS, POS)
        out[pl.ds(start, POS), 0:128] = one[0:256]
        out[pl.ds(start, POS), 128:256] = one[256:512]
        tail = spread_tail(one[512:640].astype(F32))
        out[pl.ds(start, POS), 256:320] = tail[:, 0:64].astype(BF16)


def call(body, outs, *args, scratch=(), flops=0, limit=24, hbm=0, sems=0):
    shapes = [jax.ShapeDtypeStruct(shape, kind) for shape, kind in outs]
    vmem = pl.BlockSpec(memory_space=pltpu.VMEM)
    nbytes = sum(a.size * a.dtype.itemsize for a in args) + sum(s.size * s.dtype.itemsize for s in shapes)
    scratch_shapes = [pltpu.VMEM(shape, kind) for shape, kind in scratch]
    if sems:
        scratch_shapes.append(pltpu.SemaphoreType.DMA((sems,)))
    return pl.pallas_call(
        body,
        out_shape=shapes,
        in_specs=[pl.BlockSpec(memory_space=pltpu.HBM)] * hbm + [vmem] * (len(args) - hbm),
        out_specs=[vmem] * len(shapes),
        scratch_shapes=scratch_shapes,
        compiler_params=pltpu.CompilerParams(vmem_limit_bytes=limit << 20),
        cost_estimate=pl.CostEstimate(flops=flops, bytes_accessed=nbytes, transcendentals=0),
    )(*(pltpu.with_memory_space_constraint(a, pltpu.HBM) if i < hbm else a for i, a in enumerate(args)))


def moved(value, place):
    pairs = []
    for y in range(4):
        for x in range(4):
            for z in range(8):
                for core in range(2):
                    ty, tx, frame = place(y, x, z * 2 + core)
                    pairs.append(((y * 4 + x) * 16 + z * 2 + core, (ty * 4 + tx) * 16 + frame))
    return lax.ppermute(value, AXES, pairs)


def hop_on(slot, core):
    return slot if core == 0 else 4 - slot


def swap_x(values):
    out = [values[0]]
    for slot in (1, 2, 3):
        out.append(moved(values[slot], lambda y, x, frame: (y, x ^ hop_on(slot, frame % 2), frame)))
    return out


def gather_y(value):
    out = []
    for slot in (1, 2, 3):
        out.append(moved(value, lambda y, x, frame: (y ^ hop_on(slot, frame % 2), x, frame)))
    return out


def beside(value):
    there = moved(value, lambda y, x, frame: (y, x, (frame + (1 if frame % 2 else 15)) % 16))
    return there, moved(value, lambda y, x, frame: (y, x, frame ^ 1))


def embedding_of(step_index, half_dim):
    frequencies = jnp.exp(-math.log(10000.0) * jnp.arange(half_dim, dtype=F32) / half_dim)
    angles = step_index.astype(F32) * frequencies
    return jnp.concatenate([jnp.cos(angles), jnp.sin(angles)]).astype(BF16)


def local(start_state, step_noise, timesteps, gn_gain, gn_bias, spatial_weight, temporal_weight, temb_weight):
    start = start_state.reshape(1024, 320)
    noise = step_noise.reshape(1024, 320)
    emb = embedding_of(timesteps[0], temb_weight.shape[0] // 2)
    emb = jnp.broadcast_to(jnp.pad(emb, (0, 64))[None], (16, 384))
    packed = (ROWS, LANES)
    four = (4, ROWS, LANES)

    *outgoing, start, gain, bias = call(
        pack_kernel,
        [((688, 128), BF16)] * 4 + [((1024, 320), BF16), ((320,), F32), ((320,), F32)],
        noise, start, gn_gain, gn_bias, emb,
        scratch=(((4, 256, 320), BF16),),
        hbm=4,
        sems=7,
    )
    arrived = swap_x(outgoing)
    weight = ((1024, 320), BF16)
    nq, sp, wp0 = call(
        norm_start_kernel,
        [((800, 128), BF16), (packed, BF16), weight],
        spatial_weight, start, gain, bias,
        hbm=1,
        sems=6,
    )
    there, mate = beside(nq)
    taps = ((320, 1024), BF16)
    a3 = ((256, 1024), BF16)
    pre = (256, 320)
    here, wp1, wp2, wt = call(
        first_own_kernel,
        [((1,) + pre, F32), weight, weight, ((1024, 192), BF16)],
        spatial_weight, nq, wp0,
        scratch=(taps,),
        flops=512 * 320 * 2880,
        hbm=1,
        sems=12,
    )
    conv_weights = wp0, wp1, wp2, wt
    sides, tp, tew = call(
        first_sides_kernel,
        [((2,) + pre, F32), weight, ((320, 320), BF16)],
        temporal_weight, temb_weight, there, mate, *conv_weights,
        scratch=(taps,),
        flops=1024 * 320 * 2880,
        hbm=2,
        sems=7,
    )
    rt, noises, tb = call(
        first_total_kernel,
        [(packed, BF16), (four, BF16), ((4, 16, 320), F32)],
        here, sides, tp, tew, *arrived,
        scratch=(a3, ((3, 256, 64), F32)),
        flops=512 * 320 * 960,
    )
    totals = gather_y(rt)
    prefix = call(
        first_prefix_kernel, [(four, F32)], here, sides, tb, tp, noises, scratch=(a3,), flops=1536 * 320 * 960
    )[0]
    states, *halos = call(
        states_kernel,
        [(four, BF16), ((464, 128), BF16), ((464, 128), BF16), ((72, 128), BF16)],
        sp, prefix, *totals,
    )
    _, halo1, far, halo3 = swap_x((None, halos[0], halos[2], halos[1]))
    own, total = call(
        second_sweep_kernel,
        [(four, BF16), (packed, BF16)],
        states, halo1, halo3, far, halos[2], gain, bias, *conv_weights, tb,
        scratch=(taps, ((4, 8, 384), F32)),
        flops=2048 * 320 * 2880,
    )
    sums = total, *beside(total)
    parts = own, *beside(own)
    rt = call(second_total_kernel, [(packed, BF16)], *sums, tp, noises, scratch=(a3,), flops=512 * 320 * 960)[0]
    totals = gather_y(rt)
    prefix = call(second_prefix_kernel, [(four, F32)], *parts, tp, noises, scratch=(a3,), flops=2048 * 320 * 960)[0]
    results = call(result_kernel, [(packed, BF16)] * 4, sp, prefix, *totals)
    out = call(unpack_kernel, [((1024, 320), BF16)], *swap_x(results))[0]
    return out.reshape(1, 1, 32, 32, 320)


def solution(mesh):
    split = Mesh(mesh.devices.reshape(4, 4, 8, 2), AXES)
    steps, frames = ("y", "x"), ("z", "core")
    placed = (
        P(frames, None, None, None),
        P(steps, frames, None, None, None),
        P(steps),
        P(),
        P(),
        P(),
        P(),
        P(),
    )
    return jax.shard_map(
        local,
        mesh=split,
        in_specs=placed,
        out_specs=P(steps, frames, None, None, None),
        check_vma=False,
    )
```

```python
import math

import jax
import jax.numpy as jnp
from jax import lax
from jax.experimental import pallas as pl
from jax.experimental.pallas import tpu as pltpu
from jax.sharding import Mesh, PartitionSpec as P


F32, BF16 = jnp.float32, jnp.bfloat16
AXES = ("y", "x", "z", "core")

POS, ROWS, LANES = 256, 640, 128


def silu(a):
    half = 0.5 * a
    return half + half * jnp.tanh(half)


def low_lanes(rows):
    return lax.broadcasted_iota(jnp.int32, (rows, LANES), 1) < 64


def swapped(tile):
    return pltpu.roll(tile, 64, 1)


def pack_tail(tail):
    half = tail.shape[0] // 2
    return jnp.concatenate([tail[:half], tail[half:]], axis=1)


def spread_tail(tile):
    low, other = low_lanes(tile.shape[0]), swapped(tile)
    return jnp.concatenate([jnp.where(low, tile, other), jnp.where(low, other, tile)], axis=0)


def same_group(size):
    rows = lax.broadcasted_iota(jnp.int32, (size, size), 0)
    columns = lax.broadcasted_iota(jnp.int32, (size, size), 1)
    return (((rows * 6554) >> 16) == ((columns * 6554) >> 16)).astype(F32).astype(BF16)


def thirds(value):
    parts = []
    for _ in range(3):
        part = value.astype(BF16).astype(F32)
        value = value - part
        parts.append(part)
    return parts


def group_sum(sums, members):
    wide = jnp.dot(jnp.concatenate(thirds(sums), axis=0).astype(BF16), members, preferred_element_type=F32)
    return (wide[0:8] + wide[8:16]) + wide[16:24]


def store_taps(taps, tiles):
    column = lax.broadcasted_iota(jnp.int32, (320, LANES), 0) & 31
    low = low_lanes(320)
    shifted = []
    for place, step in enumerate((-1, 0, 1)):
        moved = []
        for tile in tiles:
            if step:
                tile = pltpu.roll(tile, -step % 320, 0)
                tile = jnp.where(column == (0 if step < 0 else 31), 0.0, tile)
            moved.append(tile)
        taps[:, place * 256 : place * 256 + 128] = moved[0].astype(BF16)
        taps[:, place * 256 + 128 : place * 256 + 256] = moved[1].astype(BF16)
        shifted.append(moved[2])
    taps[:, 768:896] = jnp.where(low, shifted[0], shifted[1]).astype(BF16)
    taps[:, 896:1024] = jnp.where(low, shifted[2], 0.0).astype(BF16)


def conv_tail(taps, wt):
    wide = jnp.dot(taps[...], wt[...], preferred_element_type=F32)
    return (wide[0:256, 0:64] + wide[32:288, 64:128]) + wide[64:320, 128:192]


def conv_row(taps, wp, row):
    return jnp.dot(taps[row * 32 : row * 32 + POS, :], wp[row, :, 0:256], preferred_element_type=F32)


def hop_of(slot):
    return jnp.where(lax.axis_index("core") == 0, slot, (4 - slot) % 4)


def pack_kernel(noise_hbm, start_hbm, gain_hbm, bias_hbm, emb, o0, o1, o2, o3, start, gain, bias, noise, sems):
    x = lax.axis_index("x")
    outs = {0: o0, 1: o1, 2: o2, 3: o3}
    copies = {}
    for slot in (2, 1, 3, 0):
        at = pl.multiple_of((x ^ hop_of(slot)) * POS, POS)
        copies[slot] = pltpu.make_async_copy(noise_hbm.at[pl.ds(at, POS)], noise.at[slot], sems.at[slot])
        copies[slot].start()
    rest = [
        pltpu.make_async_copy(source, target, sems.at[4 + i])
        for i, (source, target) in enumerate(((start_hbm, start), (gain_hbm, gain), (bias_hbm, bias)))
    ]
    for copy in rest:
        copy.start()
    for slot, copy in copies.items():
        out = outs[slot]
        copy.wait()
        out[0:256] = noise[slot, :, 0:128]
        out[256:512] = noise[slot, :, 128:256]
        out[512:640] = pack_tail(noise[slot, :, 256:320].astype(F32)).astype(BF16)
        for tile in range(3):
            out[640 + 16 * tile : 656 + 16 * tile] = emb[:, tile * 128 : tile * 128 + 128]
    for copy in rest:
        copy.wait()


def norm_start_kernel(start, gain_ref, bias_ref, nq, sp):
    x = lax.axis_index("x")
    members = same_group(320)
    values = start[...].astype(F32)
    mean = group_sum(jnp.broadcast_to(jnp.sum(values, axis=0, keepdims=True), (8, 320)), members)[0:1] * (1.0 / 10240)
    centered = start[...].astype(F32) - mean
    spread = jnp.sum(centered * centered, axis=0, keepdims=True)
    var = group_sum(jnp.broadcast_to(spread, (8, 320)), members)[0:1] * (1.0 / 10240)
    scale = lax.rsqrt(var + 1e-05)
    gain, bias = gain_ref[...].reshape(1, 320), bias_ref[...].reshape(1, 320)
    first = pl.multiple_of(x * POS, POS)
    above = pl.multiple_of(jnp.maximum(x * POS - 32, 0), 32)
    below = pl.multiple_of(jnp.minimum(x * POS + POS, 992), 32)
    pieces = []
    for at, size, kept in ((above, 32, x > 0), (first, POS, None), (below, 32, x < 3)):
        block = start[pl.ds(at, size), :].astype(F32)
        normed = silu((block - mean) * scale * gain + bias)
        pieces.append(normed if kept is None else jnp.where(kept, normed, 0.0))
    normed = jnp.concatenate(pieces, axis=0)
    nq[0:320] = normed[:, 0:128].astype(BF16)
    nq[320:640] = normed[:, 128:256].astype(BF16)
    nq[640:800] = pack_tail(normed[:, 256:320]).astype(BF16)
    sp[0:256] = start[pl.ds(first, POS), 0:128]
    sp[256:512] = start[pl.ds(first, POS), 128:256]
    sp[512:640] = pack_tail(start[pl.ds(first, POS), 256:320].astype(F32)).astype(BF16)


def frame_taps(normed, taps):
    store_taps(taps, [normed[0:320].astype(F32), normed[320:640].astype(F32), spread_tail(normed[640:800].astype(F32))])


def conv_frame(wp, wt, pre, taps, before_row=None):
    main = None
    for row in range(3):
        if before_row is not None:
            before_row(row)
        term = conv_row(taps, wp, row)
        main = term if main is None else main + term
    if before_row is not None:
        before_row(3)
    pre[:, 0:256] = 0.5 * main
    pre[:, 256:320] = 0.5 * conv_tail(taps, wt)


def first_own_kernel(sw, tw, tew_hbm, normed, pre, wp, wt, tp, tew, taps, sems):
    core = lax.axis_index("core")
    frame = lax.axis_index("z") * 2 + core
    copies = []
    for row in range(4):
        out = tp if row == 3 else wp.at[row]
        for place in range(3):
            one = tw.at[place + core * (2 - 2 * place)] if row == 3 else sw.at[row, place]
            for source, target in (
                (one.at[0:256], out.at[place * 256 : place * 256 + 256]),
                (one.at[256:320], out.at[768 + 64 * place : 832 + 64 * place]),
            ):
                copies.append(pltpu.make_async_copy(source, target, sems.at[len(copies)]))
    copies.append(pltpu.make_async_copy(tew_hbm, tew, sems.at[24]))
    for copy in copies:
        copy.start()
    for row in range(3):
        wp[row, 960:1024] = jnp.zeros((64, 320), BF16)
    tp[960:1024] = jnp.zeros((64, 320), BF16)

    def before_row(row):
        if row < 3:
            for copy in copies[6 * row : 6 * row + 6]:
                copy.wait()
        else:
            wt[...] = jnp.concatenate([wp[i, :, 256:320].astype(F32) for i in range(3)], axis=1).astype(BF16)

    frame_taps(normed, taps)
    conv_frame(wp, wt, pre.at[0], taps, before_row)
    for copy in copies[18:]:
        copy.wait()

    @pl.when((frame == 0) | (frame == 15))
    def _():
        tp[0:256] = jnp.zeros((256, 320), BF16)
        tp[768:832] = jnp.zeros((64, 320), BF16)


def first_sides_kernel(there, mate, wp, wt, pre, taps):
    frame_taps(there, taps.at[0])
    frame_taps(mate, taps.at[1])
    for place in range(2):
        conv_frame(wp, wt, pre.at[place], taps.at[place])


def silu_half(half):
    return half + half * jnp.tanh(half)


SPANS = ((0, 256), (256, 512), (512, 640))


def packed_update(a3, tp):
    update = jnp.dot(a3, tp[...], preferred_element_type=F32)
    return update[:, 0:128], update[:, 128:256], pack_tail(update[:, 256:320])


def store_frames(a3, parts):
    for place, part in enumerate(parts):
        a3[:, place * 256 : place * 256 + 256] = part[:, 0:256].astype(BF16)
    a3[:, 768:896] = jnp.concatenate([parts[0][:, 256:320], parts[1][:, 256:320]], axis=1).astype(BF16)
    last = parts[2][:, 256:320]
    a3[:, 896:1024] = jnp.concatenate([last, jnp.zeros_like(last)], axis=1).astype(BF16)


def first_total_kernel(here, sides, tp, tew, n0, n1, n2, n3, rt, noise, tb, a3, tails):
    x = lax.axis_index("x")
    arrived = (n0, n1, n2, n3)
    bias = None
    for at, rows in ((640, slice(0, 128)), (656, slice(128, 256)), (672, slice(256, 320))):
        emb = jnp.concatenate([one[at : at + 16, 0 : rows.stop - rows.start] for one in arrived], axis=0)
        term = jnp.dot(emb, tew[rows], preferred_element_type=F32)
        bias = term if bias is None else bias + term
    bias = bias / (1.0 + jnp.exp(-bias))
    for slot, one in enumerate(arrived):
        step = x ^ hop_of(slot)
        noise[step] = one[0:640]
        tb[step] = bias[slot * 16 : slot * 16 + 16]
    halves = [0.5 * bias[slot * 16 : slot * 16 + 1] for slot in range(4)]

    def some_rows(block, carry):
        rows = pl.ds(pl.multiple_of(block * 32, 32), 32)
        for place, pre in enumerate((sides.at[0], here.at[0], sides.at[1])):
            half = pre[rows, :]
            ones = [silu_half(half + one) for one in halves]
            total = (ones[0] + ones[1]) + (ones[2] + ones[3])
            a3[rows, place * 256 : place * 256 + 256] = total[:, 0:256].astype(BF16)
            tails[place, rows, :] = total[:, 256:320]
        return carry

    lax.fori_loop(0, 8, some_rows, 0)
    a3[:, 768:896] = jnp.concatenate([tails[0], tails[1]], axis=1).astype(BF16)
    a3[:, 896:1024] = jnp.concatenate([tails[2], jnp.zeros((POS, 64), F32)], axis=1).astype(BF16)
    for update, (a, b) in zip(packed_update(a3[...], tp), SPANS):
        total = update
        for step in range(4):
            total = total + noise[step, a:b].astype(F32)
        rt[a:b] = (0.25 * total).astype(BF16)


def first_prefix_kernel(here, sides, tb, tp, noise, prefix, a3):
    prefix[0] = jnp.zeros((ROWS, LANES), F32)

    def one_step(step, carry):
        half = 0.5 * tb[step][0:1]
        store_frames(a3, [silu_half(pre[...] + half) for pre in (sides.at[0], here.at[0], sides.at[1])])
        for update, (a, b) in zip(packed_update(a3[...], tp), SPANS):
            prefix[step + 1, a:b] = prefix[step, a:b] + 0.25 * (update + noise[step, a:b].astype(F32))
        return carry

    lax.fori_loop(0, 3, one_step, 0)


def dup_third(parts):
    third = parts[:, 256:384]
    third = jnp.where(low_lanes(third.shape[0]), third, swapped(third))
    return jnp.concatenate([parts[:, 0:256], third], axis=1)


def slot_1_is_ahead():
    return ((lax.axis_index("x") + lax.axis_index("core")) & 1) == 0


def offset_of(totals):
    y = lax.axis_index("y")
    kept = [jnp.where((y ^ hop_of(slot)) < y, one[...].astype(F32), 0.0) for slot, one in enumerate(totals, 1)]
    return kept[0] + kept[1] + kept[2]


def position_sum(tiles):
    sums = [jnp.sum(tile, axis=0, keepdims=True) for tile in tiles]
    third = jnp.broadcast_to(sums[2], (8, LANES))
    return jnp.concatenate(sums[:2] + [(third + swapped(third))[0:1]], axis=1)


def states_kernel(sp, prefix, r1, r2, r3, states, halo1, halo3, far):
    ahead = slot_1_is_ahead()
    members = same_group(384)
    base = sp[...].astype(F32) + offset_of((r1, r2, r3))
    spans = ((0, 256), (256, 512), (512, 640))
    sums = []
    for step in range(4):
        states[step] = (base + prefix[step]).astype(BF16)
        sums.append(position_sum([states[step, a:b].astype(F32) for a, b in spans]))
        for i, (first, last) in enumerate(((0, 224), (256, 480), (512, 608))):
            at = step * 96 + i * 32
            for halo, row in ((halo1, jnp.where(ahead, last, first)), (halo3, jnp.where(ahead, first, last))):
                halo[at : at + 32] = states[step, pl.ds(pl.multiple_of(row, 32), 32)]
    means = dup_third(group_sum(jnp.concatenate(sums + sums, axis=0), members) * (1.0 / 2560))
    spreads = []
    for step in range(4):
        mean = means[step : step + 1]
        centered = [states[step, a:b].astype(F32) - mean[:, 128 * i : 128 * i + 128] for i, (a, b) in enumerate(spans)]
        spreads.append(position_sum([c * c for c in centered]))
    spread = dup_third(group_sum(jnp.concatenate(spreads + spreads, axis=0), members))
    rest = jnp.concatenate([means[0:4], spread[0:4]], axis=0)
    for part in range(3):
        piece = rest.astype(BF16)
        rest = rest - piece.astype(F32)
        for tile in range(3):
            at = (part * 3 + tile) * 8
            value = piece[:, tile * 128 : tile * 128 + 128]
            far[at : at + 8] = value
            halo1[384 + at : 392 + at] = value
            halo3[384 + at : 392 + at] = value


def stats_of(ref, base):
    total = None
    for part in range(3):
        piece = jnp.concatenate(
            [ref[base + (part * 3 + t) * 8 : base + (part * 3 + t) * 8 + 8].astype(F32) for t in range(3)], axis=1
        )
        total = piece if total is None else total + piece
    return total[0:4], total[4:8]


def wide(vector):
    vector = vector[...].reshape(1, 320)
    return jnp.concatenate([vector, vector[:, 256:320]], axis=1)


def second_sweep_kernel(states, halo1, halo3, far, mine, gain_ref, bias_ref, wp, wt, tb, out, total, taps, scales):
    gain, bias = wide(gain_ref), wide(bias_ref)
    x = lax.axis_index("x")
    ahead = slot_1_is_ahead()
    parts = [stats_of(mine, 0), stats_of(halo1, 384), stats_of(halo3, 384), stats_of(far, 0)]
    mean = (parts[0][0] + parts[1][0] + parts[2][0] + parts[3][0]) * 0.25
    spread = parts[0][1] + parts[1][1] + parts[2][1] + parts[3][1]
    for one in parts:
        spread = spread + 2560.0 * (one[0] - mean) * (one[0] - mean)
    rstd = lax.rsqrt(spread * (1.0 / 10240) + 1e-05)
    for step in range(4):
        scales[step, 0:1] = mean[step : step + 1]
        scales[step, 1:2] = rstd[step : step + 1]

    low = low_lanes(32)

    def build(step):
        here = scales[step]

        def normed(value, tile):
            lanes = slice(tile * 128, tile * 128 + 128)
            value = (value.astype(F32) - here[0:1, lanes]) * here[1:2, lanes]
            return silu(value * gain[:, lanes] + bias[:, lanes])

        tiles = []
        for tile in range(3):
            edge = slice(step * 96 + 32 * tile, step * 96 + 32 * tile + 32)
            one, three = halo1[edge].astype(F32), halo3[edge].astype(F32)
            top = normed(jnp.where(ahead, three, one), tile)
            bottom = normed(jnp.where(ahead, one, three), tile)
            if tile < 2:
                middle = normed(states[step, 256 * tile : 256 * tile + 256], tile)
            else:
                middle = spread_tail(normed(states[step, 512:640], 2))
                top = jnp.where(low, swapped(top), top)
                bottom = jnp.where(low, bottom, swapped(bottom))
            top = jnp.where(x > 0, top, 0.0)
            bottom = jnp.where(x < 3, bottom, 0.0)
            tiles.append(jnp.concatenate([top, middle, bottom], axis=0))
        store_taps(taps.at[step % 2], tiles)

    def finish(step):
        here = taps.at[step % 2]
        bias_here = tb[step][0:1]
        main = (conv_row(here, wp, 0) + conv_row(here, wp, 1)) + conv_row(here, wp, 2)
        activated = silu(main + bias_here[:, 0:256])
        tail = silu(conv_tail(here, wt) + bias_here[:, 256:320])
        out[step, 0:256] = activated[:, 0:128].astype(BF16)
        out[step, 256:512] = activated[:, 128:256].astype(BF16)
        out[step, 512:640] = pack_tail(tail).astype(BF16)

    build(0)
    for step in range(4):
        if step < 3:
            build(step + 1)
        finish(step)
    ones = [out[step].astype(F32) for step in range(4)]
    total[...] = ((ones[0] + ones[1]) + (ones[2] + ones[3])).astype(BF16)


def store_packed_frames(a3, tiles):
    low = low_lanes(POS)
    tails = []
    for place, (first, second, tail) in enumerate(tiles):
        a3[:, place * 256 : place * 256 + 128] = first.astype(BF16)
        a3[:, place * 256 + 128 : place * 256 + 256] = second.astype(BF16)
        tails.append(spread_tail(tail))
    a3[:, 768:896] = jnp.where(low, tails[0], tails[1]).astype(BF16)
    a3[:, 896:1024] = jnp.where(low, tails[2], 0.0).astype(BF16)


def second_total_kernel(own, before, after, tp, noise, rt, a3):
    store_packed_frames(a3, [[one[a:b].astype(F32) for a, b in SPANS] for one in (before, own, after)])
    for update, (a, b) in zip(packed_update(a3[...], tp), SPANS):
        total = update
        for step in range(4):
            total = total + noise[step, a:b].astype(F32)
        rt[a:b] = (0.25 * total).astype(BF16)


def second_prefix_kernel(own, before, after, tp, noise, prefix, a3):
    for step in range(4):
        store_packed_frames(a3, [[one[step, a:b].astype(F32) for a, b in SPANS] for one in (before, own, after)])
        for update, (a, b) in zip(packed_update(a3[...], tp), SPANS):
            now = 0.25 * (update + noise[step, a:b].astype(F32))
            prefix[step, a:b] = now if step == 0 else prefix[step - 1, a:b] + now


def result_kernel(sp, prefix, r1, r2, r3, *outs):
    x = lax.axis_index("x")
    base = sp[...].astype(F32) + offset_of((r1, r2, r3))
    for slot, out in enumerate(outs):
        out[...] = (base + prefix[x ^ hop_of(slot)]).astype(BF16)


def unpack_kernel(r0, r1, r2, r3, out):
    x = lax.axis_index("x")
    for slot, one in enumerate((r0, r1, r2, r3)):
        start = pl.multiple_of((x ^ hop_of(slot)) * POS, POS)
        out[pl.ds(start, POS), 0:128] = one[0:256]
        out[pl.ds(start, POS), 128:256] = one[256:512]
        tail = spread_tail(one[512:640].astype(F32))
        out[pl.ds(start, POS), 256:320] = tail[:, 0:64].astype(BF16)


def call(body, outs, *args, scratch=(), flops=0, limit=24, hbm=0, sems=0):
    shapes = [jax.ShapeDtypeStruct(shape, kind) for shape, kind in outs]
    vmem = pl.BlockSpec(memory_space=pltpu.VMEM)
    nbytes = sum(a.size * a.dtype.itemsize for a in args) + sum(s.size * s.dtype.itemsize for s in shapes)
    scratch_shapes = [pltpu.VMEM(shape, kind) for shape, kind in scratch]
    if sems:
        scratch_shapes.append(pltpu.SemaphoreType.DMA((sems,)))
    return pl.pallas_call(
        body,
        out_shape=shapes,
        in_specs=[pl.BlockSpec(memory_space=pltpu.HBM)] * hbm + [vmem] * (len(args) - hbm),
        out_specs=[vmem] * len(shapes),
        scratch_shapes=scratch_shapes,
        compiler_params=pltpu.CompilerParams(vmem_limit_bytes=limit << 20),
        cost_estimate=pl.CostEstimate(flops=flops, bytes_accessed=nbytes, transcendentals=0),
    )(*(pltpu.with_memory_space_constraint(a, pltpu.HBM) if i < hbm else a for i, a in enumerate(args)))


def moved(value, place):
    pairs = []
    for y in range(4):
        for x in range(4):
            for z in range(8):
                for core in range(2):
                    ty, tx, frame = place(y, x, z * 2 + core)
                    pairs.append(((y * 4 + x) * 16 + z * 2 + core, (ty * 4 + tx) * 16 + frame))
    return lax.ppermute(value, AXES, pairs)


def hop_on(slot, core):
    return slot if core == 0 else 4 - slot


def swap_x(values):
    out = [values[0]]
    for slot in (1, 2, 3):
        out.append(moved(values[slot], lambda y, x, frame: (y, x ^ hop_on(slot, frame % 2), frame)))
    return out


def gather_y(value):
    out = []
    for slot in (1, 2, 3):
        out.append(moved(value, lambda y, x, frame: (y ^ hop_on(slot, frame % 2), x, frame)))
    return out


def beside(value):
    there = moved(value, lambda y, x, frame: (y, x, (frame + (1 if frame % 2 else 15)) % 16))
    return there, moved(value, lambda y, x, frame: (y, x, frame ^ 1))


def embedding_of(step_index, half_dim):
    frequencies = jnp.exp(-math.log(10000.0) * jnp.arange(half_dim, dtype=F32) / half_dim)
    angles = step_index.astype(F32) * frequencies
    return jnp.concatenate([jnp.cos(angles), jnp.sin(angles)]).astype(BF16)


def local(start_state, step_noise, timesteps, gn_gain, gn_bias, spatial_weight, temporal_weight, temb_weight):
    start = start_state.reshape(1024, 320)
    noise = step_noise.reshape(1024, 320)
    emb = embedding_of(timesteps[0], temb_weight.shape[0] // 2)
    emb = jnp.broadcast_to(jnp.pad(emb, (0, 64))[None], (16, 384))
    packed = (ROWS, LANES)
    four = (4, ROWS, LANES)

    *outgoing, start, gain, bias = call(
        pack_kernel,
        [((688, 128), BF16)] * 4 + [((1024, 320), BF16), ((320,), F32), ((320,), F32)],
        noise, start, gn_gain, gn_bias, emb,
        scratch=(((4, 256, 320), BF16),),
        hbm=4,
        sems=7,
    )
    arrived = swap_x(outgoing)
    nq, sp = call(norm_start_kernel, [((800, 128), BF16), (packed, BF16)], start, gain, bias)
    there, mate = beside(nq)
    taps = ((320, 1024), BF16)
    a3 = ((256, 1024), BF16)
    pre = (256, 320)
    here, wp, wt, tp, tew = call(
        first_own_kernel,
        [((1,) + pre, F32), ((3, 1024, 320), BF16), ((1024, 192), BF16), ((1024, 320), BF16), ((320, 320), BF16)],
        spatial_weight, temporal_weight, temb_weight, nq,
        scratch=(taps,),
        flops=512 * 320 * 2880,
        hbm=3,
        sems=25,
    )
    sides = call(
        first_sides_kernel, [((2,) + pre, F32)], there, mate, wp, wt, scratch=(((2, 320, 1024), BF16),), flops=1024 * 320 * 2880
    )[0]
    rt, noises, tb = call(
        first_total_kernel,
        [(packed, BF16), (four, BF16), ((4, 16, 320), F32)],
        here, sides, tp, tew, *arrived,
        scratch=(a3, ((3, 256, 64), F32)),
        flops=512 * 320 * 960,
    )
    totals = gather_y(rt)
    prefix = call(
        first_prefix_kernel, [(four, F32)], here, sides, tb, tp, noises, scratch=(a3,), flops=1536 * 320 * 960
    )[0]
    states, *halos = call(
        states_kernel,
        [(four, BF16), ((464, 128), BF16), ((464, 128), BF16), ((72, 128), BF16)],
        sp, prefix, *totals,
    )
    _, halo1, far, halo3 = swap_x((None, halos[0], halos[2], halos[1]))
    own, total = call(
        second_sweep_kernel,
        [(four, BF16), (packed, BF16)],
        states, halo1, halo3, far, halos[2], gain, bias, wp, wt, tb,
        scratch=(((2, 320, 1024), BF16), ((4, 8, 384), F32)),
        flops=2048 * 320 * 2880,
    )
    sums = total, *beside(total)
    parts = own, *beside(own)
    rt = call(second_total_kernel, [(packed, BF16)], *sums, tp, noises, scratch=(a3,), flops=512 * 320 * 960)[0]
    totals = gather_y(rt)
    prefix = call(second_prefix_kernel, [(four, F32)], *parts, tp, noises, scratch=(a3,), flops=2048 * 320 * 960)[0]
    results = call(result_kernel, [(packed, BF16)] * 4, sp, prefix, *totals)
    out = call(unpack_kernel, [((1024, 320), BF16)], *swap_x(results))[0]
    return out.reshape(1, 1, 32, 32, 320)


def solution(mesh):
    split = Mesh(mesh.devices.reshape(4, 4, 8, 2), AXES)
    steps, frames = ("y", "x"), ("z", "core")
    placed = (
        P(frames, None, None, None),
        P(steps, frames, None, None, None),
        P(steps),
        P(),
        P(),
        P(),
        P(),
        P(),
    )
    return jax.shard_map(
        local,
        mesh=split,
        in_specs=placed,
        out_specs=P(steps, frames, None, None, None),
        check_vma=False,
    )
```
